128 devices in a mesh: req: 4 (over y), hid: 32 (over x, z, core).
Axes of the slice: x: 4, y: 4, z: 4, core: 2. Of those that a mesh axis runs over, the one named last changes fastest.
Arguments:
- tokens: bfloat16 [4096, 7168], P(('req', 'hid')), may hold values from -90 to 90
- gain_in: float32 [7168], replicated, may hold values from 0.25 to 1.75
- w_qkv: bfloat16 [7168, 3, 7168], P(None, None, 'hid'), may hold values from -0.0625 to 0.0625
- adapt_down: bfloat16 [7168, 128], replicated, may hold values from -0.0625 to 0.0625
- adapt_up: bfloat16 [128, 7168], P(None, 'hid'), may hold values from -0.5 to 0.5
- w_out: bfloat16 [7168, 3584], P('hid'), may hold values from -0.0625 to 0.0625
- gain_ff: float32 [3584], replicated, may hold values from 0.25 to 1.75
- w_gate_up: bfloat16 [3584, 2, 14336], P(None, None, 'hid'), may hold values from -0.09375 to 0.09375
- w_down: bfloat16 [14336, 3584], P('hid'), may hold values from -0.046875 to 0.046875
- prefix_cache: bfloat16 [4, 2048, 2, 7168], P('req', 'hid'), may hold values from -330 to 330
- prefix_owner: int32 [3], replicated, may hold values from 0 to 3, as said below
- group_prefix: int32 [4], replicated, may hold values from 0 to 2, as said below
- lengths: int32 [4, 6], P('req'), may hold values from 1 to 512, 1024 in all within a row
Outputs:
- attn_out: bfloat16 [4096, 3584], P(('req', 'hid'))
- block_out: bfloat16 [4096, 3584], P(('req', 'hid'))
The draws below stay inside these ranges and needn't reach their ends.
Inputs may be any that keep to these rules, and one draw needn't show every extreme that they name: `prefix_owner`: the 3 prefixes have different owners. `group_prefix`: every prefix is extended by at least one group. Each group's 6 lengths sum to 1024, and the longest of each group is exactly 512.
All inputs are finite; a program needn't handle non-finite values.
Results may differ from the reference program's by a relative error of at most 0.035.
Values may be sent and summed in bfloat16 or wider, within the bound.
A program may use at most 128 MiB of HBM per device.

```python
import math
import jax
import jax.numpy as jnp
import numpy as np
from jax import lax

DIN = 7168
DM = 3584
FF = 14336
HD = 224
RANK = 128
NPFX = 3
REQ_GRP = 6
HEADS = 32
DQ = 7168
PFX = 2048
TOK_GRP = 1024
TOKENS = 4096
N_REQ = 4


def draw_tokens(key, part):
    k_base, k_rows, k_cols = jax.random.split(key, 3)
    row_scale = jnp.exp(jax.random.uniform(k_rows, (TOKENS, 1), minval=math.log(0.3), maxval=math.log(3.0)))
    col_scale = jnp.exp(jax.random.uniform(k_cols, (1, DIN), minval=math.log(0.5), maxval=math.log(5.0)))
    base = jnp.clip(jax.random.normal(k_base, (TOKENS, DIN), dtype=jnp.float32), -6.0, 6.0)
    return (base * row_scale * col_scale).astype(jnp.bfloat16)


def draw_prefix_cache(key, part):
    k_base = jax.random.fold_in(key, 0)
    base = jnp.clip(jax.random.normal(k_base, (N_REQ, PFX, 2, DQ), dtype=jnp.float32), -6.0, 6.0)
    return base.astype(jnp.bfloat16)


def draw_prefix_owner(key, part):
    return jax.random.permutation(jax.random.fold_in(key, 7), N_REQ)[:NPFX].astype(jnp.int32)


def draw_group_prefix(key, part):
    k_first, k_rest, k_order = jax.random.split(jax.random.fold_in(key, 11), 3)
    first = jax.random.permutation(k_first, NPFX).astype(jnp.int32)
    rest = jax.random.randint(k_rest, (N_REQ - NPFX,), 0, NPFX).astype(jnp.int32)
    return jax.random.permutation(k_order, jnp.concatenate([first, rest])).astype(jnp.int32)


def block_scale(stream_key, dims, cuts, smallest, top_value):
    loudness = 1.0
    for axis_at, parts in cuts:
        steps = jax.random.uniform(jax.random.fold_in(jax.random.fold_in(stream_key, 6), axis_at), (parts,), jnp.float32, smallest / len(cuts), top_value / len(cuts))
        loudness = loudness * jnp.repeat(jnp.exp(steps), dims[axis_at] // parts).reshape((-1,) + (1,) * (len(dims) - 1 - axis_at))
    return loudness


def profile(count, total, most, lean):
    weights = [(1 << 20) // math.isqrt(rank ** lean) + 1 for rank in range(2, count + 1)]
    spare, holding = total - most - (count - 1), [1] * (count - 1)
    while spare > 0:
        candidates = [i for i in range(count - 1) if holding[i] < most]
        pool, remaining = sum([weights[i] for i in candidates]), spare
        for i in candidates:
            extra = min(most - holding[i], max(1, remaining * weights[i] // pool), spare)
            holding[i] = holding[i] + extra
            spare = spare - extra
    return np.array([most] + holding)


def ragged_sizes(key, number_of, total, most, lean):
    if number_of == 2:
        one = jax.random.randint(key, (), max(1, total - most), min(most, total - 1) + 1)
        return jnp.stack([one, total - one])
    tallies = jnp.asarray(profile(number_of, total, most, lean), jnp.int32)
    couples = (number_of - 1) // 2
    giver, sink = tallies[1:1 + 2 * couples:2], tallies[2:2 + 2 * couples:2]
    room = jnp.minimum(giver - 1, most - sink)
    passed = jax.random.randint(jax.random.fold_in(key, 1), (couples,), 0, 1 << 20) % (room + 1)
    tallies = tallies.at[1:1 + 2 * couples:2].set(giver - passed).at[2:2 + 2 * couples:2].set(sink + passed)
    return tallies[jax.random.permutation(jax.random.fold_in(key, 2), number_of)]


def scatter_about(key, extent, deviation, reach, cuts=(), kind=jnp.bfloat16):
    result = deviation * jax.random.normal(key, extent, jnp.float32)
    if cuts:
        result = result * block_scale(key, extent, cuts, -0.22, 0.18)
    return jnp.clip(result, -reach, reach).astype(kind)


def setup_inputs(seed: int = 0) -> dict:
    arg_keys = jax.random.split(jax.random.key(seed), 14)
    return {
        "tokens": draw_tokens(jax.random.fold_in(arg_keys[13], 71), 0),
        "gain_in": jnp.clip(1.0 + 0.15 * jax.random.normal(arg_keys[1], (DIN,), jnp.float32), 0.25, 1.75),
        "w_qkv": scatter_about(arg_keys[2], (DIN, 3, DQ), DIN ** -0.5, 0.0625, ((2, 32),)),
        "adapt_down": scatter_about(arg_keys[3], (DIN, RANK), DIN ** -0.5, 0.0625),
        "adapt_up": scatter_about(arg_keys[4], (RANK, DQ), RANK ** -0.5, 0.5, ((1, 32),)),
        "w_out": scatter_about(arg_keys[5], (DQ, DM), DQ ** -0.5, 0.0625, ((0, 32),)),
        "gain_ff": jnp.clip(1.0 + 0.15 * jax.random.normal(arg_keys[6], (DM,), jnp.float32), 0.25, 1.75),
        "w_gate_up": scatter_about(arg_keys[7], (DM, 2, FF), DM ** -0.5, 0.09375, ((2, 32),)),
        "w_down": scatter_about(arg_keys[8], (FF, DM), FF ** -0.5, 0.046875, ((0, 32),)),
        "prefix_cache": draw_prefix_cache(jax.random.fold_in(arg_keys[13], 71), 0),
        "prefix_owner": draw_prefix_owner(jax.random.fold_in(arg_keys[13], 71), 0),
        "group_prefix": draw_group_prefix(jax.random.fold_in(arg_keys[13], 71), 0),
        "lengths": jax.vmap(lambda own: ragged_sizes(own, REQ_GRP, TOK_GRP, TOK_GRP // 2, 2))(jax.random.split(arg_keys[12], N_REQ)).reshape((N_REQ, REQ_GRP)).astype(jnp.int32),
    }


EPS = 1e-05

def rms_scale(matrix, gain_vec):
    return matrix * lax.rsqrt(lax.optimization_barrier(jnp.mean(matrix * matrix, axis=-1, keepdims=True)) + EPS) * gain_vec

def rounded_f32(matrix):
    return lax.optimization_barrier(matrix.astype(jnp.bfloat16)).astype(jnp.float32)

def reference(tokens, gain_in, w_qkv, adapt_down, adapt_up, w_out, gain_ff, w_gate_up, w_down, prefix_cache, prefix_owner, group_prefix, lengths):
    normed = rms_scale(tokens.astype(jnp.float32), gain_in).astype(jnp.bfloat16)
    latent = jnp.dot(normed, adapt_down, preferred_element_type=jnp.float32).astype(jnp.bfloat16)
    joint = jnp.dot(normed, w_qkv.reshape(DIN, 3 * DQ), preferred_element_type=jnp.float32)
    queries = (joint[:, :DQ] + jnp.dot(latent, adapt_up, preferred_element_type=jnp.float32)).astype(jnp.bfloat16)
    suffix_keys = joint[:, DQ:2 * DQ].astype(jnp.bfloat16)
    suffix_vals = joint[:, 2 * DQ:].astype(jnp.bfloat16)
    score_scale = HD ** (-0.5)
    position = jnp.arange(TOK_GRP, dtype=jnp.int32)
    outputs = []
    for group_index in range(N_REQ):
        row_begin = group_index * TOK_GRP
        group_q = queries[row_begin:row_begin + TOK_GRP].astype(jnp.float32).reshape(TOK_GRP, HEADS, HD)
        group_k = suffix_keys[row_begin:row_begin + TOK_GRP].astype(jnp.float32).reshape(TOK_GRP, HEADS, HD)
        group_v = suffix_vals[row_begin:row_begin + TOK_GRP].astype(jnp.float32).reshape(TOK_GRP, HEADS, HD)
        owner_slot = prefix_owner[group_prefix[group_index]]
        cached = prefix_cache[owner_slot].astype(jnp.float32)
        cached_k = cached[:, 0].reshape(PFX, HEADS, HD)
        cached_v = cached[:, 1].reshape(PFX, HEADS, HD)
        request_ends = jnp.cumsum(lengths[group_index]).astype(jnp.int32)
        request = lax.optimization_barrier(jnp.sum((position[:, None] >= request_ends[None, :]).astype(jnp.int32), axis=1))
        allowed = jnp.logical_and(request[:, None] == request[None, :], position[None, :] <= position[:, None])
        score_pre = jnp.einsum('thd,phd->htp', group_q, cached_k) * score_scale
        score_suf = jnp.einsum('thd,shd->hts', group_q, group_k) * score_scale
        score_suf = jnp.where(allowed[None], score_suf, -jnp.inf)
        row_max = jnp.maximum(lax.optimization_barrier(jnp.max(score_pre, axis=-1)), lax.optimization_barrier(jnp.max(score_suf, axis=-1)))
        expo_pre = jnp.exp(score_pre - row_max[..., None])
        expo_suf = jnp.exp(score_suf - row_max[..., None])
        row_sum = lax.optimization_barrier(jnp.sum(expo_pre, axis=-1)) + lax.optimization_barrier(jnp.sum(expo_suf, axis=-1))
        weighted = jnp.einsum('htp,phd->thd', rounded_f32(expo_pre), cached_v)
        weighted = weighted + jnp.einsum('hts,shd->thd', rounded_f32(expo_suf), group_v)
        heads_out = (weighted / row_sum.T[..., None]).astype(jnp.bfloat16).reshape(TOK_GRP, DQ)
        outputs.append(heads_out)
    heads_all = jnp.concatenate(outputs, axis=0)
    summed = jnp.dot(heads_all, w_out, preferred_element_type=jnp.float32)
    attn_out = summed.astype(jnp.bfloat16)
    ff_in = rms_scale(summed, gain_ff).astype(jnp.bfloat16)
    gate_up = jnp.dot(ff_in, w_gate_up.reshape(DM, 2 * FF), preferred_element_type=jnp.float32)
    hidden = (jax.nn.silu(gate_up[:, :FF]) * gate_up[:, FF:]).astype(jnp.bfloat16)
    block_out = jnp.dot(hidden, w_down, preferred_element_type=jnp.float32).astype(jnp.bfloat16)
    return (attn_out, block_out)
```

```python
import jax
import jax.numpy as jnp
from jax import lax
from jax.experimental import pallas as pl
from jax.experimental.pallas import tpu as pltpu
from jax.sharding import PartitionSpec as P

HD = 224


EPS = 1e-05


def rms_scale(matrix, gain_vec):
    return matrix * lax.rsqrt(jnp.mean(matrix * matrix, axis=-1, keepdims=True) + EPS) * gain_vec


def prefix_part(queries, kv_block):
    span_len = kv_block.shape[0]
    head_count = queries.shape[1]
    head_size = queries.shape[2]
    cached_k = kv_block[:, 0].reshape(span_len, head_count, head_size)
    cached_v = kv_block[:, 1].reshape(span_len, head_count, head_size)
    scores = jnp.einsum(
        "thd,phd->htp", queries, cached_k, preferred_element_type=jnp.float32
    ) * head_size ** (-0.5)
    row_max = jnp.max(scores, axis=-1)
    expos = jnp.exp(scores - row_max[..., None])
    row_sum = jnp.sum(expos, axis=-1)
    weighted = jnp.einsum(
        "htp,phd->htd", expos.astype(jnp.bfloat16), cached_v, preferred_element_type=jnp.float32
    )
    return (row_max, row_sum, weighted)


def suffix_part(queries, suffix_keys, suffix_vals, allowed):
    head_size = queries.shape[2]
    scores = jnp.einsum(
        "thd,shd->hts", queries, suffix_keys, preferred_element_type=jnp.float32
    ) * head_size ** (-0.5)
    scores = jnp.where(allowed[None], scores, -jnp.inf)
    row_max = jnp.max(scores, axis=-1)
    expos = jnp.exp(scores - row_max[..., None])
    row_sum = jnp.sum(expos, axis=-1)
    weighted = jnp.einsum(
        "hts,shd->htd", expos.astype(jnp.bfloat16), suffix_vals, preferred_element_type=jnp.float32
    )
    return (row_max, row_sum, weighted)


def combine(first_part, second_part):
    joint_max = jnp.maximum(first_part[0], second_part[0])
    first_factor = jnp.exp(first_part[0] - joint_max)
    second_factor = jnp.exp(second_part[0] - joint_max)
    joint_sum = first_part[1] * first_factor + second_part[1] * second_factor
    joint_acc = first_part[2] * first_factor[..., None] + second_part[2] * second_factor[..., None]
    return (joint_max, joint_sum, joint_acc)


MESH = pl.DeviceIdType.MESH
NX, NZ = 4, 4


def place():
    hid = lax.axis_index("hid")
    return hid // 8, (hid // 2) % 4, hid % 2


def moved(da, db, core_flip=0):
    x, z, c = place()
    xn = (x + 4 + (1 - c) * db + c * da) % 4
    zn = (z + 4 + (1 - c) * da + c * db) % 4
    cn = c + core_flip * (1 - 2 * c)
    return xn * 8 + zn * 2 + cn


def remote(src, dst, send, recv, hid):
    return pltpu.make_async_remote_copy(
        src_ref=src, dst_ref=dst, send_sem=send, recv_sem=recv,
        device_id={"hid": hid}, device_id_type=MESH,
    )


def greet(peers):
    barrier = pltpu.get_barrier_semaphore()
    for peer in peers:
        pl.semaphore_signal(barrier, inc=1, device_id=peer, device_id_type=MESH)
    pl.semaphore_wait(barrier, len(peers))


class Mail:
    def __init__(self, send_sems, recv_sems):
        self.send_sems, self.recv_sems, self.sent = send_sems, recv_sems, []

    def send(self, role, src, dst, hid):
        copy = remote(src, dst, self.send_sems.at[role], self.recv_sems.at[role], hid)
        copy.start()
        self.sent.append(copy)

    def await_recv(self, role, dst, hid):
        remote(dst, dst, self.send_sems.at[role], self.recv_sems.at[role], hid).wait_recv()

    def drain(self):
        for copy in self.sent:
            copy.wait_send()


GATHER_ROLES = 36


def gather_rows(mail, base, buf, rows, on_pair=None):
    half = rows // 2
    x, z, c = place()

    def blk(hid, part=None):
        start = pl.multiple_of(hid * rows, rows)
        if part is None:
            return buf.at[pl.ds(start, rows)]
        return buf.at[pl.ds(start + part * half, half)]

    offs = (0, -1, 1, 2)
    a_plus, a_minus = moved(1, 0), moved(-1, 0)
    b_plus, b_minus = moved(0, 1), moved(0, -1)
    partner = moved(0, 0, 1)

    def role2(i, k):
        return base + 4 + 4 * i + k

    def to_partner(ia, ib):
        owner = moved(offs[ia], offs[ib])
        mail.send(base + 20 + ia * 4 + ib, blk(owner), blk(owner), partner)

    def line_out(i):
        owner = moved(0, offs[i])
        mail.send(role2(i, 0), blk(owner), blk(owner), a_plus)
        mail.send(role2(i, 1), blk(owner), blk(owner), a_minus)

    def line_relay(i):
        low, high = moved(-1, offs[i]), moved(1, offs[i])
        mail.await_recv(role2(i, 0), blk(low), a_minus)
        mail.send(role2(i, 2), blk(low, 0), blk(low, 0), a_plus)
        mail.await_recv(role2(i, 1), blk(high), a_plus)
        mail.send(role2(i, 3), blk(high, 1), blk(high, 1), a_minus)
        to_partner(1, i)
        to_partner(2, i)

    def line_far(i):
        far = moved(2, offs[i])
        mail.await_recv(role2(i, 2), blk(far, 0), a_minus)
        mail.await_recv(role2(i, 3), blk(far, 1), a_plus)
        to_partner(3, i)

    own = moved(0, 0)
    mail.send(base + 0, blk(own), blk(own), b_plus)
    mail.send(base + 1, blk(own), blk(own), b_minus)
    line_out(0)
    to_partner(0, 0)
    low, high = moved(0, -1), moved(0, 1)
    mail.await_recv(base + 0, blk(low), b_minus)
    mail.send(base + 2, blk(low, 0), blk(low, 0), b_plus)
    line_out(1)
    to_partner(0, 1)
    mail.await_recv(base + 1, blk(high), b_plus)
    mail.send(base + 3, blk(high, 1), blk(high, 1), b_minus)
    line_out(2)
    to_partner(0, 2)
    line_relay(0)
    far = moved(0, 2)
    mail.await_recv(base + 2, blk(far, 0), b_minus)
    mail.await_recv(base + 3, blk(far, 1), b_plus)
    line_out(3)
    to_partner(0, 3)
    line_relay(1)
    line_relay(2)
    line_far(0)
    line_relay(3)
    line_far(1)
    line_far(2)
    line_far(3)

    def from_partner(ia, ib):
        owner = moved(offs[ib], offs[ia], 1)
        mail.await_recv(base + 20 + ia * 4 + ib, blk(owner), partner)

    for ia in range(4):
        for ib in range(4):
            from_partner(ia, ib)


SCATTER_ROLES = 17


def reduce_rows(mail, base, product, width, xs, xr, sums, acc, near, mid, last, swap_out, swap_in):
    x, z, c = place()
    a = (1 - c) * z + c * x
    b = (1 - c) * x + c * z
    partner = moved(0, 0, 1)
    a_plus, a_minus = moved(1, 0), moved(-1, 0)
    b_plus, b_minus = moved(0, 1), moved(0, -1)
    steps = (2, 1, 3, 0)

    def set_chips(k, cc):
        return [(1 - cc) * (j * 4 + k) + cc * (k * 4 + j) for j in range(4)]

    def partner_part(idx):
        k = (b + steps[idx]) % 4
        product(set_chips(k, 1 - c), 1 - c, xs.at[idx], None)
        mail.send(base + idx, xs.at[idx], xr.at[idx], partner)

    def own_part(idx, out):
        k = (a + steps[idx]) % 4
        mail.await_recv(base + idx, xr.at[idx], partner)
        product(set_chips(k, c), c, out, xr.at[idx])

    lo, hi = pl.ds(0, 128), pl.ds(128, 128)
    partner_part(0)
    partner_part(1)
    own_part(0, sums.at[0])
    mail.send(base + 4, sums.at[0, lo], near.at[0, lo], a_plus)
    mail.send(base + 5, sums.at[0, hi], near.at[1, hi], a_minus)
    partner_part(2)
    own_part(1, sums.at[1])
    mail.send(base + 6, sums.at[1, hi], mid.at[0, hi], a_plus)
    partner_part(3)
    own_part(2, sums.at[2])
    mail.send(base + 7, sums.at[2, lo], mid.at[1, lo], a_minus)
    mail.await_recv(base + 4, near.at[0, lo], a_minus)
    sums[1, lo] = (sums[1, lo].astype(jnp.float32) + near[0, lo].astype(jnp.float32)).astype(jnp.bfloat16)
    mail.send(base + 8, sums.at[1, lo], mid.at[0, lo], a_plus)
    mail.await_recv(base + 5, near.at[1, hi], a_plus)
    sums[2, hi] = (sums[2, hi].astype(jnp.float32) + near[1, hi].astype(jnp.float32)).astype(jnp.bfloat16)
    mail.send(base + 9, sums.at[2, hi], mid.at[1, hi], a_minus)
    own_part(3, acc)
    mail.await_recv(base + 6, mid.at[0, hi], a_minus)
    mail.await_recv(base + 7, mid.at[1, lo], a_plus)
    mail.await_recv(base + 8, mid.at[0, lo], a_minus)
    mail.await_recv(base + 9, mid.at[1, hi], a_plus)

    def chunk(j, low, size):
        return pl.ds(pl.multiple_of(j * 64 + low, 32), size)

    def chunk_sum(j, low, size):
        at = chunk(j, low, size)
        return acc[at] + mid[0, at].astype(jnp.float32) + mid[1, at].astype(jnp.float32)

    far, up, down, own = (b + 2) % 4, (b + 1) % 4, (b + 3) % 4, b
    q = sums.at[3]
    q[chunk(far, 0, 64)] = chunk_sum(far, 0, 64).astype(jnp.bfloat16)
    mail.send(base + 10, q.at[chunk(far, 0, 32)], last.at[0], b_plus)
    mail.send(base + 11, q.at[chunk(far, 32, 32)], last.at[1], b_minus)
    q[chunk(up, 32, 32)] = chunk_sum(up, 32, 32).astype(jnp.bfloat16)
    mail.send(base + 12, q.at[chunk(up, 32, 32)], last.at[2], b_plus)
    q[chunk(down, 0, 32)] = chunk_sum(down, 0, 32).astype(jnp.bfloat16)
    mail.send(base + 13, q.at[chunk(down, 0, 32)], last.at[3], b_minus)
    mail.await_recv(base + 10, last.at[0], b_minus)
    q[chunk(up, 0, 32)] = (chunk_sum(up, 0, 32) + last[0].astype(jnp.float32)).astype(jnp.bfloat16)
    mail.send(base + 14, q.at[chunk(up, 0, 32)], last.at[4], b_plus)
    mail.await_recv(base + 11, last.at[1], b_plus)
    q[chunk(down, 32, 32)] = (chunk_sum(down, 32, 32) + last[1].astype(jnp.float32)).astype(jnp.bfloat16)
    mail.send(base + 15, q.at[chunk(down, 32, 32)], last.at[5], b_minus)
    top, bottom = chunk_sum(own, 0, 32), chunk_sum(own, 32, 32)
    mail.await_recv(base + 12, last.at[2], b_minus)
    mail.await_recv(base + 13, last.at[3], b_plus)
    mail.await_recv(base + 14, last.at[4], b_minus)
    mail.await_recv(base + 15, last.at[5], b_plus)
    top = top + last[3].astype(jnp.float32) + last[4].astype(jnp.float32)
    bottom = bottom + last[2].astype(jnp.float32) + last[5].astype(jnp.float32)
    is_first = c == 0
    swap_out[...] = jnp.where(is_first, bottom, top)
    mail.send(base + 16, swap_out, swap_in, partner)
    mine = jnp.where(is_first, top, bottom)
    mail.await_recv(base + 16, swap_in, partner)
    return mine


TAIL_ROLES = SCATTER_ROLES * 2 + GATHER_ROLES


def tail_kernel(
    heads_ref, w_out_hbm, gain_ref, w_gu_hbm, w_down_hbm, attn_ref, block_ref,
    w_out, w_gu, w_down, load_sems, send_sems, recv_sems,
    xs, xr, sums, acc, near, mid, last, swap_out, swap_in,
    xs2, xr2, sums2, near2, mid2, last2, swap_out2, swap_in2,
    ff_buf, hidden,
):
    x, z, c = place()
    loads = [
        pltpu.make_async_copy(w_out_hbm, w_out, load_sems.at[0]),
        pltpu.make_async_copy(w_gu_hbm, w_gu, load_sems.at[1]),
        pltpu.make_async_copy(w_down_hbm, w_down, load_sems.at[2]),
    ]
    for load in loads:
        load.start()
    greet([
        {"hid": moved(1, 0)}, {"hid": moved(-1, 0)}, {"hid": moved(0, 1)},
        {"hid": moved(0, -1)}, {"hid": moved(0, 0, 1)},
    ])
    mail = Mail(send_sems, recv_sems)
    width = w_out.shape[1] // 2
    step = width // 2

    def product_of(lhs, weight):
        def product(chips, half, out, other):
            rows = jnp.concatenate(
                [lhs[pl.ds(pl.multiple_of(chip * 64, 64), 64), :] for chip in chips], axis=0
            )
            for n in range(2):
                at = pl.ds(n * step, step)
                cols = pl.ds(pl.multiple_of(half * width + n * step, 128), step)
                value = jnp.dot(rows, weight[:, cols], preferred_element_type=jnp.float32)
                if other is not None:
                    value = value + other[:, at].astype(jnp.float32)
                out[:, at] = value.astype(out.dtype)
        return product

    mine_at = pl.ds(pl.multiple_of(c * width, 128), width)
    other_at = pl.ds(pl.multiple_of((1 - c) * width, 128), width)

    loads[0].wait()
    mine = reduce_rows(
        mail, 0, product_of(heads_ref, w_out), width,
        xs, xr, sums, acc, near, mid, last, swap_out, swap_in,
    )
    other = swap_in[...]
    attn_ref[:, mine_at] = mine.astype(jnp.bfloat16)
    attn_ref[:, other_at] = other.astype(jnp.bfloat16)
    total = jnp.sum(mine * mine, axis=1, keepdims=True) + jnp.sum(other * other, axis=1, keepdims=True)
    scale = lax.rsqrt(total / (2 * width) + EPS)
    own_rows = pl.ds(pl.multiple_of(moved(0, 0) * 32, 32), 32)
    ff_buf[own_rows, mine_at] = (mine * scale * gain_ref[:, mine_at]).astype(jnp.bfloat16)
    ff_buf[own_rows, other_at] = (other * scale * gain_ref[:, other_at]).astype(jnp.bfloat16)

    gather_rows(mail, SCATTER_ROLES, ff_buf, 32)

    units = w_down.shape[0]
    loads[1].wait()

    @pl.loop(0, 4)
    def _(i):
        at = pl.ds(pl.multiple_of(i * 256, 256), 256)
        rows = ff_buf[at, :]
        contract = (((1,), (1,)), ((), ()))
        gate = lax.dot_general(rows, w_gu[pl.ds(0, units), :], contract, preferred_element_type=jnp.float32)
        up = lax.dot_general(rows, w_gu[pl.ds(units, units), :], contract, preferred_element_type=jnp.float32)
        hidden[at, :] = (jax.nn.silu(gate) * up).astype(jnp.bfloat16)

    loads[2].wait()
    mine = reduce_rows(
        mail, SCATTER_ROLES + GATHER_ROLES, product_of(hidden, w_down), width,
        xs2, xr2, sums2, acc, near2, mid2, last2, swap_out2, swap_in2,
    )
    block_ref[:, mine_at] = mine.astype(jnp.bfloat16)
    block_ref[:, other_at] = swap_in2[...].astype(jnp.bfloat16)
    mail.drain()


def tail(heads_out, w_out, gain_ff, w_gu, w_down):
    tok_grp = heads_out.shape[0]
    width = w_out.shape[1]
    half = width // 2
    units = w_down.shape[0]
    bf16, f32 = jnp.bfloat16, jnp.float32
    vmem = pl.BlockSpec(memory_space=pltpu.VMEM)
    anywhere = pl.BlockSpec(memory_space=pl.ANY)

    def travel():
        return [
            pltpu.VMEM((4, 256, half), bf16), pltpu.VMEM((4, 256, half), bf16),
            pltpu.VMEM((4, 256, half), bf16),
        ]

    def landing():
        return [
            pltpu.VMEM((2, 256, half), bf16), pltpu.VMEM((2, 256, half), bf16),
            pltpu.VMEM((6, 32, half), bf16), pltpu.VMEM((32, half), f32), pltpu.VMEM((32, half), f32),
        ]

    return pl.pallas_call(
        tail_kernel,
        out_shape=(jax.ShapeDtypeStruct((32, width), bf16), jax.ShapeDtypeStruct((32, width), bf16)),
        in_specs=[vmem, anywhere, vmem, anywhere, anywhere],
        out_specs=(vmem, vmem),
        scratch_shapes=[
            pltpu.VMEM(w_out.shape, bf16), pltpu.VMEM(w_gu.shape, bf16), pltpu.VMEM(w_down.shape, bf16),
            pltpu.SemaphoreType.DMA((3,)), pltpu.SemaphoreType.DMA((TAIL_ROLES,)),
            pltpu.SemaphoreType.DMA((TAIL_ROLES,)),
            *travel(), pltpu.VMEM((256, half), f32), *landing(),
            *travel(), *landing(),
            pltpu.VMEM((tok_grp, width), bf16), pltpu.VMEM((tok_grp, units), bf16),
        ],
        compiler_params=pltpu.CompilerParams(
            collective_id=0, has_side_effects=True, vmem_limit_bytes=66000000
        ),
        name="tail",
    )(heads_out, w_out, gain_ff.reshape(1, width), w_gu, w_down)


def per_device(
    tokens,
    gain_in,
    w_qkv,
    adapt_down,
    adapt_up,
    w_out,
    gain_ff,
    w_gate_up,
    w_down,
    prefix_cache,
    prefix_owner,
    group_prefix,
    lengths,
):
    tok_dev = tokens.shape[0]
    width_in = tokens.shape[1]
    head_cols = w_qkv.shape[2]
    head_count = head_cols // HD
    model_width = w_out.shape[1]
    normed = rms_scale(tokens.astype(jnp.float32), gain_in).astype(jnp.bfloat16)
    latent = jnp.dot(normed, adapt_down, preferred_element_type=jnp.float32).astype(jnp.bfloat16)
    row_block = jnp.concatenate([normed, latent], axis=1)
    joint_weight = w_qkv.reshape(width_in, 3 * head_cols)
    shard_rows = lax.all_gather(row_block, "hid", axis=0, tiled=True)
    joint = jnp.dot(shard_rows[:, :width_in], joint_weight, preferred_element_type=jnp.float32)
    query_part = joint[:, :head_cols] + jnp.dot(
        shard_rows[:, width_in:], adapt_up, preferred_element_type=jnp.float32
    )
    projected = jnp.concatenate([query_part, joint[:, head_cols:]], axis=1).astype(jnp.bfloat16)
    tok_grp = projected.shape[0]
    queries = projected[:, :head_cols].reshape(tok_grp, head_count, HD)
    suffix_keys = projected[:, head_cols : 2 * head_cols].reshape(tok_grp, head_count, HD)
    suffix_vals = projected[:, 2 * head_cols :].reshape(tok_grp, head_count, HD)
    request_ends = jnp.cumsum(lengths[0])
    position = jnp.arange(tok_grp, dtype=jnp.int32)
    request = jnp.sum((position[:, None] >= request_ends[None, :]).astype(jnp.int32), axis=1)
    allowed = jnp.logical_and(
        request[:, None] == request[None, :], position[None, :] <= position[:, None]
    )
    partial_value = suffix_part(queries, suffix_keys, suffix_vals, allowed)
    group_index = lax.axis_index("req")
    target = prefix_owner[group_prefix[group_index]]
    heads_cache = lax.all_to_all(prefix_cache[0], "hid", split_axis=2, concat_axis=0, tiled=True)
    span_len = heads_cache.shape[0]
    shard_rows = lax.all_gather(heads_cache, "req", axis=0, tiled=True)
    slot_count = shard_rows.shape[0] // span_len
    inside = jnp.logical_and(target >= 0, target < slot_count)
    chosen = lax.dynamic_slice_in_dim(
        shard_rows, jnp.clip(target, 0, slot_count - 1) * span_len, span_len, 0
    )
    partial_value = lax.cond(
        inside,
        lambda kept: combine(kept, prefix_part(queries, chosen)),
        lambda kept: kept,
        partial_value,
    )
    heads_out = (partial_value[2] / partial_value[1][..., None]).astype(jnp.bfloat16)
    unit_count = w_gate_up.shape[2]
    w_gu = jnp.transpose(w_gate_up, (1, 2, 0)).reshape(2 * unit_count, model_width)
    attn_out, block_out = tail(heads_out.reshape(tok_grp, head_cols), w_out, gain_ff, w_gu, w_down)
    return (attn_out, block_out)


def solution(mesh):
    placed = (
        P(("req", "hid"), None),
        P(),
        P(None, None, "hid"),
        P(),
        P(None, "hid"),
        P("hid", None),
        P(),
        P(None, None, "hid"),
        P("hid", None),
        P("req", "hid", None, None),
        P(),
        P(),
        P("req", None),
    )
    return jax.shard_map(
        per_device,
        mesh=mesh,
        in_specs=placed,
        out_specs=(P(("req", "hid"), None), P(("req", "hid"), None)),
        check_vma=False,
    )
```

```python
import jax
import jax.numpy as jnp
from jax import lax
from jax.experimental import pallas as pl
from jax.experimental.pallas import tpu as pltpu
from jax.sharding import PartitionSpec as P

HD = 224


EPS = 1e-05


def rms_scale(matrix, gain_vec):
    return matrix * lax.rsqrt(jnp.mean(matrix * matrix, axis=-1, keepdims=True) + EPS) * gain_vec


MESH = pl.DeviceIdType.MESH
NX, NZ = 4, 4


def place():
    hid = lax.axis_index("hid")
    return hid // 8, (hid // 2) % 4, hid % 2


def moved(da, db, core_flip=0):
    x, z, c = place()
    xn = (x + 4 + (1 - c) * db + c * da) % 4
    zn = (z + 4 + (1 - c) * da + c * db) % 4
    cn = c + core_flip * (1 - 2 * c)
    return xn * 8 + zn * 2 + cn


def remote(src, dst, send, recv, hid):
    return pltpu.make_async_remote_copy(
        src_ref=src, dst_ref=dst, send_sem=send, recv_sem=recv,
        device_id={"hid": hid}, device_id_type=MESH,
    )


def greet(peers):
    barrier = pltpu.get_barrier_semaphore()
    for peer in peers:
        pl.semaphore_signal(barrier, inc=1, device_id=peer, device_id_type=MESH)
    pl.semaphore_wait(barrier, len(peers))


class Mail:
    def __init__(self, send_sems, recv_sems):
        self.send_sems, self.recv_sems, self.sent = send_sems, recv_sems, []

    def send(self, role, src, dst, hid):
        copy = remote(src, dst, self.send_sems.at[role], self.recv_sems.at[role], hid)
        copy.start()
        self.sent.append(copy)

    def await_recv(self, role, dst, hid):
        remote(dst, dst, self.send_sems.at[role], self.recv_sems.at[role], hid).wait_recv()

    def drain(self):
        for copy in self.sent:
            copy.wait_send()


GATHER_ROLES = 36


def gather_rows(mail, base, buf, rows):
    half = rows // 2
    x, z, c = place()

    def blk(hid, part=None):
        start = pl.multiple_of(hid * rows, rows)
        if part is None:
            return buf.at[pl.ds(start, rows)]
        return buf.at[pl.ds(start + part * half, half)]

    offs = (0, -1, 1, 2)
    a_plus, a_minus = moved(1, 0), moved(-1, 0)
    b_plus, b_minus = moved(0, 1), moved(0, -1)
    partner = moved(0, 0, 1)

    def role2(i, k):
        return base + 4 + 4 * i + k

    def to_partner(ia, ib):
        owner = moved(offs[ia], offs[ib])
        mail.send(base + 20 + ia * 4 + ib, blk(owner), blk(owner), partner)

    def line_out(i):
        owner = moved(0, offs[i])
        mail.send(role2(i, 0), blk(owner), blk(owner), a_plus)
        mail.send(role2(i, 1), blk(owner), blk(owner), a_minus)

    def line_relay(i):
        low, high = moved(-1, offs[i]), moved(1, offs[i])
        mail.await_recv(role2(i, 0), blk(low), a_minus)
        mail.send(role2(i, 2), blk(low, 0), blk(low, 0), a_plus)
        mail.await_recv(role2(i, 1), blk(high), a_plus)
        mail.send(role2(i, 3), blk(high, 1), blk(high, 1), a_minus)
        to_partner(1, i)
        to_partner(2, i)

    def line_far(i):
        far = moved(2, offs[i])
        mail.await_recv(role2(i, 2), blk(far, 0), a_minus)
        mail.await_recv(role2(i, 3), blk(far, 1), a_plus)
        to_partner(3, i)

    own = moved(0, 0)
    mail.send(base + 0, blk(own), blk(own), b_plus)
    mail.send(base + 1, blk(own), blk(own), b_minus)
    line_out(0)
    to_partner(0, 0)
    low, high = moved(0, -1), moved(0, 1)
    mail.await_recv(base + 0, blk(low), b_minus)
    mail.send(base + 2, blk(low, 0), blk(low, 0), b_plus)
    line_out(1)
    to_partner(0, 1)
    mail.await_recv(base + 1, blk(high), b_plus)
    mail.send(base + 3, blk(high, 1), blk(high, 1), b_minus)
    line_out(2)
    to_partner(0, 2)
    line_relay(0)
    yield "relay0"
    far = moved(0, 2)
    mail.await_recv(base + 2, blk(far, 0), b_minus)
    mail.await_recv(base + 3, blk(far, 1), b_plus)
    line_out(3)
    to_partner(0, 3)
    line_relay(1)
    yield "relay1"
    line_relay(2)
    yield "relay2"
    line_far(0)
    yield "far0"
    line_relay(3)
    yield "relay3"
    line_far(1)
    yield "far1"
    line_far(2)
    yield "far2"
    line_far(3)
    yield "far3"

    def from_partner(ia, ib):
        owner = moved(offs[ib], offs[ia], 1)
        mail.await_recv(base + 20 + ia * 4 + ib, blk(owner), partner)

    for ia in range(4):
        for ib in range(4):
            from_partner(ia, ib)


SCATTER_ROLES = 17


def reduce_rows(mail, base, product, width, xs, xr, sums, acc, near, mid, last, swap_out, swap_in):
    x, z, c = place()
    a = (1 - c) * z + c * x
    b = (1 - c) * x + c * z
    partner = moved(0, 0, 1)
    a_plus, a_minus = moved(1, 0), moved(-1, 0)
    b_plus, b_minus = moved(0, 1), moved(0, -1)
    steps = (2, 1, 3, 0)

    def set_chips(k, cc):
        return [(1 - cc) * (j * 4 + k) + cc * (k * 4 + j) for j in range(4)]

    def partner_part(idx):
        k = (b + steps[idx]) % 4
        product(set_chips(k, 1 - c), 1 - c, xs.at[idx], None)
        mail.send(base + idx, xs.at[idx], xr.at[idx], partner)

    def own_part(idx, out):
        k = (a + steps[idx]) % 4
        mail.await_recv(base + idx, xr.at[idx], partner)
        product(set_chips(k, c), c, out, xr.at[idx])

    lo, hi = pl.ds(0, 128), pl.ds(128, 128)
    partner_part(0)
    partner_part(1)
    own_part(0, sums.at[0])
    mail.send(base + 4, sums.at[0, lo], near.at[0, lo], a_plus)
    mail.send(base + 5, sums.at[0, hi], near.at[1, hi], a_minus)
    partner_part(2)
    own_part(1, sums.at[1])
    mail.send(base + 6, sums.at[1, hi], mid.at[0, hi], a_plus)
    partner_part(3)
    own_part(2, sums.at[2])
    mail.send(base + 7, sums.at[2, lo], mid.at[1, lo], a_minus)
    mail.await_recv(base + 4, near.at[0, lo], a_minus)
    sums[1, lo] = (sums[1, lo].astype(jnp.float32) + near[0, lo].astype(jnp.float32)).astype(jnp.bfloat16)
    mail.send(base + 8, sums.at[1, lo], mid.at[0, lo], a_plus)
    mail.await_recv(base + 5, near.at[1, hi], a_plus)
    sums[2, hi] = (sums[2, hi].astype(jnp.float32) + near[1, hi].astype(jnp.float32)).astype(jnp.bfloat16)
    mail.send(base + 9, sums.at[2, hi], mid.at[1, hi], a_minus)
    own_part(3, acc)
    mail.await_recv(base + 6, mid.at[0, hi], a_minus)
    mail.await_recv(base + 7, mid.at[1, lo], a_plus)
    mail.await_recv(base + 8, mid.at[0, lo], a_minus)
    mail.await_recv(base + 9, mid.at[1, hi], a_plus)

    def chunk(j, low, size):
        return pl.ds(pl.multiple_of(j * 64 + low, 32), size)

    def chunk_sum(j, low, size):
        at = chunk(j, low, size)
        return acc[at] + mid[0, at].astype(jnp.float32) + mid[1, at].astype(jnp.float32)

    far, up, down, own = (b + 2) % 4, (b + 1) % 4, (b + 3) % 4, b
    q = sums.at[3]
    q[chunk(far, 0, 64)] = chunk_sum(far, 0, 64).astype(jnp.bfloat16)
    mail.send(base + 10, q.at[chunk(far, 0, 32)], last.at[0], b_plus)
    mail.send(base + 11, q.at[chunk(far, 32, 32)], last.at[1], b_minus)
    q[chunk(up, 32, 32)] = chunk_sum(up, 32, 32).astype(jnp.bfloat16)
    mail.send(base + 12, q.at[chunk(up, 32, 32)], last.at[2], b_plus)
    q[chunk(down, 0, 32)] = chunk_sum(down, 0, 32).astype(jnp.bfloat16)
    mail.send(base + 13, q.at[chunk(down, 0, 32)], last.at[3], b_minus)
    mail.await_recv(base + 10, last.at[0], b_minus)
    q[chunk(up, 0, 32)] = (chunk_sum(up, 0, 32) + last[0].astype(jnp.float32)).astype(jnp.bfloat16)
    mail.send(base + 14, q.at[chunk(up, 0, 32)], last.at[4], b_plus)
    mail.await_recv(base + 11, last.at[1], b_plus)
    q[chunk(down, 32, 32)] = (chunk_sum(down, 32, 32) + last[1].astype(jnp.float32)).astype(jnp.bfloat16)
    mail.send(base + 15, q.at[chunk(down, 32, 32)], last.at[5], b_minus)
    top, bottom = chunk_sum(own, 0, 32), chunk_sum(own, 32, 32)
    mail.await_recv(base + 12, last.at[2], b_minus)
    mail.await_recv(base + 13, last.at[3], b_plus)
    mail.await_recv(base + 14, last.at[4], b_minus)
    mail.await_recv(base + 15, last.at[5], b_plus)
    top = top + last[3].astype(jnp.float32) + last[4].astype(jnp.float32)
    bottom = bottom + last[2].astype(jnp.float32) + last[5].astype(jnp.float32)
    is_first = c == 0
    swap_out[...] = jnp.where(is_first, bottom, top)
    mail.send(base + 16, swap_out, swap_in, partner)
    mine = jnp.where(is_first, top, bottom)
    mail.await_recv(base + 16, swap_in, partner)
    return mine


TAIL_ROLES = SCATTER_ROLES * 2 + GATHER_ROLES


def tail_kernel(
    heads_ref, w_out_hbm, gain_ref, w_gu_hbm, w_down_hbm, attn_ref, block_ref,
    w_out, w_gu, w_down, load_sems, send_sems, recv_sems,
    xs, xr, sums, acc, near, mid, last, swap_out, swap_in,
    xs2, xr2, sums2, near2, mid2, last2, swap_out2, swap_in2,
    ff_buf, hidden,
):
    x, z, c = place()
    loads = [
        pltpu.make_async_copy(w_out_hbm, w_out, load_sems.at[0]),
        pltpu.make_async_copy(w_gu_hbm, w_gu, load_sems.at[1]),
        pltpu.make_async_copy(w_down_hbm, w_down, load_sems.at[2]),
    ]
    for load in loads:
        load.start()
    greet([
        {"hid": moved(1, 0)}, {"hid": moved(-1, 0)}, {"hid": moved(0, 1)},
        {"hid": moved(0, -1)}, {"hid": moved(0, 0, 1)},
    ])
    mail = Mail(send_sems, recv_sems)
    width = w_out.shape[1] // 2
    step = width // 2

    def product_of(lhs, weight):
        def product(chips, half, out, other):
            rows = jnp.concatenate(
                [lhs[pl.ds(pl.multiple_of(chip * 64, 64), 64), :] for chip in chips], axis=0
            )
            for n in range(2):
                at = pl.ds(n * step, step)
                cols = pl.ds(pl.multiple_of(half * width + n * step, 128), step)
                value = jnp.dot(rows, weight[:, cols], preferred_element_type=jnp.float32)
                if other is not None:
                    value = value + other[:, at].astype(jnp.float32)
                out[:, at] = value.astype(out.dtype)
        return product

    mine_at = pl.ds(pl.multiple_of(c * width, 128), width)
    other_at = pl.ds(pl.multiple_of((1 - c) * width, 128), width)

    loads[0].wait()
    mine = reduce_rows(
        mail, 0, product_of(heads_ref, w_out), width,
        xs, xr, sums, acc, near, mid, last, swap_out, swap_in,
    )
    other = swap_in[...]
    attn_ref[:, mine_at] = mine.astype(jnp.bfloat16)
    attn_ref[:, other_at] = other.astype(jnp.bfloat16)
    total = jnp.sum(mine * mine, axis=1, keepdims=True) + jnp.sum(other * other, axis=1, keepdims=True)
    scale = lax.rsqrt(total / (2 * width) + EPS)
    own_rows = pl.ds(pl.multiple_of(moved(0, 0) * 32, 32), 32)
    ff_buf[own_rows, mine_at] = (mine * scale * gain_ref[:, mine_at]).astype(jnp.bfloat16)
    ff_buf[own_rows, other_at] = (other * scale * gain_ref[:, other_at]).astype(jnp.bfloat16)

    for _ in gather_rows(mail, SCATTER_ROLES, ff_buf, 32):
        pass

    units = w_down.shape[0]
    loads[1].wait()

    @pl.loop(0, 4)
    def _(i):
        at = pl.ds(pl.multiple_of(i * 256, 256), 256)
        rows = ff_buf[at, :]
        contract = (((1,), (1,)), ((), ()))
        gate = lax.dot_general(rows, w_gu[pl.ds(0, units), :], contract, preferred_element_type=jnp.float32)
        up = lax.dot_general(rows, w_gu[pl.ds(units, units), :], contract, preferred_element_type=jnp.float32)
        hidden[at, :] = (jax.nn.silu(gate) * up).astype(jnp.bfloat16)

    loads[2].wait()
    mine = reduce_rows(
        mail, SCATTER_ROLES + GATHER_ROLES, product_of(hidden, w_down), width,
        xs2, xr2, sums2, acc, near2, mid2, last2, swap_out2, swap_in2,
    )
    block_ref[:, mine_at] = mine.astype(jnp.bfloat16)
    block_ref[:, other_at] = swap_in2[...].astype(jnp.bfloat16)
    mail.drain()


def tail(heads_out, w_out, gain_ff, w_gu, w_down):
    tok_grp = heads_out.shape[0]
    width = w_out.shape[1]
    half = width // 2
    units = w_down.shape[0]
    bf16, f32 = jnp.bfloat16, jnp.float32
    vmem = pl.BlockSpec(memory_space=pltpu.VMEM)
    anywhere = pl.BlockSpec(memory_space=pl.ANY)

    def travel():
        return [
            pltpu.VMEM((4, 256, half), bf16), pltpu.VMEM((4, 256, half), bf16),
            pltpu.VMEM((4, 256, half), bf16),
        ]

    def landing():
        return [
            pltpu.VMEM((2, 256, half), bf16), pltpu.VMEM((2, 256, half), bf16),
            pltpu.VMEM((6, 32, half), bf16), pltpu.VMEM((32, half), f32), pltpu.VMEM((32, half), f32),
        ]

    return pl.pallas_call(
        tail_kernel,
        out_shape=(jax.ShapeDtypeStruct((32, width), bf16), jax.ShapeDtypeStruct((32, width), bf16)),
        in_specs=[vmem, anywhere, vmem, anywhere, anywhere],
        out_specs=(vmem, vmem),
        scratch_shapes=[
            pltpu.VMEM(w_out.shape, bf16), pltpu.VMEM(w_gu.shape, bf16), pltpu.VMEM(w_down.shape, bf16),
            pltpu.SemaphoreType.DMA((3,)), pltpu.SemaphoreType.DMA((TAIL_ROLES,)),
            pltpu.SemaphoreType.DMA((TAIL_ROLES,)),
            *travel(), pltpu.VMEM((256, half), f32), *landing(),
            *travel(), *landing(),
            pltpu.VMEM((tok_grp, width), bf16), pltpu.VMEM((tok_grp, units), bf16),
        ],
        compiler_params=pltpu.CompilerParams(
            collective_id=0, has_side_effects=True, vmem_limit_bytes=66000000
        ),
        name="tail",
    )(heads_out, w_out, gain_ff.reshape(1, width), w_gu, w_down)


FRONT_BLOCKS = 36
WINDOW = 768


def front_kernel(
    owner_ref, lengths_ref, tokens_ref, gain_ref, down_ref, up_ref, w_hbm, cache_hbm, heads_ref,
    w_qkv, rows_buf, load_sems, send_sems, recv_sems,
    first_0, first_1, second_0, second_1, pass_0, pass_1, split_0, split_1,
    prefix, qkv,
):
    x, z, c = place()
    hid = lax.axis_index("hid")
    req = lax.axis_index("req")
    lower, upper = (req + 3) % 4, (req + 1) % 4
    width = tokens_ref.shape[1]
    bf16, f32 = jnp.bfloat16, jnp.float32
    first, second = (first_0, first_1), (second_0, second_1)
    passed, split = (pass_0, pass_1), (split_0, split_1)

    loads = []
    for k in range(2):
        for half in range(2):
            copy = pltpu.make_async_copy(
                cache_hbm.at[pl.ds(half * 32 + k * 16, 16)], first[k].at[half], load_sems.at[1 + 2 * k + half]
            )
            copy.start()
            loads.append(copy)
    w_load = pltpu.make_async_copy(w_hbm, w_qkv, load_sems.at[0])
    w_load.start()

    peers = [{"hid": (hid + d) % 32} for d in range(1, 32)] + [{"req": lower}, {"req": upper}]
    barrier = pltpu.get_barrier_semaphore()
    for peer in peers:
        pl.semaphore_signal(barrier, inc=1, device_id=peer, device_id_type=MESH)
    matrix = tokens_ref[...].astype(f32)
    normed = rms_scale(matrix, gain_ref[...]).astype(bf16)
    own_rows = pl.ds(pl.multiple_of(hid * 32, 32), 32)
    rows_buf[own_rows, pl.ds(0, width)] = normed
    latent = jnp.dot(normed, down_ref[...], preferred_element_type=f32)
    rows_buf[own_rows, pl.ds(width, 128)] = latent.astype(bf16)
    pl.semaphore_wait(barrier, len(peers))

    mail = Mail(send_sems, recv_sems)
    y_base = GATHER_ROLES
    deal_base = y_base + 8

    def y_copy(role, src, dst, to):
        return pltpu.make_async_remote_copy(
            src_ref=src, dst_ref=dst, send_sem=send_sems.at[role], recv_sem=recv_sems.at[role],
            device_id={"req": to}, device_id_type=MESH,
        )

    def y_send(role, src, dst, to):
        copy = y_copy(role, src, dst, to)
        copy.start()
        mail.sent.append(copy)

    def y_start():
        for k in range(2):
            y_send(y_base + k, cache_hbm.at[pl.ds(k * 16, 16)], first[k].at[2], lower)
            y_send(y_base + 2 + k, cache_hbm.at[pl.ds(32 + k * 16, 16)], first[k].at[3], upper)

    def y_pass(k):
        loads[2 * k].wait()
        loads[2 * k + 1].wait()
        y_copy(y_base + k, first[k].at[2], first[k].at[2], upper).wait_recv()
        y_copy(y_base + 2 + k, first[k].at[3], first[k].at[3], lower).wait_recv()
        passed[k][0] = first[k][jnp.where(owner_ref[lower] == req, 1, 2)]
        y_send(y_base + 4 + k, passed[k].at[0], second[k].at[0], lower)
        passed[k][1] = first[k][jnp.where(owner_ref[upper] == req, 0, 3)]
        y_send(y_base + 6 + k, passed[k].at[1], second[k].at[1], upper)

    def deal(k):
        y_copy(y_base + 4 + k, second[k].at[0], second[k].at[0], upper).wait_recv()
        y_copy(y_base + 6 + k, second[k].at[1], second[k].at[1], lower).wait_recv()
        away = (owner_ref[req] - req + 4) % 4
        late_a = jnp.full((1, 1, 1), (away >= 2).astype(jnp.int32)) > 0
        late_b = jnp.full((1, 1, 1), jnp.logical_or(away == 1, away == 2).astype(jnp.int32)) > 0
        half_a = jnp.where(late_a, second[k][jnp.where(away == 2, 0, 1)], first[k][jnp.where(away == 0, 0, 2)])
        half_b = jnp.where(late_b, second[k][jnp.where(away == 1, 0, 1)], first[k][jnp.where(away == 0, 1, 3)])
        r = lax.broadcasted_iota(jnp.int32, (32, 32), 0)
        s = lax.broadcasted_iota(jnp.int32, (32, 32), 1)
        sort = (s == jnp.where(r < 16, 2 * r, 2 * r - 31)).astype(bf16)
        zeros = jnp.zeros((16, 256 - HD), bf16)
        for half, value in enumerate((half_a, half_b)):
            planes = jnp.dot(sort, value.reshape(32, width), preferred_element_type=f32).astype(bf16)
            for kv in range(2):
                for h in range(32):
                    piece = planes[kv * 16:(kv + 1) * 16, h * HD:(h + 1) * HD]
                    split[k][h, kv, pl.ds(half * 16, 16), :] = jnp.concatenate([piece, zeros], axis=1)

        landing = prefix.at[:, pl.ds(pl.multiple_of(hid * 64 + k * 32, 32), 32)]
        for d in range(1, 32):
            to = (hid + d) % 32
            mail.send(deal_base + k * 31 + d - 1, split[k].at[to], landing, to)
        prefix[:, pl.ds(pl.multiple_of(hid * 64 + k * 32, 32), 32)] = split[k][hid]

    def deal_done():
        for k in range(2):
            for d in range(1, 32):
                source = (hid + 32 - d) % 32
                landing = prefix.at[:, pl.ds(pl.multiple_of(source * 64 + k * 32, 32), 32)]
                mail.await_recv(deal_base + k * 31 + d - 1, landing, source)

    y_start()
    for stage in gather_rows(mail, 0, rows_buf, 32):
        if stage == "relay0":
            y_pass(0)
        if stage == "relay2":
            y_pass(1)
        if stage == "far1":
            deal(0)
    deal(1)

    w_load.wait()
    contract = (((1,), (1,)), ((), ()))
    pad = jnp.zeros((256, 256 - HD), bf16)

    @pl.loop(0, 4)
    def _(i):
        at = pl.ds(pl.multiple_of(i * 256, 256), 256)
        rows = rows_buf[at, pl.ds(0, width)]
        for part in range(3):
            value = lax.dot_general(
                rows, w_qkv[pl.ds(part * HD, HD), :], contract, preferred_element_type=f32
            )
            if part == 0:
                value = value + lax.dot_general(
                    rows_buf[at, pl.ds(width, 128)], up_ref[...], contract, preferred_element_type=f32
                )
            qkv[part, at, :] = jnp.concatenate([value.astype(bf16), pad], axis=1)

    deal_done()

    ends = [lengths_ref[0, 0]]
    for n in range(1, lengths_ref.shape[1]):
        ends.append(ends[-1] + lengths_ref[0, n])
    factor = HD ** (-0.5)

    @pl.loop(0, 8)
    def _(i):
        at = pl.ds(pl.multiple_of(i * 128, 128), 128)
        begin = jnp.maximum(i * 128 - 512, 0) // 128 * 128
        begin = jnp.minimum(begin, 1024 - WINDOW)
        near = pl.ds(pl.multiple_of(begin, 128), WINDOW)
        q = qkv[0, at, :]
        s_far = lax.dot_general(q, prefix[0], contract, preferred_element_type=f32) * factor
        s_near = lax.dot_general(q, qkv[1, near, :], contract, preferred_element_type=f32) * factor
        row = lax.broadcasted_iota(jnp.int32, (128, 1), 0) + i * 128
        since = jnp.zeros((128, 1), jnp.int32)
        for end in ends:
            since = jnp.where(row >= end, jnp.maximum(since, end), since)
        col = lax.broadcasted_iota(jnp.int32, (128, WINDOW), 1) + begin
        s_near = jnp.where(jnp.logical_and(col >= since, col <= row), s_near, -jnp.inf)
        row_max = jnp.maximum(
            jnp.max(s_far, axis=1, keepdims=True), jnp.max(s_near, axis=1, keepdims=True)
        )
        e_far = jnp.exp(s_far - row_max)
        e_near = jnp.exp(s_near - row_max)
        row_sum = jnp.sum(e_far, axis=1, keepdims=True) + jnp.sum(e_near, axis=1, keepdims=True)
        out = jnp.dot(e_far.astype(bf16), prefix[1], preferred_element_type=f32)
        out = out + jnp.dot(e_near.astype(bf16), qkv[2, near, :], preferred_element_type=f32)
        heads_ref[at, :] = (out / row_sum)[:, :HD].astype(bf16)

    mail.drain()


def front(owners, lengths, tokens, gain_in, adapt_down, up_t, w_t, cache):
    rows, width = tokens.shape
    tok_grp = rows * 32
    bf16 = jnp.bfloat16
    smem = pl.BlockSpec(memory_space=pltpu.SMEM)
    vmem = pl.BlockSpec(memory_space=pltpu.VMEM)
    anywhere = pl.BlockSpec(memory_space=pl.ANY)
    roles = GATHER_ROLES + 8 + 62

    def halves(count):
        return pltpu.VMEM((count, 16, 2, width), bf16)

    return pl.pallas_call(
        front_kernel,
        out_shape=jax.ShapeDtypeStruct((tok_grp, HD), bf16),
        in_specs=[smem, smem, vmem, vmem, vmem, vmem, anywhere, anywhere],
        out_specs=vmem,
        scratch_shapes=[
            pltpu.VMEM(w_t.shape, bf16), pltpu.VMEM((tok_grp, width + 128), bf16),
            pltpu.SemaphoreType.DMA((5,)), pltpu.SemaphoreType.DMA((roles,)),
            pltpu.SemaphoreType.DMA((roles,)),
            halves(4), halves(4), halves(2), halves(2), halves(2), halves(2),
            pltpu.VMEM((32, 2, 32, 256), bf16), pltpu.VMEM((32, 2, 32, 256), bf16),
            pltpu.VMEM((2, 2048, 256), bf16), pltpu.VMEM((3, tok_grp, 256), bf16),
        ],
        compiler_params=pltpu.CompilerParams(
            collective_id=1, has_side_effects=True, vmem_limit_bytes=66000000
        ),
        name="front",
    )(owners, lengths, tokens, gain_in.reshape(1, width), adapt_down, up_t, w_t, cache)


def per_device(
    tokens,
    gain_in,
    w_qkv,
    adapt_down,
    adapt_up,
    w_out,
    gain_ff,
    w_gate_up,
    w_down,
    prefix_cache,
    prefix_owner,
    group_prefix,
    lengths,
):
    w_t = jnp.transpose(w_qkv, (1, 2, 0)).reshape(3 * w_qkv.shape[2], w_qkv.shape[0])
    w_gu = jnp.transpose(w_gate_up, (1, 2, 0)).reshape(2 * w_gate_up.shape[2], w_gate_up.shape[0])
    heads_out = front(
        prefix_owner[group_prefix], lengths, tokens, gain_in, adapt_down, adapt_up.T, w_t, prefix_cache[0]
    )
    return tail(heads_out, w_out, gain_ff, w_gu, w_down)


def solution(mesh):
    placed = (
        P(("req", "hid"), None),
        P(),
        P(None, None, "hid"),
        P(),
        P(None, "hid"),
        P("hid", None),
        P(),
        P(None, None, "hid"),
        P("hid", None),
        P("req", "hid", None, None),
        P(),
        P(),
        P("req", None),
    )
    return jax.shard_map(
        per_device,
        mesh=mesh,
        in_specs=placed,
        out_specs=(P(("req", "hid"), None), P(("req", "hid"), None)),
        check_vma=False,
    )
```

```python
import jax
import jax.numpy as jnp
from jax import lax
from jax.experimental import pallas as pl
from jax.experimental.pallas import tpu as pltpu
from jax.sharding import PartitionSpec as P

HD = 224


EPS = 1e-05


def rms_scale(matrix, gain_vec):
    return matrix * lax.rsqrt(jnp.mean(matrix * matrix, axis=-1, keepdims=True) + EPS) * gain_vec


MESH = pl.DeviceIdType.MESH
NX, NZ = 4, 4


def place():
    hid = lax.axis_index("hid")
    return hid // 8, (hid // 2) % 4, hid % 2


def moved(da, db, core_flip=0):
    x, z, c = place()
    xn = (x + 4 + (1 - c) * db + c * da) % 4
    zn = (z + 4 + (1 - c) * da + c * db) % 4
    cn = c + core_flip * (1 - 2 * c)
    return xn * 8 + zn * 2 + cn


def remote(src, dst, send, recv, hid):
    return pltpu.make_async_remote_copy(
        src_ref=src, dst_ref=dst, send_sem=send, recv_sem=recv,
        device_id={"hid": hid}, device_id_type=MESH,
    )


def greet(peers):
    barrier = pltpu.get_barrier_semaphore()
    for peer in peers:
        pl.semaphore_signal(barrier, inc=1, device_id=peer, device_id_type=MESH)
    pl.semaphore_wait(barrier, len(peers))


class Mail:
    def __init__(self, send_sems, recv_sems):
        self.send_sems, self.recv_sems, self.sent = send_sems, recv_sems, {}

    def send(self, role, src, dst, hid):
        copy = remote(src, dst, self.send_sems.at[role], self.recv_sems.at[role], hid)
        copy.start()
        self.sent[role] = copy

    def release(self, *roles):
        for role in roles:
            self.sent.pop(role).wait_send()

    def await_recv(self, role, dst, hid):
        remote(dst, dst, self.send_sems.at[role], self.recv_sems.at[role], hid).wait_recv()

    def drain(self):
        for copy in self.sent.values():
            copy.wait_send()


GATHER_ROLES = 36
OFFS = (0, -1, 1, 2)


class Gather:
    def __init__(self, mail, base, buf, rows):
        self.mail, self.base, self.buf, self.rows = mail, base, buf, rows
        self.a_plus, self.a_minus = moved(1, 0), moved(-1, 0)
        self.b_plus, self.b_minus = moved(0, 1), moved(0, -1)
        self.partner = moved(0, 0, 1)
        self.seen = set()

    def blk(self, hid, part=None):
        start = pl.multiple_of(hid * self.rows, self.rows)
        if part is None:
            return self.buf.at[pl.ds(start, self.rows)]
        half = self.rows // 2
        return self.buf.at[pl.ds(start + part * half, half)]

    def owner(self, ia, ib, from_partner=False):
        if from_partner:
            return moved(OFFS[ib], OFFS[ia], 1)
        return moved(OFFS[ia], OFFS[ib])

    def forward(self, role, block, to):
        self.mail.send(self.base + role, block, block, to)

    def to_partner(self, ia, ib):
        self.forward(20 + ia * 4 + ib, self.blk(self.owner(ia, ib)), self.partner)

    def from_partner(self, *places):
        for ia, ib in places:
            if (ia, ib) not in self.seen:
                self.seen.add((ia, ib))
                self.mail.await_recv(
                    self.base + 20 + ia * 4 + ib, self.blk(self.owner(ia, ib, True)), self.partner
                )

    def line_out(self, i):
        block = self.blk(self.owner(0, i))
        self.forward(4 + 4 * i, block, self.a_plus)
        self.forward(5 + 4 * i, block, self.a_minus)

    def line_relay(self, i):
        low, high = self.owner(1, i), self.owner(2, i)
        self.mail.await_recv(self.base + 4 + 4 * i, self.blk(low), self.a_minus)
        self.forward(6 + 4 * i, self.blk(low, 0), self.a_plus)
        self.mail.await_recv(self.base + 5 + 4 * i, self.blk(high), self.a_plus)
        self.forward(7 + 4 * i, self.blk(high, 1), self.a_minus)
        self.to_partner(1, i)
        self.to_partner(2, i)

    def line_far(self, i):
        far = self.owner(3, i)
        self.mail.await_recv(self.base + 6 + 4 * i, self.blk(far, 0), self.a_minus)
        self.mail.await_recv(self.base + 7 + 4 * i, self.blk(far, 1), self.a_plus)
        self.to_partner(3, i)

    def stages(self):
        mail, base, blk = self.mail, self.base, self.blk
        own, low, high, far = (self.owner(0, i) for i in range(4))
        self.forward(0, blk(own), self.b_plus)
        self.forward(1, blk(own), self.b_minus)
        self.line_out(0)
        self.to_partner(0, 0)
        mail.await_recv(base + 0, blk(low), self.b_minus)
        self.forward(2, blk(low, 0), self.b_plus)
        self.line_out(1)
        self.to_partner(0, 1)
        mail.await_recv(base + 1, blk(high), self.b_plus)
        self.forward(3, blk(high, 1), self.b_minus)
        self.line_out(2)
        self.to_partner(0, 2)
        self.line_relay(0)
        yield "relay0"
        mail.await_recv(base + 2, blk(far, 0), self.b_minus)
        mail.await_recv(base + 3, blk(far, 1), self.b_plus)
        self.line_out(3)
        self.to_partner(0, 3)
        self.line_relay(1)
        yield "relay1"
        self.line_relay(2)
        yield "relay2"
        self.line_far(0)
        yield "far0"
        self.line_relay(3)
        yield "relay3"
        self.line_far(1)
        yield "far1"
        self.line_far(2)
        yield "far2"
        self.line_far(3)
        yield "far3"

    def finish(self):
        self.from_partner(*[(ia, ib) for ia in range(4) for ib in range(4)])


PIECES = 2
SCATTER_ROLES = 13 * PIECES + 1


def reduce_rows(mail, base, product, width, xs, xr, sums, acc, near, mid, last, swap_out, swap_in):
    x, z, c = place()
    a = (1 - c) * z + c * x
    b = (1 - c) * x + c * z
    partner = moved(0, 0, 1)
    a_plus, a_minus = moved(1, 0), moved(-1, 0)
    b_plus, b_minus, b_far = moved(0, 1), moved(0, -1), moved(0, 2)
    steps = (2, 1, 3, 0)
    f32, bf16 = jnp.float32, jnp.bfloat16
    lo, hi = pl.ds(0, 128), pl.ds(128, 128)

    def set_chips(k, cc):
        return [(1 - cc) * (j * 4 + k) + cc * (k * 4 + j) for j in range(4)]

    def role(p, n):
        return base + 13 * p + n

    def partner_part(p, idx):
        product(set_chips((b + steps[idx]) % 4, 1 - c), 1 - c, p, xs.at[p, idx], None)
        mail.send(role(p, idx), xs.at[p, idx], xr.at[p, idx], partner)

    def own_part(p, idx, out):
        mail.await_recv(role(p, idx), xr.at[p, idx], partner)
        product(set_chips((a + steps[idx]) % 4, c), c, p, out, xr.at[p, idx])

    def far_sets(p):
        partner_part(p, 0)
        partner_part(p, 1)
        own_part(p, 0, sums.at[p, 0])
        mail.send(role(p, 4), sums.at[p, 0, lo], near.at[p, lo], a_plus)
        mail.send(role(p, 5), sums.at[p, 0, hi], near.at[p, hi], a_minus)

    def next_sets(p):
        partner_part(p, 2)
        own_part(p, 1, sums.at[p, 1])
        mail.send(role(p, 6), sums.at[p, 1, hi], mid.at[p, 0, hi], a_plus)
        partner_part(p, 3)
        own_part(p, 2, sums.at[p, 2])
        mail.send(role(p, 7), sums.at[p, 2, lo], mid.at[p, 1, lo], a_minus)

    def pass_on(p):
        mail.await_recv(role(p, 4), near.at[p, lo], a_minus)
        sums[p, 1, lo] = (sums[p, 1, lo].astype(f32) + near[p, lo].astype(f32)).astype(bf16)
        mail.send(role(p, 8), sums.at[p, 1, lo], mid.at[p, 0, lo], a_plus)
        mail.await_recv(role(p, 5), near.at[p, hi], a_plus)
        sums[p, 2, hi] = (sums[p, 2, hi].astype(f32) + near[p, hi].astype(f32)).astype(bf16)
        mail.send(role(p, 9), sums.at[p, 2, hi], mid.at[p, 1, hi], a_minus)

    def own_set(p):
        own_part(p, 3, acc.at[p])

    def chunk(j):
        return pl.ds(pl.multiple_of(j * 64, 64), 64)

    def chunk_sum(p, j):
        at = chunk(j)
        return acc[p, at] + mid[p, 0, at].astype(f32) + mid[p, 1, at].astype(f32)

    def second(p):
        mail.await_recv(role(p, 6), mid.at[p, 0, hi], a_minus)
        mail.await_recv(role(p, 7), mid.at[p, 1, lo], a_plus)
        mail.await_recv(role(p, 8), mid.at[p, 0, lo], a_minus)
        mail.await_recv(role(p, 9), mid.at[p, 1, hi], a_plus)
        for n, (step, to) in enumerate(((2, b_far), (1, b_plus), (3, b_minus))):
            at = chunk((b + step) % 4)
            sums[p, 0, at] = chunk_sum(p, (b + step) % 4).astype(bf16)
            mail.send(role(p, 10 + n), sums.at[p, 0, at], last.at[p, n], to)

    def finish(p):
        value = chunk_sum(p, b)
        for n, source in ((1, b_minus), (2, b_plus), (0, b_far)):
            mail.await_recv(role(p, 10 + n), last.at[p, n], source)
        for n in range(3):
            value = value + last[p, n].astype(f32)
        return value

    far_sets(0)
    next_sets(0)
    far_sets(1)
    pass_on(0)
    next_sets(1)
    own_set(0)
    pass_on(1)
    mail.release(role(0, 4), role(0, 5))
    second(0)
    own_set(1)
    mail.release(role(1, 4), role(1, 5))
    second(1)
    value = jnp.concatenate([finish(0), finish(1)], axis=1)
    is_first = c == 0
    swap_out[...] = jnp.where(is_first, value[32:], value[:32])
    mail.send(base + 13 * PIECES, swap_out, swap_in, partner)
    mine = jnp.where(is_first, value[:32], value[32:])
    mail.await_recv(base + 13 * PIECES, swap_in, partner)
    return mine


TAIL_ROLES = SCATTER_ROLES * 2 + GATHER_ROLES


def tail_kernel(
    heads_ref, w_out_hbm, gain_ref, w_gu_hbm, w_down_hbm, attn_ref, block_ref,
    w_out, w_gu, w_down, load_sems, send_sems, recv_sems,
    xs, xr, sums, acc, near, mid, last, swap_out, swap_in,
    xs2, xr2, sums2, near2, mid2, last2, swap_out2, swap_in2,
    ff_buf, hidden,
):
    x, z, c = place()
    loads = [
        pltpu.make_async_copy(w_out_hbm, w_out, load_sems.at[0]),
        pltpu.make_async_copy(w_gu_hbm, w_gu, load_sems.at[1]),
        pltpu.make_async_copy(w_down_hbm, w_down, load_sems.at[2]),
    ]
    for load in loads:
        load.start()
    greet([
        {"hid": moved(1, 0)}, {"hid": moved(-1, 0)}, {"hid": moved(0, 1)},
        {"hid": moved(0, -1)}, {"hid": moved(0, 2)}, {"hid": moved(0, 0, 1)},
    ])
    mail = Mail(send_sems, recv_sems)
    width = w_out.shape[1] // 2
    step = width // PIECES

    def product_of(lhs, weight):
        def product(chips, half, piece, out, other):
            rows = jnp.concatenate(
                [lhs[pl.ds(pl.multiple_of(chip * 64, 64), 64), :] for chip in chips], axis=0
            )
            cols = pl.ds(pl.multiple_of(half * width + piece * step, 128), step)
            value = jnp.dot(rows, weight[:, cols], preferred_element_type=jnp.float32)
            if other is not None:
                value = value + other[...].astype(jnp.float32)
            out[...] = value.astype(out.dtype)
        return product

    mine_at = pl.ds(pl.multiple_of(c * width, 128), width)
    other_at = pl.ds(pl.multiple_of((1 - c) * width, 128), width)

    loads[0].wait()
    mine = reduce_rows(
        mail, 0, product_of(heads_ref, w_out), width,
        xs, xr, sums, acc, near, mid, last, swap_out, swap_in,
    )
    other = swap_in[...]
    attn_ref[:, mine_at] = mine.astype(jnp.bfloat16)
    attn_ref[:, other_at] = other.astype(jnp.bfloat16)
    total = jnp.sum(mine * mine, axis=1, keepdims=True) + jnp.sum(other * other, axis=1, keepdims=True)
    scale = lax.rsqrt(total / (2 * width) + EPS)
    own_rows = pl.ds(pl.multiple_of(moved(0, 0) * 32, 32), 32)
    gain_mine = gain_ref[mine_at].reshape(1, width)
    gain_other = gain_ref[other_at].reshape(1, width)
    ff_buf[own_rows, mine_at] = (mine * scale * gain_mine).astype(jnp.bfloat16)
    ff_buf[own_rows, other_at] = (other * scale * gain_other).astype(jnp.bfloat16)

    units = w_down.shape[0]
    contract = (((1,), (1,)), ((), ()))
    gather = Gather(mail, SCATTER_ROLES, ff_buf, 32)

    def feed(own, partners):
        gather.from_partner(*partners)
        places = [gather.owner(*at) for at in own] + [gather.owner(*at, True) for at in partners]
        slices = [pl.ds(pl.multiple_of(hid * 32, 32), 32) for hid in places]
        rows = jnp.concatenate([ff_buf[at, :] for at in slices], axis=0)
        gate = lax.dot_general(rows, w_gu[pl.ds(0, units), :], contract, preferred_element_type=jnp.float32)
        up = lax.dot_general(rows, w_gu[pl.ds(units, units), :], contract, preferred_element_type=jnp.float32)
        value = (jax.nn.silu(gate) * up).astype(jnp.bfloat16)
        for n, at in enumerate(slices):
            hidden[at, :] = value[n * 32:(n + 1) * 32]

    for stage in gather.stages():
        if stage == "relay2":
            loads[1].wait()
            feed([(0, 0), (0, 1), (0, 2), (1, 0), (2, 0)], [(0, 0), (0, 1), (0, 2)])
        if stage == "relay3":
            feed([(1, 1), (2, 1), (1, 2), (2, 2), (0, 3), (3, 0)], [(1, 0), (2, 0)])
        if stage == "far3":
            feed([(1, 3), (2, 3)], [(0, 3), (1, 1), (2, 1), (1, 2), (2, 2), (3, 0)])
    feed([(3, 1), (3, 2), (3, 3)], [(1, 3), (2, 3), (3, 1), (3, 2), (3, 3)])

    loads[2].wait()
    mine = reduce_rows(
        mail, SCATTER_ROLES + GATHER_ROLES, product_of(hidden, w_down), width,
        xs2, xr2, sums2, acc, near2, mid2, last2, swap_out2, swap_in2,
    )
    block_ref[:, mine_at] = mine.astype(jnp.bfloat16)
    block_ref[:, other_at] = swap_in2[...].astype(jnp.bfloat16)
    mail.drain()


def tail(heads_out, w_out, gain_ff, w_gu, w_down):
    tok_grp = heads_out.shape[0]
    width = w_out.shape[1]
    half = width // 2
    units = w_down.shape[0]
    bf16, f32 = jnp.bfloat16, jnp.float32
    vmem = pl.BlockSpec(memory_space=pltpu.VMEM)
    anywhere = pl.BlockSpec(memory_space=pl.ANY)

    piece = half // PIECES

    def travel():
        return [
            pltpu.VMEM((PIECES, 4, 256, piece), bf16), pltpu.VMEM((PIECES, 4, 256, piece), bf16),
            pltpu.VMEM((PIECES, 3, 256, piece), bf16),
        ]

    def landing():
        return [
            pltpu.VMEM((PIECES, 256, piece), bf16), pltpu.VMEM((PIECES, 2, 256, piece), bf16),
            pltpu.VMEM((PIECES, 3, 64, piece), bf16), pltpu.VMEM((32, half), f32), pltpu.VMEM((32, half), f32),
        ]

    return pl.pallas_call(
        tail_kernel,
        out_shape=(jax.ShapeDtypeStruct((32, width), bf16), jax.ShapeDtypeStruct((32, width), bf16)),
        in_specs=[vmem, anywhere, vmem, anywhere, anywhere],
        out_specs=(vmem, vmem),
        scratch_shapes=[
            pltpu.VMEM(w_out.shape, bf16), pltpu.VMEM(w_gu.shape, bf16), pltpu.VMEM(w_down.shape, bf16),
            pltpu.SemaphoreType.DMA((3,)), pltpu.SemaphoreType.DMA((TAIL_ROLES,)),
            pltpu.SemaphoreType.DMA((TAIL_ROLES,)),
            *travel(), pltpu.VMEM((PIECES, 256, piece), f32), *landing(),
            *travel(), *landing(),
            pltpu.VMEM((tok_grp, width), bf16), pltpu.VMEM((tok_grp, units), bf16),
        ],
        compiler_params=pltpu.CompilerParams(
            collective_id=0, has_side_effects=True, vmem_limit_bytes=66000000
        ),
        name="tail",
    )(heads_out, w_out, gain_ff, w_gu, w_down)


FRONT_BLOCKS = 36
WINDOW = 768


def front_kernel(
    slot_ref, choice_ref, lengths_ref, tokens_ref, gain_ref, down_hbm, up_ref, w_hbm, cache_hbm, heads_ref,
    w_qkv, w_latent, rows_buf, load_sems, send_sems, recv_sems,
    first_0, first_1, second_0, second_1, pass_0, pass_1, split_0, split_1,
    prefix, qkv, top, denom, total,
):
    x, z, c = place()
    hid = lax.axis_index("hid")
    req = lax.axis_index("req")
    lower, upper = (req + 3) % 4, (req + 1) % 4
    width = tokens_ref.shape[1]
    bf16, f32 = jnp.bfloat16, jnp.float32
    first, second = (first_0, first_1), (second_0, second_1)
    passed, split = (pass_0, pass_1), (split_0, split_1)

    def owner(group):
        return slot_ref[choice_ref[group]]

    peers = [{"hid": (hid + d) % 32} for d in range(1, 32)] + [{"req": lower}, {"req": upper}]
    barrier = pltpu.get_barrier_semaphore()
    for peer in peers:
        pl.semaphore_signal(barrier, inc=1, device_id=peer, device_id_type=MESH)
    latent_load = pltpu.make_async_copy(down_hbm, w_latent, load_sems.at[5])
    latent_load.start()
    loads = []
    for k in range(2):
        for half in range(2):
            copy = pltpu.make_async_copy(
                cache_hbm.at[pl.ds(half * 32 + k * 16, 16)], first[k].at[half], load_sems.at[1 + 2 * k + half]
            )
            copy.start()
            loads.append(copy)
    w_load = pltpu.make_async_copy(w_hbm, w_qkv, load_sems.at[0])
    w_load.start()

    matrix = tokens_ref[...].astype(f32)
    normed = rms_scale(matrix, gain_ref[...].reshape(1, width)).astype(bf16)
    own_rows = pl.ds(pl.multiple_of(hid * 32, 32), 32)
    rows_buf[own_rows, pl.ds(0, width)] = normed
    pl.semaphore_wait(barrier, len(peers))

    mail = Mail(send_sems, recv_sems)
    y_base = GATHER_ROLES
    deal_base = y_base + 8

    def y_copy(role, src, dst, to):
        return pltpu.make_async_remote_copy(
            src_ref=src, dst_ref=dst, send_sem=send_sems.at[role], recv_sem=recv_sems.at[role],
            device_id={"req": to}, device_id_type=MESH,
        )

    def y_send(role, src, dst, to):
        copy = y_copy(role, src, dst, to)
        copy.start()
        mail.sent[role] = copy

    def y_start():
        for k in range(2):
            y_send(y_base + k, cache_hbm.at[pl.ds(k * 16, 16)], first[k].at[2], lower)
            y_send(y_base + 2 + k, cache_hbm.at[pl.ds(32 + k * 16, 16)], first[k].at[3], upper)

    def y_pass(k):
        loads[2 * k].wait()
        loads[2 * k + 1].wait()
        y_copy(y_base + k, first[k].at[2], first[k].at[2], upper).wait_recv()
        y_copy(y_base + 2 + k, first[k].at[3], first[k].at[3], lower).wait_recv()
        passed[k][0] = first[k][jnp.where(owner(lower) == req, 1, 2)]
        y_send(y_base + 4 + k, passed[k].at[0], second[k].at[0], lower)
        passed[k][1] = first[k][jnp.where(owner(upper) == req, 0, 3)]
        y_send(y_base + 6 + k, passed[k].at[1], second[k].at[1], upper)

    def deal(k):
        y_copy(y_base + 4 + k, second[k].at[0], second[k].at[0], upper).wait_recv()
        y_copy(y_base + 6 + k, second[k].at[1], second[k].at[1], lower).wait_recv()
        away = (owner(req) - req + 4) % 4
        late_a = jnp.full((1, 1, 1), (away >= 2).astype(jnp.int32)) > 0
        late_b = jnp.full((1, 1, 1), jnp.logical_or(away == 1, away == 2).astype(jnp.int32)) > 0
        half_a = jnp.where(late_a, second[k][jnp.where(away == 2, 0, 1)], first[k][jnp.where(away == 0, 0, 2)])
        half_b = jnp.where(late_b, second[k][jnp.where(away == 1, 0, 1)], first[k][jnp.where(away == 0, 1, 3)])
        r = lax.broadcasted_iota(jnp.int32, (32, 32), 0)
        s = lax.broadcasted_iota(jnp.int32, (32, 32), 1)
        sort = (s == jnp.where(r < 16, 2 * r, 2 * r - 31)).astype(bf16)
        zeros = jnp.zeros((16, 256 - HD), bf16)
        for half, value in enumerate((half_a, half_b)):
            planes = jnp.dot(sort, value.reshape(32, width), preferred_element_type=f32).astype(bf16)
            for kv in range(2):
                for h in range(32):
                    piece = planes[kv * 16:(kv + 1) * 16, h * HD:(h + 1) * HD]
                    split[k][h, kv, pl.ds(half * 16, 16), :] = jnp.concatenate([piece, zeros], axis=1)

        landing = prefix.at[k, :, own_rows]
        for d in range(1, 32):
            to = (hid + d) % 32
            mail.send(deal_base + k * 31 + d - 1, split[k].at[to], landing, to)
        prefix[k, :, own_rows] = split[k][hid]

    def dealt(k):
        for d in range(1, 32):
            source = (hid + 32 - d) % 32
            landing = prefix.at[k, :, pl.ds(pl.multiple_of(source * 32, 32), 32)]
            mail.await_recv(deal_base + k * 31 + d - 1, landing, source)

    y_start()
    latent_load.wait()
    latent = jnp.dot(normed, w_latent[...], preferred_element_type=f32)
    rows_buf[own_rows, pl.ds(width, 128)] = latent.astype(bf16)
    gather = Gather(mail, 0, rows_buf, 32)
    for stage in gather.stages():
        if stage == "relay0":
            y_pass(0)
        if stage == "relay2":
            y_pass(1)
        if stage == "relay3":
            deal(0)
    deal(1)
    gather.finish()

    w_load.wait()
    contract = (((1,), (1,)), ((), ()))
    pad = jnp.zeros((256, 256 - HD), bf16)

    @pl.loop(0, 4)
    def _(i):
        at = pl.ds(pl.multiple_of(i * 256, 256), 256)
        rows = rows_buf[at, pl.ds(0, width)]
        for part in range(3):
            value = lax.dot_general(
                rows, w_qkv[pl.ds(part * HD, HD), :], contract, preferred_element_type=f32
            )
            if part == 0:
                value = value + lax.dot_general(
                    rows_buf[at, pl.ds(width, 128)], up_ref[...], contract, preferred_element_type=f32
                )
            qkv[part, at, :] = jnp.concatenate([value.astype(bf16), pad], axis=1)

    dealt(0)

    ends = [lengths_ref[0, 0]]
    for n in range(1, lengths_ref.shape[1]):
        ends.append(ends[-1] + lengths_ref[0, n])
    factor = HD ** (-0.5)

    @pl.loop(0, 8)
    def _(i):
        at = pl.ds(pl.multiple_of(i * 128, 128), 128)
        begin = jnp.minimum(jnp.maximum(i * 128 - 512, 0), 1024 - WINDOW)
        near = pl.ds(pl.multiple_of(begin, 128), WINDOW)
        q = qkv[0, at, :]
        s_far = lax.dot_general(q, prefix[0, 0], contract, preferred_element_type=f32) * factor
        s_near = lax.dot_general(q, qkv[1, near, :], contract, preferred_element_type=f32) * factor
        row = lax.broadcasted_iota(jnp.int32, (128, 1), 0) + i * 128
        since = jnp.zeros((128, 1), jnp.int32)
        for end in ends:
            since = jnp.where(row >= end, jnp.maximum(since, end), since)
        col = lax.broadcasted_iota(jnp.int32, (128, WINDOW), 1) + begin
        s_near = jnp.where(jnp.logical_and(col >= since, col <= row), s_near, -jnp.inf)
        row_max = jnp.maximum(
            jnp.max(s_far, axis=1, keepdims=True), jnp.max(s_near, axis=1, keepdims=True)
        )
        e_far = jnp.exp(s_far - row_max)
        e_near = jnp.exp(s_near - row_max)
        top[at, :] = row_max
        denom[at, :] = jnp.sum(e_far, axis=1, keepdims=True) + jnp.sum(e_near, axis=1, keepdims=True)
        out = jnp.dot(e_far.astype(bf16), prefix[0, 1], preferred_element_type=f32)
        total[at, :] = out + jnp.dot(e_near.astype(bf16), qkv[2, near, :], preferred_element_type=f32)

    dealt(1)

    @pl.loop(0, 8)
    def _(i):
        at = pl.ds(pl.multiple_of(i * 128, 128), 128)
        scores = lax.dot_general(qkv[0, at, :], prefix[1, 0], contract, preferred_element_type=f32) * factor
        row_max = jnp.maximum(top[at, :], jnp.max(scores, axis=1, keepdims=True))
        keep = jnp.exp(top[at, :] - row_max)
        expos = jnp.exp(scores - row_max)
        row_sum = denom[at, :] * keep + jnp.sum(expos, axis=1, keepdims=True)
        out = total[at, :] * keep + jnp.dot(expos.astype(bf16), prefix[1, 1], preferred_element_type=f32)
        heads_ref[at, :] = (out / row_sum)[:, :HD].astype(bf16)

    mail.drain()


def front(slots, choices, lengths, tokens, gain_in, adapt_down, up_t, w_t, cache):
    rows, width = tokens.shape
    tok_grp = rows * 32
    bf16 = jnp.bfloat16
    smem = pl.BlockSpec(memory_space=pltpu.SMEM)
    vmem = pl.BlockSpec(memory_space=pltpu.VMEM)
    anywhere = pl.BlockSpec(memory_space=pl.ANY)
    roles = GATHER_ROLES + 8 + 62

    def halves(count):
        return pltpu.VMEM((count, 16, 2, width), bf16)

    return pl.pallas_call(
        front_kernel,
        out_shape=jax.ShapeDtypeStruct((tok_grp, HD), bf16),
        in_specs=[smem, smem, smem, vmem, vmem, anywhere, vmem, anywhere, anywhere],
        out_specs=vmem,
        scratch_shapes=[
            pltpu.VMEM(w_t.shape, bf16), pltpu.VMEM(adapt_down.shape, bf16),
            pltpu.VMEM((tok_grp, width + 128), bf16),
            pltpu.SemaphoreType.DMA((6,)), pltpu.SemaphoreType.DMA((roles,)),
            pltpu.SemaphoreType.DMA((roles,)),
            halves(4), halves(4), halves(2), halves(2), halves(2), halves(2),
            pltpu.VMEM((32, 2, 32, 256), bf16), pltpu.VMEM((32, 2, 32, 256), bf16),
            pltpu.VMEM((2, 2, tok_grp, 256), bf16), pltpu.VMEM((3, tok_grp, 256), bf16),
            pltpu.VMEM((tok_grp, 1), jnp.float32), pltpu.VMEM((tok_grp, 1), jnp.float32),
            pltpu.VMEM((tok_grp, 256), jnp.float32),
        ],
        compiler_params=pltpu.CompilerParams(
            collective_id=1, has_side_effects=True, vmem_limit_bytes=66000000
        ),
        name="front",
    )(slots, choices, lengths, tokens, gain_in, adapt_down, up_t, w_t, cache)


def settle_kernel(attn_ref, block_ref, attn_out, block_out):
    attn_out[...] = attn_ref[...]
    block_out[...] = block_ref[...]


def settle(attn, block):
    vmem = pl.BlockSpec(memory_space=pltpu.VMEM)
    return pl.pallas_call(
        settle_kernel,
        out_shape=(jax.ShapeDtypeStruct(attn.shape, attn.dtype), jax.ShapeDtypeStruct(block.shape, block.dtype)),
        in_specs=[vmem, vmem],
        out_specs=(vmem, vmem),
        name="settle",
    )(attn, block)


def per_device(
    tokens,
    gain_in,
    w_qkv,
    adapt_down,
    adapt_up,
    w_out,
    gain_ff,
    w_gate_up,
    w_down,
    prefix_cache,
    prefix_owner,
    group_prefix,
    lengths,
):
    w_t = jnp.transpose(w_qkv, (1, 2, 0)).reshape(3 * w_qkv.shape[2], w_qkv.shape[0])
    w_gu = jnp.transpose(w_gate_up, (1, 2, 0)).reshape(2 * w_gate_up.shape[2], w_gate_up.shape[0])
    heads_out = front(
        prefix_owner, group_prefix, lengths, tokens, gain_in, adapt_down, adapt_up.T, w_t, prefix_cache[0]
    )
    return settle(*tail(heads_out, w_out, gain_ff, w_gu, w_down))


def solution(mesh):
    placed = (
        P(("req", "hid"), None),
        P(),
        P(None, None, "hid"),
        P(),
        P(None, "hid"),
        P("hid", None),
        P(),
        P(None, None, "hid"),
        P("hid", None),
        P("req", "hid", None, None),
        P(),
        P(),
        P("req", None),
    )
    return jax.shard_map(
        per_device,
        mesh=mesh,
        in_specs=placed,
        out_specs=(P(("req", "hid"), None), P(("req", "hid"), None)),
        check_vma=False,
    )
```

```python
import jax
import jax.numpy as jnp
from jax import lax
from jax.experimental import pallas as pl
from jax.experimental.pallas import tpu as pltpu
from jax.sharding import PartitionSpec as P

HD = 224


EPS = 1e-05


def rms_scale(matrix, gain_vec):
    return matrix * lax.rsqrt(jnp.mean(matrix * matrix, axis=-1, keepdims=True) + EPS) * gain_vec


MESH = pl.DeviceIdType.MESH
NX, NZ = 4, 4


def place():
    hid = lax.axis_index("hid")
    return hid // 8, (hid // 2) % 4, hid % 2


def moved(da, db, core_flip=0):
    x, z, c = place()
    xn = (x + 4 + (1 - c) * db + c * da) % 4
    zn = (z + 4 + (1 - c) * da + c * db) % 4
    cn = c + core_flip * (1 - 2 * c)
    return xn * 8 + zn * 2 + cn


def remote(src, dst, send, recv, hid):
    return pltpu.make_async_remote_copy(
        src_ref=src, dst_ref=dst, send_sem=send, recv_sem=recv,
        device_id={"hid": hid}, device_id_type=MESH,
    )


class Mail:
    def __init__(self, send_sems, recv_sems):
        self.send_sems, self.recv_sems, self.sent = send_sems, recv_sems, {}

    def send(self, role, src, dst, hid):
        copy = remote(src, dst, self.send_sems.at[role], self.recv_sems.at[role], hid)
        copy.start()
        self.sent[role] = copy

    def await_recv(self, role, dst, hid):
        remote(dst, dst, self.send_sems.at[role], self.recv_sems.at[role], hid).wait_recv()

    def drain(self):
        for copy in self.sent.values():
            copy.wait_send()


GATHER_ROLES = 36
OFFS = (0, -1, 1, 2)


class Gather:
    def __init__(self, mail, base, buf, rows, first_row=0, split_columns=False):
        self.mail, self.base, self.buf, self.rows = mail, base, buf, rows
        self.first_row, self.split_columns = first_row, split_columns
        self.a_plus, self.a_minus = moved(1, 0), moved(-1, 0)
        self.b_plus, self.b_minus = moved(0, 1), moved(0, -1)
        self.partner = moved(0, 0, 1)
        self.seen = set()

    def row_slice(self, hid):
        return pl.ds(pl.multiple_of(self.first_row + hid * self.rows, self.rows), self.rows)

    def blk(self, hid, part=None):
        start = pl.multiple_of(self.first_row + hid * self.rows, self.rows)
        if part is None:
            return self.buf.at[self.row_slice(hid)]
        if self.split_columns:
            half = self.buf.shape[1] // 2
            return self.buf.at[self.row_slice(hid), pl.ds(part * half, half)]
        half = self.rows // 2
        return self.buf.at[pl.ds(start + part * half, half)]

    def owner(self, ia, ib, from_partner=False):
        if from_partner:
            return moved(OFFS[ib], OFFS[ia], 1)
        return moved(OFFS[ia], OFFS[ib])

    def forward(self, role, block, to):
        self.mail.send(self.base + role, block, block, to)

    def to_partner(self, ia, ib):
        self.forward(20 + ia * 4 + ib, self.blk(self.owner(ia, ib)), self.partner)

    def from_partner(self, *places):
        for ia, ib in places:
            if (ia, ib) not in self.seen:
                self.seen.add((ia, ib))
                self.mail.await_recv(
                    self.base + 20 + ia * 4 + ib, self.blk(self.owner(ia, ib, True)), self.partner
                )

    def line_out(self, i):
        block = self.blk(self.owner(0, i))
        self.forward(4 + 4 * i, block, self.a_plus)
        self.forward(5 + 4 * i, block, self.a_minus)

    def line_relay(self, i):
        low, high = self.owner(1, i), self.owner(2, i)
        self.mail.await_recv(self.base + 4 + 4 * i, self.blk(low), self.a_minus)
        self.forward(6 + 4 * i, self.blk(low, 0), self.a_plus)
        self.mail.await_recv(self.base + 5 + 4 * i, self.blk(high), self.a_plus)
        self.forward(7 + 4 * i, self.blk(high, 1), self.a_minus)
        self.to_partner(1, i)
        self.to_partner(2, i)

    def line_far(self, i):
        far = self.owner(3, i)
        self.mail.await_recv(self.base + 6 + 4 * i, self.blk(far, 0), self.a_minus)
        self.mail.await_recv(self.base + 7 + 4 * i, self.blk(far, 1), self.a_plus)
        self.to_partner(3, i)

    def stages(self):
        mail, base, blk = self.mail, self.base, self.blk
        own, low, high, far = (self.owner(0, i) for i in range(4))
        self.forward(0, blk(own), self.b_plus)
        self.forward(1, blk(own), self.b_minus)
        self.line_out(0)
        self.to_partner(0, 0)
        yield "start"
        mail.await_recv(base + 0, blk(low), self.b_minus)
        self.forward(2, blk(low, 0), self.b_plus)
        self.line_out(1)
        self.to_partner(0, 1)
        mail.await_recv(base + 1, blk(high), self.b_plus)
        self.forward(3, blk(high, 1), self.b_minus)
        self.line_out(2)
        self.to_partner(0, 2)
        self.line_relay(0)
        yield "relay0"
        mail.await_recv(base + 2, blk(far, 0), self.b_minus)
        mail.await_recv(base + 3, blk(far, 1), self.b_plus)
        self.line_out(3)
        self.to_partner(0, 3)
        self.line_relay(1)
        yield "relay1"
        self.line_relay(2)
        yield "relay2"
        self.line_far(0)
        yield "far0"
        self.line_relay(3)
        yield "relay3"
        self.line_far(1)
        yield "far1"
        self.line_far(2)
        yield "far2"
        self.line_far(3)
        yield "far3"

    def finish(self):
        self.from_partner(*[(ia, ib) for ia in range(4) for ib in range(4)])


PIECES = 2
PART = 16
PIECE_ROLES = 14


class Scatter:
    def __init__(self, mail, base, product, xs, xr, sums, acc, near, mid, last, swap_out, swap_in):
        self.mail, self.base, self.product = mail, base, product
        self.xs, self.xr, self.sums, self.acc = xs, xr, sums, acc
        self.near, self.mid, self.last = near, mid, last
        self.swap_out, self.swap_in = swap_out, swap_in
        x, z, c = place()
        self.c = c
        self.a = (1 - c) * z + c * x
        self.b = (1 - c) * x + c * z
        self.partner = moved(0, 0, 1)
        self.a_plus, self.a_minus = moved(1, 0), moved(-1, 0)
        self.b_plus, self.b_minus, self.b_far = moved(0, 1), moved(0, -1), moved(0, 2)
        self.lo, self.hi = pl.ds(0, 4 * PART), pl.ds(4 * PART, 4 * PART)

    def role(self, p, n):
        return self.base + PIECE_ROLES * p + n

    def set_chips(self, k, cc):
        return [(1 - cc) * (j * 4 + k) + cc * (k * 4 + j) for j in range(4)]

    def partner_part(self, p, idx):
        c, step = self.c, (2, 1, 3, 0)[idx]
        chips = self.set_chips((self.b + step) % 4, 1 - c)
        self.product(chips, 1 - c, p, self.xs.at[p, idx], None)
        self.mail.send(self.role(p, idx), self.xs.at[p, idx], self.xr.at[p, idx], self.partner)

    def own_part(self, p, idx, out):
        c, step = self.c, (2, 1, 3, 0)[idx]
        self.mail.await_recv(self.role(p, idx), self.xr.at[p, idx], self.partner)
        self.product(self.set_chips((self.a + step) % 4, c), c, p, out, self.xr.at[p, idx])

    def far_sets(self, p):
        sums, near = self.sums, self.near
        self.partner_part(p, 0)
        self.partner_part(p, 1)
        self.own_part(p, 0, sums.at[p, 0])
        self.mail.send(self.role(p, 4), sums.at[p, 0, self.lo], near.at[p, self.lo], self.a_plus)
        self.mail.send(self.role(p, 5), sums.at[p, 0, self.hi], near.at[p, self.hi], self.a_minus)

    def next_sets(self, p):
        sums, mid = self.sums, self.mid
        self.partner_part(p, 2)
        self.own_part(p, 1, sums.at[p, 1])
        self.mail.send(self.role(p, 6), sums.at[p, 1, self.hi], mid.at[p, 0, self.hi], self.a_plus)
        self.partner_part(p, 3)
        self.own_part(p, 2, sums.at[p, 2])
        self.mail.send(self.role(p, 7), sums.at[p, 2, self.lo], mid.at[p, 1, self.lo], self.a_minus)

    def pass_on(self, p):
        f32, bf16 = jnp.float32, jnp.bfloat16
        sums, near, mid, lo, hi = self.sums, self.near, self.mid, self.lo, self.hi
        self.mail.await_recv(self.role(p, 4), near.at[p, lo], self.a_minus)
        sums[p, 1, lo] = (sums[p, 1, lo].astype(f32) + near[p, lo].astype(f32)).astype(bf16)
        self.mail.send(self.role(p, 8), sums.at[p, 1, lo], mid.at[p, 0, lo], self.a_plus)
        self.mail.await_recv(self.role(p, 5), near.at[p, hi], self.a_plus)
        sums[p, 2, hi] = (sums[p, 2, hi].astype(f32) + near[p, hi].astype(f32)).astype(bf16)
        self.mail.send(self.role(p, 9), sums.at[p, 2, hi], mid.at[p, 1, hi], self.a_minus)

    def own_set(self, p):
        self.own_part(p, 3, self.acc.at[p])

    def chunk(self, j):
        return pl.ds(pl.multiple_of(j * 2 * PART, 2 * PART), 2 * PART)

    def chunk_sum(self, p, j):
        at = self.chunk(j)
        value = self.acc[p, at] + self.mid[p, 0, at].astype(jnp.float32)
        return value + self.mid[p, 1, at].astype(jnp.float32)

    def second(self, p):
        mid, q = self.mid, self.sums
        self.mail.await_recv(self.role(p, 6), mid.at[p, 0, self.hi], self.a_minus)
        self.mail.await_recv(self.role(p, 7), mid.at[p, 1, self.lo], self.a_plus)
        self.mail.await_recv(self.role(p, 8), mid.at[p, 0, self.lo], self.a_minus)
        self.mail.await_recv(self.role(p, 9), mid.at[p, 1, self.hi], self.a_plus)
        for n, (step, to) in enumerate(((2, self.b_far), (1, self.b_plus), (3, self.b_minus))):
            j = (self.b + step) % 4
            q[p, 3, self.chunk(j)] = self.chunk_sum(p, j).astype(jnp.bfloat16)
            self.mail.send(self.role(p, 10 + n), q.at[p, 3, self.chunk(j)], self.last.at[p, n], to)

    def settle(self, p):
        value = self.chunk_sum(p, self.b)
        for n, source in ((1, self.b_minus), (2, self.b_plus), (0, self.b_far)):
            self.mail.await_recv(self.role(p, 10 + n), self.last.at[p, n], source)
        for n in range(3):
            value = value + self.last[p, n].astype(jnp.float32)
        is_first = self.c == 0
        self.swap_out[p] = jnp.where(is_first, value[PART:], value[:PART])
        self.mail.send(self.role(p, 13), self.swap_out.at[p], self.swap_in.at[p], self.partner)
        return jnp.where(is_first, value[:PART], value[PART:])

    def other(self, p):
        self.mail.await_recv(self.role(p, 13), self.swap_in.at[p], self.partner)
        return self.swap_in[p]


TAIL_ROLES = PIECE_ROLES * PIECES * 2 + GATHER_ROLES * PIECES


def tail_kernel(
    heads_ref, w_out_hbm, gain_ref, w_gu_hbm, w_down_hbm, attn_ref, block_ref,
    w_out, w_gu, w_down, load_sems, send_sems, recv_sems, *scratch,
):
    *scatter_refs, ff_buf, hidden = scratch
    x, z, c = place()
    loads = [
        pltpu.make_async_copy(w_out_hbm, w_out, load_sems.at[0]),
        pltpu.make_async_copy(w_gu_hbm, w_gu, load_sems.at[1]),
        pltpu.make_async_copy(w_down_hbm, w_down, load_sems.at[2]),
    ]
    peers = [
        {"hid": moved(1, 0)}, {"hid": moved(-1, 0)}, {"hid": moved(0, 1)},
        {"hid": moved(0, -1)}, {"hid": moved(0, 2)}, {"hid": moved(0, 0, 1)},
    ]
    barrier = pltpu.get_barrier_semaphore()
    for peer in peers:
        pl.semaphore_signal(barrier, inc=1, device_id=peer, device_id_type=MESH)
    for load in loads:
        load.start()
    pl.semaphore_wait(barrier, len(peers))
    mail = Mail(send_sems, recv_sems)
    width = w_out.shape[1] // 2
    units = w_down.shape[0]
    count = heads_ref.shape[0] // PIECES

    def product_of(lhs_rows, weight):
        def product(chips, half, p, out, other):
            rows = jnp.concatenate([r for chip in chips for r in lhs_rows(p, chip)], axis=0)
            cols = pl.ds(pl.multiple_of(half * width, 128), width)
            value = jnp.dot(rows, weight[:, cols], preferred_element_type=jnp.float32)
            if other is not None:
                value = value + other[...].astype(jnp.float32)
            out[...] = value.astype(out.dtype)
        return product

    def heads_rows(p, chip):
        return [
            heads_ref[pl.ds(pl.multiple_of(chip * 64 + core * 32 + p * PART, PART), PART), :]
            for core in range(2)
        ]

    def hidden_rows(p, chip):
        return [hidden[pl.ds(pl.multiple_of(p * count + chip * 2 * PART, 2 * PART), 2 * PART), :]]

    outer = Scatter(mail, 0, product_of(heads_rows, w_out), *scatter_refs[:9])
    gathers = [
        Gather(
            mail, PIECE_ROLES * PIECES + GATHER_ROLES * p, ff_buf, PART,
            first_row=p * count, split_columns=True,
        )
        for p in range(PIECES)
    ]
    inner = Scatter(
        mail, PIECE_ROLES * PIECES + GATHER_ROLES * PIECES, product_of(hidden_rows, w_down), *scatter_refs[9:]
    )
    mine_at = pl.ds(pl.multiple_of(c * width, 128), width)
    other_at = pl.ds(pl.multiple_of((1 - c) * width, 128), width)
    gain_mine = gain_ref[mine_at].reshape(1, width)
    gain_other = gain_ref[other_at].reshape(1, width)

    def normalise(p, mine):
        other = outer.other(p)
        rows = pl.ds(p * PART, PART)
        attn_ref[rows, mine_at] = mine.astype(jnp.bfloat16)
        attn_ref[rows, other_at] = other.astype(jnp.bfloat16)
        total = jnp.sum(mine * mine, axis=1, keepdims=True) + jnp.sum(other * other, axis=1, keepdims=True)
        scale = lax.rsqrt(total / (2 * width) + EPS)
        own_rows = gathers[p].row_slice(moved(0, 0))
        ff_buf[own_rows, mine_at] = (mine * scale * gain_mine).astype(jnp.bfloat16)
        ff_buf[own_rows, other_at] = (other * scale * gain_other).astype(jnp.bfloat16)

    def feed(p, part):
        contract = (((1,), (1,)), ((), ()))
        at = pl.ds(p * count + part * (count // 2), count // 2)
        rows = ff_buf[at, :]
        gate = lax.dot_general(rows, w_gu[pl.ds(0, units), :], contract, preferred_element_type=jnp.float32)
        up = lax.dot_general(rows, w_gu[pl.ds(units, units), :], contract, preferred_element_type=jnp.float32)
        hidden[at, :] = (jax.nn.silu(gate) * up).astype(jnp.bfloat16)

    loads[0].wait()
    outer.far_sets(0)
    outer.next_sets(0)
    outer.far_sets(1)
    outer.pass_on(0)
    outer.next_sets(1)
    outer.own_set(0)
    outer.second(0)
    outer.pass_on(1)
    outer.own_set(1)
    first = outer.settle(0)
    outer.second(1)
    stages = [gather.stages() for gather in gathers]
    normalise(0, first)
    next(stages[0])
    second = outer.settle(1)
    normalise(1, second)
    next(stages[1])
    for name in ("relay0", "relay1", "relay2", "far0", "relay3"):
        for stage in stages:
            assert next(stage) == name
    for name in ("far1", "far2", "far3"):
        next(stages[0])
    loads[1].wait()
    gathers[0].finish()
    feed(0, 0)
    for name in ("far1", "far2", "far3"):
        next(stages[1])
    feed(0, 1)
    loads[2].wait()
    inner.far_sets(0)
    inner.next_sets(0)
    gathers[1].finish()
    feed(1, 0)
    inner.pass_on(0)
    feed(1, 1)
    inner.far_sets(1)
    inner.next_sets(1)
    inner.own_set(0)
    inner.second(0)
    inner.pass_on(1)
    inner.own_set(1)
    first = inner.settle(0)
    inner.second(1)
    for p, mine in enumerate((first, None)):
        if mine is None:
            mine = inner.settle(p)
        rows = pl.ds(p * PART, PART)
        block_ref[rows, mine_at] = mine.astype(jnp.bfloat16)
        block_ref[rows, other_at] = inner.other(p).astype(jnp.bfloat16)
    mail.drain()


def tail(heads_out, w_out, gain_ff, w_gu, w_down):
    tok_grp = heads_out.shape[0]
    width = w_out.shape[1]
    half = width // 2
    units = w_down.shape[0]
    bf16, f32 = jnp.bfloat16, jnp.float32
    vmem = pl.BlockSpec(memory_space=pltpu.VMEM)
    anywhere = pl.BlockSpec(memory_space=pl.ANY)

    set_rows = 8 * PART

    def scatter_scratch():
        return [
            pltpu.VMEM((PIECES, 4, set_rows, half), bf16), pltpu.VMEM((PIECES, 4, set_rows, half), bf16),
            pltpu.VMEM((PIECES, 4, set_rows, half), bf16), pltpu.VMEM((PIECES, set_rows, half), f32),
            pltpu.VMEM((PIECES, set_rows, half), bf16), pltpu.VMEM((PIECES, 2, set_rows, half), bf16),
            pltpu.VMEM((PIECES, 3, 2 * PART, half), bf16), pltpu.VMEM((PIECES, PART, half), f32),
            pltpu.VMEM((PIECES, PART, half), f32),
        ]

    return pl.pallas_call(
        tail_kernel,
        out_shape=(jax.ShapeDtypeStruct((32, width), bf16), jax.ShapeDtypeStruct((32, width), bf16)),
        in_specs=[vmem, anywhere, vmem, anywhere, anywhere],
        out_specs=(vmem, vmem),
        scratch_shapes=[
            pltpu.VMEM(w_out.shape, bf16), pltpu.VMEM(w_gu.shape, bf16), pltpu.VMEM(w_down.shape, bf16),
            pltpu.SemaphoreType.DMA((3,)), pltpu.SemaphoreType.DMA((TAIL_ROLES,)),
            pltpu.SemaphoreType.DMA((TAIL_ROLES,)),
            *scatter_scratch(), *scatter_scratch(),
            pltpu.VMEM((tok_grp, width), bf16), pltpu.VMEM((tok_grp, units), bf16),
        ],
        compiler_params=pltpu.CompilerParams(
            collective_id=0, has_side_effects=True, vmem_limit_bytes=66000000
        ),
        name="tail",
    )(heads_out, w_out, gain_ff, w_gu, w_down)


FRONT_BLOCKS = 36
WINDOW = 768


def front_kernel(
    slot_ref, choice_ref, lengths_ref, tokens_ref, gain_ref, down_hbm, up_ref, w_hbm, cache_hbm, heads_ref,
    w_qkv, w_latent, rows_buf, load_sems, send_sems, recv_sems,
    first_0, first_1, second_0, second_1, pass_0, pass_1, split_0, split_1,
    prefix, qkv, top, denom, total,
):
    x, z, c = place()
    hid = lax.axis_index("hid")
    req = lax.axis_index("req")
    lower, upper = (req + 3) % 4, (req + 1) % 4
    width = tokens_ref.shape[1]
    bf16, f32 = jnp.bfloat16, jnp.float32
    first, second = (first_0, first_1), (second_0, second_1)
    passed, split = (pass_0, pass_1), (split_0, split_1)

    def owner(group):
        return slot_ref[choice_ref[group]]

    peers = [{"hid": (hid + d) % 32} for d in range(1, 32)] + [{"req": lower}, {"req": upper}]
    barrier = pltpu.get_barrier_semaphore()
    for peer in peers:
        pl.semaphore_signal(barrier, inc=1, device_id=peer, device_id_type=MESH)
    latent_load = pltpu.make_async_copy(down_hbm, w_latent, load_sems.at[5])
    latent_load.start()
    loads = []
    for k in range(2):
        for half in range(2):
            copy = pltpu.make_async_copy(
                cache_hbm.at[pl.ds(half * 32 + k * 16, 16)], first[k].at[half], load_sems.at[1 + 2 * k + half]
            )
            copy.start()
            loads.append(copy)
    w_load = pltpu.make_async_copy(w_hbm, w_qkv, load_sems.at[0])
    w_load.start()

    matrix = tokens_ref[...].astype(f32)
    normed = rms_scale(matrix, gain_ref[...].reshape(1, width)).astype(bf16)
    own_rows = pl.ds(pl.multiple_of(hid * 32, 32), 32)
    rows_buf[own_rows, pl.ds(0, width)] = normed
    pl.semaphore_wait(barrier, len(peers))

    mail = Mail(send_sems, recv_sems)
    y_base = GATHER_ROLES
    deal_base = y_base + 8

    def y_copy(role, src, dst, to):
        return pltpu.make_async_remote_copy(
            src_ref=src, dst_ref=dst, send_sem=send_sems.at[role], recv_sem=recv_sems.at[role],
            device_id={"req": to}, device_id_type=MESH,
        )

    def y_send(role, src, dst, to):
        copy = y_copy(role, src, dst, to)
        copy.start()
        mail.sent[role] = copy

    def y_start():
        for k in range(2):
            y_send(y_base + k, cache_hbm.at[pl.ds(k * 16, 16)], first[k].at[2], lower)
            y_send(y_base + 2 + k, cache_hbm.at[pl.ds(32 + k * 16, 16)], first[k].at[3], upper)

    def y_pass(k):
        loads[2 * k].wait()
        loads[2 * k + 1].wait()
        y_copy(y_base + k, first[k].at[2], first[k].at[2], upper).wait_recv()
        y_copy(y_base + 2 + k, first[k].at[3], first[k].at[3], lower).wait_recv()
        passed[k][0] = first[k][jnp.where(owner(lower) == req, 1, 2)]
        y_send(y_base + 4 + k, passed[k].at[0], second[k].at[0], lower)
        passed[k][1] = first[k][jnp.where(owner(upper) == req, 0, 3)]
        y_send(y_base + 6 + k, passed[k].at[1], second[k].at[1], upper)

    def deal(k):
        y_copy(y_base + 4 + k, second[k].at[0], second[k].at[0], upper).wait_recv()
        y_copy(y_base + 6 + k, second[k].at[1], second[k].at[1], lower).wait_recv()
        away = (owner(req) - req + 4) % 4
        late_a = jnp.full((1, 1, 1), (away >= 2).astype(jnp.int32)) > 0
        late_b = jnp.full((1, 1, 1), jnp.logical_or(away == 1, away == 2).astype(jnp.int32)) > 0
        half_a = jnp.where(late_a, second[k][jnp.where(away == 2, 0, 1)], first[k][jnp.where(away == 0, 0, 2)])
        half_b = jnp.where(late_b, second[k][jnp.where(away == 1, 0, 1)], first[k][jnp.where(away == 0, 1, 3)])
        r = lax.broadcasted_iota(jnp.int32, (32, 32), 0)
        s = lax.broadcasted_iota(jnp.int32, (32, 32), 1)
        sort = (s == jnp.where(r < 16, 2 * r, 2 * r - 31)).astype(bf16)
        zeros = jnp.zeros((16, 256 - HD), bf16)
        for half, value in enumerate((half_a, half_b)):
            planes = jnp.dot(sort, value.reshape(32, width), preferred_element_type=f32).astype(bf16)
            for kv in range(2):
                for h in range(32):
                    piece = planes[kv * 16:(kv + 1) * 16, h * HD:(h + 1) * HD]
                    split[k][h, kv, pl.ds(half * 16, 16), :] = jnp.concatenate([piece, zeros], axis=1)

        landing = prefix.at[k, :, own_rows]
        for d in range(1, 32):
            to = (hid + d) % 32
            mail.send(deal_base + k * 31 + d - 1, split[k].at[to], landing, to)
        prefix[k, :, own_rows] = split[k][hid]

    def dealt(k):
        for d in range(1, 32):
            source = (hid + 32 - d) % 32
            landing = prefix.at[k, :, pl.ds(pl.multiple_of(source * 32, 32), 32)]
            mail.await_recv(deal_base + k * 31 + d - 1, landing, source)

    y_start()
    latent_load.wait()
    latent = jnp.dot(normed, w_latent[...], preferred_element_type=f32)
    rows_buf[own_rows, pl.ds(width, 128)] = latent.astype(bf16)
    gather = Gather(mail, 0, rows_buf, 32)
    contract = (((1,), (1,)), ((), ()))

    def project(own, partners):
        gather.from_partner(*partners)
        places = [gather.owner(*at) for at in own] + [gather.owner(*at, True) for at in partners]
        slices = [pl.ds(pl.multiple_of(place * 32, 32), 32) for place in places]
        rows = jnp.concatenate([rows_buf[at, pl.ds(0, width)] for at in slices], axis=0)
        latents = jnp.concatenate([rows_buf[at, pl.ds(width, 128)] for at in slices], axis=0)
        pad = jnp.zeros((rows.shape[0], 256 - HD), bf16)
        for part in range(3):
            value = lax.dot_general(
                rows, w_qkv[pl.ds(part * HD, HD), :], contract, preferred_element_type=f32
            )
            if part == 0:
                value = value + lax.dot_general(latents, up_ref[...], contract, preferred_element_type=f32)
            value = jnp.concatenate([value.astype(bf16), pad], axis=1)
            for n, at in enumerate(slices):
                qkv[part, at, :] = value[n * 32:(n + 1) * 32]

    for stage in gather.stages():
        if stage == "relay0":
            y_pass(0)
        if stage == "relay2":
            w_load.wait()
            project([(0, 0), (0, 1), (0, 2), (1, 0), (2, 0)], [(0, 0), (0, 1), (0, 2)])
        if stage == "relay3":
            y_pass(1)
            project([(1, 1), (2, 1), (1, 2), (2, 2), (0, 3), (3, 0)], [(1, 0), (2, 0)])
            deal(0)
        if stage == "far3":
            project([(1, 3), (2, 3)], [(0, 3), (1, 1), (2, 1), (1, 2), (2, 2), (3, 0)])
    deal(1)
    project([(3, 1), (3, 2), (3, 3)], [(1, 3), (2, 3), (3, 1), (3, 2), (3, 3)])

    dealt(0)

    ends = [lengths_ref[0, 0]]
    for n in range(1, lengths_ref.shape[1]):
        ends.append(ends[-1] + lengths_ref[0, n])
    factor = HD ** (-0.5)

    @pl.loop(0, 8)
    def _(i):
        at = pl.ds(pl.multiple_of(i * 128, 128), 128)
        begin = jnp.minimum(jnp.maximum(i * 128 - 512, 0), 1024 - WINDOW)
        near = pl.ds(pl.multiple_of(begin, 128), WINDOW)
        q = qkv[0, at, :]
        s_far = lax.dot_general(q, prefix[0, 0], contract, preferred_element_type=f32) * factor
        s_near = lax.dot_general(q, qkv[1, near, :], contract, preferred_element_type=f32) * factor
        row = lax.broadcasted_iota(jnp.int32, (128, 1), 0) + i * 128
        since = jnp.zeros((128, 1), jnp.int32)
        for end in ends:
            since = jnp.where(row >= end, jnp.maximum(since, end), since)
        col = lax.broadcasted_iota(jnp.int32, (128, WINDOW), 1) + begin
        s_near = jnp.where(jnp.logical_and(col >= since, col <= row), s_near, -jnp.inf)
        row_max = jnp.maximum(
            jnp.max(s_far, axis=1, keepdims=True), jnp.max(s_near, axis=1, keepdims=True)
        )
        e_far = jnp.exp(s_far - row_max)
        e_near = jnp.exp(s_near - row_max)
        top[at, :] = row_max
        denom[at, :] = jnp.sum(e_far, axis=1, keepdims=True) + jnp.sum(e_near, axis=1, keepdims=True)
        out = jnp.dot(e_far.astype(bf16), prefix[0, 1], preferred_element_type=f32)
        total[at, :] = out + jnp.dot(e_near.astype(bf16), qkv[2, near, :], preferred_element_type=f32)

    dealt(1)

    @pl.loop(0, 8)
    def _(i):
        at = pl.ds(pl.multiple_of(i * 128, 128), 128)
        scores = lax.dot_general(qkv[0, at, :], prefix[1, 0], contract, preferred_element_type=f32) * factor
        row_max = jnp.maximum(top[at, :], jnp.max(scores, axis=1, keepdims=True))
        keep = jnp.exp(top[at, :] - row_max)
        expos = jnp.exp(scores - row_max)
        row_sum = denom[at, :] * keep + jnp.sum(expos, axis=1, keepdims=True)
        out = total[at, :] * keep + jnp.dot(expos.astype(bf16), prefix[1, 1], preferred_element_type=f32)
        heads_ref[at, :] = (out / row_sum)[:, :HD].astype(bf16)

    mail.drain()


def front(slots, choices, lengths, tokens, gain_in, adapt_down, up_t, w_t, cache):
    rows, width = tokens.shape
    tok_grp = rows * 32
    bf16 = jnp.bfloat16
    smem = pl.BlockSpec(memory_space=pltpu.SMEM)
    vmem = pl.BlockSpec(memory_space=pltpu.VMEM)
    anywhere = pl.BlockSpec(memory_space=pl.ANY)
    roles = GATHER_ROLES + 8 + 62

    def halves(count):
        return pltpu.VMEM((count, 16, 2, width), bf16)

    return pl.pallas_call(
        front_kernel,
        out_shape=jax.ShapeDtypeStruct((tok_grp, HD), bf16),
        in_specs=[smem, smem, smem, vmem, vmem, anywhere, vmem, anywhere, anywhere],
        out_specs=vmem,
        scratch_shapes=[
            pltpu.VMEM(w_t.shape, bf16), pltpu.VMEM(adapt_down.shape, bf16),
            pltpu.VMEM((tok_grp, width + 128), bf16),
            pltpu.SemaphoreType.DMA((6,)), pltpu.SemaphoreType.DMA((roles,)),
            pltpu.SemaphoreType.DMA((roles,)),
            halves(4), halves(4), halves(2), halves(2), halves(2), halves(2),
            pltpu.VMEM((32, 2, 32, 256), bf16), pltpu.VMEM((32, 2, 32, 256), bf16),
            pltpu.VMEM((2, 2, tok_grp, 256), bf16), pltpu.VMEM((3, tok_grp, 256), bf16),
            pltpu.VMEM((tok_grp, 1), jnp.float32), pltpu.VMEM((tok_grp, 1), jnp.float32),
            pltpu.VMEM((tok_grp, 256), jnp.float32),
        ],
        compiler_params=pltpu.CompilerParams(
            collective_id=1, has_side_effects=True, vmem_limit_bytes=66000000
        ),
        name="front",
    )(slots, choices, lengths, tokens, gain_in, adapt_down, up_t, w_t, cache)


def settle_kernel(attn_ref, block_ref, attn_out, block_out):
    attn_out[...] = attn_ref[...]
    block_out[...] = block_ref[...]


def settle(attn, block):
    vmem = pl.BlockSpec(memory_space=pltpu.VMEM)
    return pl.pallas_call(
        settle_kernel,
        out_shape=(jax.ShapeDtypeStruct(attn.shape, attn.dtype), jax.ShapeDtypeStruct(block.shape, block.dtype)),
        in_specs=[vmem, vmem],
        out_specs=(vmem, vmem),
        name="settle",
    )(attn, block)


def per_device(
    tokens,
    gain_in,
    w_qkv,
    adapt_down,
    adapt_up,
    w_out,
    gain_ff,
    w_gate_up,
    w_down,
    prefix_cache,
    prefix_owner,
    group_prefix,
    lengths,
):
    w_t = jnp.transpose(w_qkv, (1, 2, 0)).reshape(3 * w_qkv.shape[2], w_qkv.shape[0])
    w_gu = jnp.transpose(w_gate_up, (1, 2, 0)).reshape(2 * w_gate_up.shape[2], w_gate_up.shape[0])
    heads_out = front(
        prefix_owner, group_prefix, lengths, tokens, gain_in, adapt_down, adapt_up.T, w_t, prefix_cache[0]
    )
    return settle(*tail(heads_out, w_out, gain_ff, w_gu, w_down))


def solution(mesh):
    placed = (
        P(("req", "hid"), None),
        P(),
        P(None, None, "hid"),
        P(),
        P(None, "hid"),
        P("hid", None),
        P(),
        P(None, None, "hid"),
        P("hid", None),
        P("req", "hid", None, None),
        P(),
        P(),
        P("req", None),
    )
    return jax.shard_map(
        per_device,
        mesh=mesh,
        in_specs=placed,
        out_specs=(P(("req", "hid"), None), P(("req", "hid"), None)),
        check_vma=False,
    )
```

```python
import jax
import jax.numpy as jnp
from jax import lax
from jax.experimental import pallas as pl
from jax.experimental.pallas import tpu as pltpu
from jax.sharding import PartitionSpec as P

HD = 224


EPS = 1e-05


def rms_scale(matrix, gain_vec):
    return matrix * lax.rsqrt(jnp.mean(matrix * matrix, axis=-1, keepdims=True) + EPS) * gain_vec


MESH = pl.DeviceIdType.MESH
NX, NZ = 4, 4


def place():
    hid = lax.axis_index("hid")
    return hid // 8, (hid // 2) % 4, hid % 2


def moved(da, db, core_flip=0):
    x, z, c = place()
    xn = (x + 4 + (1 - c) * db + c * da) % 4
    zn = (z + 4 + (1 - c) * da + c * db) % 4
    cn = c + core_flip * (1 - 2 * c)
    return xn * 8 + zn * 2 + cn


def remote(src, dst, send, recv, hid):
    return pltpu.make_async_remote_copy(
        src_ref=src, dst_ref=dst, send_sem=send, recv_sem=recv,
        device_id={"hid": hid}, device_id_type=MESH,
    )


class Mail:
    def __init__(self, send_sems, recv_sems):
        self.send_sems, self.recv_sems, self.sent = send_sems, recv_sems, {}

    def send(self, role, src, dst, hid):
        copy = remote(src, dst, self.send_sems.at[role], self.recv_sems.at[role], hid)
        copy.start()
        self.sent[role] = copy

    def await_recv(self, role, dst, hid):
        remote(dst, dst, self.send_sems.at[role], self.recv_sems.at[role], hid).wait_recv()

    def drain(self):
        for copy in self.sent.values():
            copy.wait_send()


GATHER_ROLES = 36
OFFS = (0, -1, 1, 2)


class Gather:
    def __init__(self, mail, base, buf, rows, first_row=0, split_columns=False):
        self.mail, self.base, self.buf, self.rows = mail, base, buf, rows
        self.first_row, self.split_columns = first_row, split_columns
        self.a_plus, self.a_minus = moved(1, 0), moved(-1, 0)
        self.b_plus, self.b_minus = moved(0, 1), moved(0, -1)
        self.partner = moved(0, 0, 1)
        self.seen = set()

    def row_slice(self, hid):
        return pl.ds(pl.multiple_of(self.first_row + hid * self.rows, self.rows), self.rows)

    def blk(self, hid, part=None):
        start = pl.multiple_of(self.first_row + hid * self.rows, self.rows)
        if part is None:
            return self.buf.at[self.row_slice(hid)]
        if self.split_columns:
            half = self.buf.shape[1] // 2
            return self.buf.at[self.row_slice(hid), pl.ds(part * half, half)]
        half = self.rows // 2
        return self.buf.at[pl.ds(start + part * half, half)]

    def owner(self, ia, ib, from_partner=False):
        if from_partner:
            return moved(OFFS[ib], OFFS[ia], 1)
        return moved(OFFS[ia], OFFS[ib])

    def forward(self, role, block, to):
        self.mail.send(self.base + role, block, block, to)

    def to_partner(self, ia, ib):
        self.forward(20 + ia * 4 + ib, self.blk(self.owner(ia, ib)), self.partner)

    def from_partner(self, *places):
        for ia, ib in places:
            if (ia, ib) not in self.seen:
                self.seen.add((ia, ib))
                self.mail.await_recv(
                    self.base + 20 + ia * 4 + ib, self.blk(self.owner(ia, ib, True)), self.partner
                )

    def line_out(self, i):
        block = self.blk(self.owner(0, i))
        self.forward(4 + 4 * i, block, self.a_plus)
        self.forward(5 + 4 * i, block, self.a_minus)

    def line_relay(self, i):
        low, high = self.owner(1, i), self.owner(2, i)
        self.mail.await_recv(self.base + 4 + 4 * i, self.blk(low), self.a_minus)
        self.forward(6 + 4 * i, self.blk(low, 0), self.a_plus)
        self.mail.await_recv(self.base + 5 + 4 * i, self.blk(high), self.a_plus)
        self.forward(7 + 4 * i, self.blk(high, 1), self.a_minus)
        self.to_partner(1, i)
        self.to_partner(2, i)

    def line_far(self, i):
        far = self.owner(3, i)
        self.mail.await_recv(self.base + 6 + 4 * i, self.blk(far, 0), self.a_minus)
        self.mail.await_recv(self.base + 7 + 4 * i, self.blk(far, 1), self.a_plus)
        self.to_partner(3, i)

    def stages(self):
        mail, base, blk = self.mail, self.base, self.blk
        own, low, high, far = (self.owner(0, i) for i in range(4))
        self.forward(0, blk(own), self.b_plus)
        self.forward(1, blk(own), self.b_minus)
        self.line_out(0)
        self.to_partner(0, 0)
        yield "start"
        mail.await_recv(base + 0, blk(low), self.b_minus)
        self.forward(2, blk(low, 0), self.b_plus)
        self.line_out(1)
        self.to_partner(0, 1)
        mail.await_recv(base + 1, blk(high), self.b_plus)
        self.forward(3, blk(high, 1), self.b_minus)
        self.line_out(2)
        self.to_partner(0, 2)
        self.line_relay(0)
        yield "relay0"
        mail.await_recv(base + 2, blk(far, 0), self.b_minus)
        mail.await_recv(base + 3, blk(far, 1), self.b_plus)
        self.line_out(3)
        self.to_partner(0, 3)
        self.line_relay(1)
        yield "relay1"
        self.line_relay(2)
        yield "relay2"
        self.line_far(0)
        yield "far0"
        self.line_relay(3)
        yield "relay3"
        self.line_far(1)
        yield "far1"
        self.line_far(2)
        yield "far2"
        self.line_far(3)
        yield "far3"

    def finish(self):
        self.from_partner(*[(ia, ib) for ia in range(4) for ib in range(4)])


PIECES = 2
PART = 16
PIECE_ROLES = 14


class Scatter:
    def __init__(self, mail, base, product, xs, xr, sums, acc, near, mid, last, swap_out, swap_in):
        self.mail, self.base, self.product = mail, base, product
        self.xs, self.xr, self.sums, self.acc = xs, xr, sums, acc
        self.near, self.mid, self.last = near, mid, last
        self.swap_out, self.swap_in = swap_out, swap_in
        x, z, c = place()
        self.c = c
        self.a = (1 - c) * z + c * x
        self.b = (1 - c) * x + c * z
        self.partner = moved(0, 0, 1)
        self.a_plus, self.a_minus = moved(1, 0), moved(-1, 0)
        self.b_plus, self.b_minus, self.b_far = moved(0, 1), moved(0, -1), moved(0, 2)
        self.lo, self.hi = pl.ds(0, 4 * PART), pl.ds(4 * PART, 4 * PART)

    def role(self, p, n):
        return self.base + PIECE_ROLES * p + n

    def set_chips(self, k, cc):
        return [(1 - cc) * (j * 4 + k) + cc * (k * 4 + j) for j in range(4)]

    def partner_part(self, p, idx):
        c, step = self.c, (2, 1, 3, 0)[idx]
        chips = self.set_chips((self.b + step) % 4, 1 - c)
        self.product(chips, 1 - c, p, self.xs.at[p, idx], None)
        self.mail.send(self.role(p, idx), self.xs.at[p, idx], self.xr.at[p, idx], self.partner)

    def own_part(self, p, idx, out):
        c, step = self.c, (2, 1, 3, 0)[idx]
        self.mail.await_recv(self.role(p, idx), self.xr.at[p, idx], self.partner)
        self.product(self.set_chips((self.a + step) % 4, c), c, p, out, self.xr.at[p, idx])

    def far_sets(self, p):
        sums, near = self.sums, self.near
        self.partner_part(p, 0)
        self.partner_part(p, 1)
        self.own_part(p, 0, sums.at[p, 0])
        self.mail.send(self.role(p, 4), sums.at[p, 0, self.lo], near.at[p, self.lo], self.a_plus)
        self.mail.send(self.role(p, 5), sums.at[p, 0, self.hi], near.at[p, self.hi], self.a_minus)

    def next_sets(self, p):
        sums, mid = self.sums, self.mid
        self.partner_part(p, 2)
        self.own_part(p, 1, sums.at[p, 1])
        self.mail.send(self.role(p, 6), sums.at[p, 1, self.hi], mid.at[p, 0, self.hi], self.a_plus)
        self.partner_part(p, 3)
        self.own_part(p, 2, sums.at[p, 2])
        self.mail.send(self.role(p, 7), sums.at[p, 2, self.lo], mid.at[p, 1, self.lo], self.a_minus)

    def pass_on(self, p):
        f32, bf16 = jnp.float32, jnp.bfloat16
        sums, near, mid, lo, hi = self.sums, self.near, self.mid, self.lo, self.hi
        self.mail.await_recv(self.role(p, 4), near.at[p, lo], self.a_minus)
        sums[p, 1, lo] = (sums[p, 1, lo].astype(f32) + near[p, lo].astype(f32)).astype(bf16)
        self.mail.send(self.role(p, 8), sums.at[p, 1, lo], mid.at[p, 0, lo], self.a_plus)
        self.mail.await_recv(self.role(p, 5), near.at[p, hi], self.a_plus)
        sums[p, 2, hi] = (sums[p, 2, hi].astype(f32) + near[p, hi].astype(f32)).astype(bf16)
        self.mail.send(self.role(p, 9), sums.at[p, 2, hi], mid.at[p, 1, hi], self.a_minus)

    def own_set(self, p):
        self.own_part(p, 3, self.acc.at[p])

    def chunk(self, j):
        return pl.ds(pl.multiple_of(j * 2 * PART, 2 * PART), 2 * PART)

    def chunk_sum(self, p, j):
        at = self.chunk(j)
        value = self.acc[p, at] + self.mid[p, 0, at].astype(jnp.float32)
        return value + self.mid[p, 1, at].astype(jnp.float32)

    def second(self, p):
        mid, q = self.mid, self.sums
        self.mail.await_recv(self.role(p, 6), mid.at[p, 0, self.hi], self.a_minus)
        self.mail.await_recv(self.role(p, 7), mid.at[p, 1, self.lo], self.a_plus)
        self.mail.await_recv(self.role(p, 8), mid.at[p, 0, self.lo], self.a_minus)
        self.mail.await_recv(self.role(p, 9), mid.at[p, 1, self.hi], self.a_plus)
        for n, (step, to) in enumerate(((2, self.b_far), (1, self.b_plus), (3, self.b_minus))):
            j = (self.b + step) % 4
            q[p, 3, self.chunk(j)] = self.chunk_sum(p, j).astype(jnp.bfloat16)
            self.mail.send(self.role(p, 10 + n), q.at[p, 3, self.chunk(j)], self.last.at[p, n], to)

    def settle(self, p):
        value = self.chunk_sum(p, self.b)
        for n, source in ((1, self.b_minus), (2, self.b_plus), (0, self.b_far)):
            self.mail.await_recv(self.role(p, 10 + n), self.last.at[p, n], source)
        for n in range(3):
            value = value + self.last[p, n].astype(jnp.float32)
        is_first = self.c == 0
        self.swap_out[p] = jnp.where(is_first, value[PART:], value[:PART])
        self.mail.send(self.role(p, 13), self.swap_out.at[p], self.swap_in.at[p], self.partner)
        return jnp.where(is_first, value[:PART], value[PART:])

    def other(self, p):
        self.mail.await_recv(self.role(p, 13), self.swap_in.at[p], self.partner)
        return self.swap_in[p]


TAIL_ROLES = PIECE_ROLES * PIECES * 2 + GATHER_ROLES * PIECES


def tail_kernel(
    heads_ref, w_out_hbm, gain_ref, w_gu_hbm, w_down_hbm, attn_ref, block_ref,
    w_out, w_gu, w_down, load_sems, send_sems, recv_sems, *scratch,
):
    *scatter_refs, ff_buf, hidden = scratch
    x, z, c = place()
    loads = [
        pltpu.make_async_copy(w_out_hbm, w_out, load_sems.at[0]),
        pltpu.make_async_copy(w_gu_hbm, w_gu, load_sems.at[1]),
        pltpu.make_async_copy(w_down_hbm, w_down, load_sems.at[2]),
    ]
    peers = [
        {"hid": moved(1, 0)}, {"hid": moved(-1, 0)}, {"hid": moved(0, 1)},
        {"hid": moved(0, -1)}, {"hid": moved(0, 2)}, {"hid": moved(0, 0, 1)},
    ]
    barrier = pltpu.get_barrier_semaphore()
    for peer in peers:
        pl.semaphore_signal(barrier, inc=1, device_id=peer, device_id_type=MESH)
    for load in loads:
        load.start()
    pl.semaphore_wait(barrier, len(peers))
    mail = Mail(send_sems, recv_sems)
    width = w_out.shape[1] // 2
    units = w_down.shape[0]
    count = heads_ref.shape[0] // PIECES

    def product_of(lhs_rows, weight):
        def product(chips, half, p, out, other):
            rows = jnp.concatenate([r for chip in chips for r in lhs_rows(p, chip)], axis=0)
            cols = pl.ds(pl.multiple_of(half * width, 128), width)
            value = jnp.dot(rows, weight[:, cols], preferred_element_type=jnp.float32)
            if other is not None:
                value = value + other[...].astype(jnp.float32)
            out[...] = value.astype(out.dtype)
        return product

    def heads_rows(p, chip):
        return [
            heads_ref[pl.ds(pl.multiple_of(chip * 64 + core * 32 + p * PART, PART), PART), :]
            for core in range(2)
        ]

    def hidden_rows(p, chip):
        return [hidden[pl.ds(pl.multiple_of(p * count + chip * 2 * PART, 2 * PART), 2 * PART), :]]

    outer = Scatter(mail, 0, product_of(heads_rows, w_out), *scatter_refs[:9])
    gathers = [
        Gather(
            mail, PIECE_ROLES * PIECES + GATHER_ROLES * p, ff_buf, PART,
            first_row=p * count, split_columns=True,
        )
        for p in range(PIECES)
    ]
    inner = Scatter(
        mail, PIECE_ROLES * PIECES + GATHER_ROLES * PIECES, product_of(hidden_rows, w_down), *scatter_refs[9:]
    )
    mine_at = pl.ds(pl.multiple_of(c * width, 128), width)
    other_at = pl.ds(pl.multiple_of((1 - c) * width, 128), width)
    gain_mine = gain_ref[mine_at].reshape(1, width)
    gain_other = gain_ref[other_at].reshape(1, width)

    def normalise(p, mine):
        other = outer.other(p)
        rows = pl.ds(p * PART, PART)
        attn_ref[rows, mine_at] = mine.astype(jnp.bfloat16)
        attn_ref[rows, other_at] = other.astype(jnp.bfloat16)
        total = jnp.sum(mine * mine, axis=1, keepdims=True) + jnp.sum(other * other, axis=1, keepdims=True)
        scale = lax.rsqrt(total / (2 * width) + EPS)
        own_rows = gathers[p].row_slice(moved(0, 0))
        ff_buf[own_rows, mine_at] = (mine * scale * gain_mine).astype(jnp.bfloat16)
        ff_buf[own_rows, other_at] = (other * scale * gain_other).astype(jnp.bfloat16)

    def feed(p, part):
        contract = (((1,), (1,)), ((), ()))
        at = pl.ds(p * count + part * (count // 2), count // 2)
        rows = ff_buf[at, :]
        gate = lax.dot_general(rows, w_gu[pl.ds(0, units), :], contract, preferred_element_type=jnp.float32)
        up = lax.dot_general(rows, w_gu[pl.ds(units, units), :], contract, preferred_element_type=jnp.float32)
        hidden[at, :] = (jax.nn.silu(gate) * up).astype(jnp.bfloat16)

    loads[0].wait()
    outer.far_sets(0)
    outer.next_sets(0)
    outer.pass_on(0)
    outer.far_sets(1)
    outer.next_sets(1)
    outer.own_set(0)
    outer.second(0)
    outer.pass_on(1)
    outer.own_set(1)
    stages = [gather.stages() for gather in gathers]
    normalise(0, outer.settle(0))
    next(stages[0])
    outer.second(1)
    assert next(stages[0]) == "relay0"
    normalise(1, outer.settle(1))
    next(stages[1])
    assert next(stages[0]) == "relay1"
    assert next(stages[1]) == "relay0"
    assert next(stages[0]) == "relay2"
    assert next(stages[1]) == "relay1"
    next(stages[0])
    assert next(stages[0]) == "relay3"
    assert next(stages[1]) == "relay2"
    next(stages[1])
    for name in ("far1", "far2", "far3"):
        assert next(stages[0]) == name
    assert next(stages[1]) == "relay3"
    loads[1].wait()
    gathers[0].finish()
    feed(0, 0)
    for name in ("far1", "far2", "far3"):
        assert next(stages[1]) == name
    feed(0, 1)
    loads[2].wait()
    inner.far_sets(0)
    inner.next_sets(0)
    gathers[1].finish()
    feed(1, 0)
    inner.pass_on(0)
    feed(1, 1)
    inner.far_sets(1)
    inner.next_sets(1)
    inner.own_set(0)
    inner.second(0)
    inner.pass_on(1)
    inner.own_set(1)
    first = inner.settle(0)
    inner.second(1)
    for p, mine in enumerate((first, None)):
        if mine is None:
            mine = inner.settle(p)
        rows = pl.ds(p * PART, PART)
        block_ref[rows, mine_at] = mine.astype(jnp.bfloat16)
        block_ref[rows, other_at] = inner.other(p).astype(jnp.bfloat16)
    mail.drain()


def tail(heads_out, w_out, gain_ff, w_gu, w_down):
    tok_grp = heads_out.shape[0]
    width = w_out.shape[1]
    half = width // 2
    units = w_down.shape[0]
    bf16, f32 = jnp.bfloat16, jnp.float32
    vmem = pl.BlockSpec(memory_space=pltpu.VMEM)
    anywhere = pl.BlockSpec(memory_space=pl.ANY)

    set_rows = 8 * PART

    def scatter_scratch():
        return [
            pltpu.VMEM((PIECES, 4, set_rows, half), bf16), pltpu.VMEM((PIECES, 4, set_rows, half), bf16),
            pltpu.VMEM((PIECES, 4, set_rows, half), bf16), pltpu.VMEM((PIECES, set_rows, half), f32),
            pltpu.VMEM((PIECES, set_rows, half), bf16), pltpu.VMEM((PIECES, 2, set_rows, half), bf16),
            pltpu.VMEM((PIECES, 3, 2 * PART, half), bf16), pltpu.VMEM((PIECES, PART, half), f32),
            pltpu.VMEM((PIECES, PART, half), f32),
        ]

    return pl.pallas_call(
        tail_kernel,
        out_shape=(jax.ShapeDtypeStruct((32, width), bf16), jax.ShapeDtypeStruct((32, width), bf16)),
        in_specs=[vmem, anywhere, vmem, anywhere, anywhere],
        out_specs=(vmem, vmem),
        scratch_shapes=[
            pltpu.VMEM(w_out.shape, bf16), pltpu.VMEM(w_gu.shape, bf16), pltpu.VMEM(w_down.shape, bf16),
            pltpu.SemaphoreType.DMA((3,)), pltpu.SemaphoreType.DMA((TAIL_ROLES,)),
            pltpu.SemaphoreType.DMA((TAIL_ROLES,)),
            *scatter_scratch(), *scatter_scratch(),
            pltpu.VMEM((tok_grp, width), bf16), pltpu.VMEM((tok_grp, units), bf16),
        ],
        compiler_params=pltpu.CompilerParams(
            collective_id=0, has_side_effects=True, vmem_limit_bytes=66000000
        ),
        name="tail",
    )(heads_out, w_out, gain_ff, w_gu, w_down)


CHUNKS = 4
STEP = 8
WINDOW = 768


def front_kernel(
    slot_ref, choice_ref, lengths_ref, tokens_ref, gain_ref, down_hbm, up_ref, w_hbm, cache_hbm, heads_ref,
    w_qkv, w_latent, rows_buf, load_sems, send_sems, recv_sems,
    prefix, qkv, top, denom, total, *chunked,
):
    x, z, c = place()
    hid = lax.axis_index("hid")
    req = lax.axis_index("req")
    lower, upper = (req + 3) % 4, (req + 1) % 4
    width = tokens_ref.shape[1]
    bf16, f32 = jnp.bfloat16, jnp.float32
    first, second, passed, split = (chunked[n * CHUNKS:(n + 1) * CHUNKS] for n in range(4))

    def owner(group):
        return slot_ref[choice_ref[group]]

    peers = [{"hid": (hid + d) % 32} for d in range(1, 32)] + [{"req": lower}, {"req": upper}]
    barrier = pltpu.get_barrier_semaphore()
    for peer in peers:
        pl.semaphore_signal(barrier, inc=1, device_id=peer, device_id_type=MESH)
    latent_load = pltpu.make_async_copy(down_hbm, w_latent, load_sems.at[1])
    latent_load.start()
    def part_of(half, k):
        return cache_hbm.at[pl.ds(half * STEP * CHUNKS + k * STEP, STEP)]

    loads = []
    for k in range(CHUNKS):
        for half in range(2):
            copy = pltpu.make_async_copy(part_of(half, k), first[k].at[half], load_sems.at[2 + 2 * k + half])
            copy.start()
            loads.append(copy)
    w_load = pltpu.make_async_copy(w_hbm, w_qkv, load_sems.at[0])
    w_load.start()

    matrix = tokens_ref[...].astype(f32)
    normed = rms_scale(matrix, gain_ref[...].reshape(1, width)).astype(bf16)
    own_rows = pl.ds(pl.multiple_of(hid * 32, 32), 32)
    rows_buf[own_rows, pl.ds(0, width)] = normed
    pl.semaphore_wait(barrier, len(peers))

    mail = Mail(send_sems, recv_sems)
    y_base = GATHER_ROLES
    deal_base = y_base + 4 * CHUNKS
    deal_rows = 2 * STEP

    def y_copy(role, src, dst, to):
        return pltpu.make_async_remote_copy(
            src_ref=src, dst_ref=dst, send_sem=send_sems.at[role], recv_sem=recv_sems.at[role],
            device_id={"req": to}, device_id_type=MESH,
        )

    def y_send(role, src, dst, to):
        copy = y_copy(role, src, dst, to)
        copy.start()
        mail.sent[role] = copy

    def y_start():
        for k in range(CHUNKS):
            y_send(y_base + k, part_of(0, k), first[k].at[2], lower)
            y_send(y_base + CHUNKS + k, part_of(1, k), first[k].at[3], upper)

    def y_pass(k):
        loads[2 * k].wait()
        loads[2 * k + 1].wait()
        y_copy(y_base + k, first[k].at[2], first[k].at[2], upper).wait_recv()
        y_copy(y_base + CHUNKS + k, first[k].at[3], first[k].at[3], lower).wait_recv()
        passed[k][0] = first[k][jnp.where(owner(lower) == req, 1, 2)]
        y_send(y_base + 2 * CHUNKS + k, passed[k].at[0], second[k].at[0], lower)
        passed[k][1] = first[k][jnp.where(owner(upper) == req, 0, 3)]
        y_send(y_base + 3 * CHUNKS + k, passed[k].at[1], second[k].at[1], upper)

    def deal(k):
        y_copy(y_base + 2 * CHUNKS + k, second[k].at[0], second[k].at[0], upper).wait_recv()
        y_copy(y_base + 3 * CHUNKS + k, second[k].at[1], second[k].at[1], lower).wait_recv()
        away = (owner(req) - req + 4) % 4
        late_a = jnp.full((1, 1, 1), (away >= 2).astype(jnp.int32)) > 0
        late_b = jnp.full((1, 1, 1), jnp.logical_or(away == 1, away == 2).astype(jnp.int32)) > 0
        half_a = jnp.where(late_a, second[k][jnp.where(away == 2, 0, 1)], first[k][jnp.where(away == 0, 0, 2)])
        half_b = jnp.where(late_b, second[k][jnp.where(away == 1, 0, 1)], first[k][jnp.where(away == 0, 1, 3)])
        r = lax.broadcasted_iota(jnp.int32, (32, 32), 0)
        s = lax.broadcasted_iota(jnp.int32, (32, 32), 1)
        sort = (s == jnp.where(r < 16, 2 * r, 2 * r - 31)).astype(bf16)
        zeros = jnp.zeros((deal_rows, 256 - HD), bf16)
        value = jnp.concatenate([half_a.reshape(2 * STEP, width), half_b.reshape(2 * STEP, width)], axis=0)
        planes = jnp.dot(sort, value, preferred_element_type=f32).astype(bf16)
        for kv in range(2):
            for h in range(32):
                piece = planes[kv * deal_rows:(kv + 1) * deal_rows, h * HD:(h + 1) * HD]
                split[k][h, kv] = jnp.concatenate([piece, zeros], axis=1)

        for d in range(1, 32):
            to = (hid + d) % 32
            mail.send(deal_base + k * 31 + d - 1, split[k].at[to], landing(k, hid), to)
        prefix[:, pl.ds(pl.multiple_of(k * 512 + hid * deal_rows, deal_rows), deal_rows)] = split[k][hid]

    def landing(k, source):
        start = pl.multiple_of(k * 512 + source * deal_rows, deal_rows)
        return prefix.at[:, pl.ds(start, deal_rows)]

    def dealt(k):
        for d in range(1, 32):
            source = (hid + 32 - d) % 32
            mail.await_recv(deal_base + k * 31 + d - 1, landing(k, source), source)

    y_start()
    latent_load.wait()
    latent = jnp.dot(normed, w_latent[...], preferred_element_type=f32)
    rows_buf[own_rows, pl.ds(width, 128)] = latent.astype(bf16)
    gather = Gather(mail, 0, rows_buf, 32)
    contract = (((1,), (1,)), ((), ()))

    def project(own, partners):
        gather.from_partner(*partners)
        places = [gather.owner(*at) for at in own] + [gather.owner(*at, True) for at in partners]
        slices = [pl.ds(pl.multiple_of(place * 32, 32), 32) for place in places]
        rows = jnp.concatenate([rows_buf[at, pl.ds(0, width)] for at in slices], axis=0)
        latents = jnp.concatenate([rows_buf[at, pl.ds(width, 128)] for at in slices], axis=0)
        pad = jnp.zeros((rows.shape[0], 256 - HD), bf16)
        for part in range(3):
            value = lax.dot_general(
                rows, w_qkv[pl.ds(part * HD, HD), :], contract, preferred_element_type=f32
            )
            if part == 0:
                value = value + lax.dot_general(latents, up_ref[...], contract, preferred_element_type=f32)
            value = jnp.concatenate([value.astype(bf16), pad], axis=1)
            for n, at in enumerate(slices):
                qkv[part, at, :] = value[n * 32:(n + 1) * 32]

    for stage in gather.stages():
        if stage == "relay0":
            y_pass(0)
            y_pass(1)
        if stage == "relay2":
            w_load.wait()
            project([(0, 0), (0, 1), (0, 2), (1, 0), (2, 0)], [(0, 0), (0, 1), (0, 2)])
            y_pass(2)
            y_pass(3)
        if stage == "relay3":
            project([(1, 1), (2, 1), (1, 2), (2, 2), (0, 3), (3, 0)], [(1, 0), (2, 0)])
            deal(0)
        if stage == "far1":
            deal(1)
        if stage == "far3":
            deal(2)
            project([(1, 3), (2, 3)], [(0, 3), (1, 1), (2, 1), (1, 2), (2, 2), (3, 0)])
    deal(3)
    project([(3, 1), (3, 2), (3, 3)], [(1, 3), (2, 3), (3, 1), (3, 2), (3, 3)])

    dealt(0)
    dealt(1)

    ends = [lengths_ref[0, 0]]
    for n in range(1, lengths_ref.shape[1]):
        ends.append(ends[-1] + lengths_ref[0, n])
    factor = HD ** (-0.5)

    @pl.loop(0, 8)
    def _(i):
        at = pl.ds(pl.multiple_of(i * 128, 128), 128)
        begin = jnp.minimum(jnp.maximum(i * 128 - 512, 0), 1024 - WINDOW)
        near = pl.ds(pl.multiple_of(begin, 128), WINDOW)
        q = qkv[0, at, :]
        s_far = lax.dot_general(q, prefix[0, pl.ds(0, 1024), :], contract, preferred_element_type=f32) * factor
        s_near = lax.dot_general(q, qkv[1, near, :], contract, preferred_element_type=f32) * factor
        row = lax.broadcasted_iota(jnp.int32, (128, 1), 0) + i * 128
        since = jnp.zeros((128, 1), jnp.int32)
        for end in ends:
            since = jnp.where(row >= end, jnp.maximum(since, end), since)
        col = lax.broadcasted_iota(jnp.int32, (128, WINDOW), 1) + begin
        s_near = jnp.where(jnp.logical_and(col >= since, col <= row), s_near, -jnp.inf)
        row_max = jnp.maximum(
            jnp.max(s_far, axis=1, keepdims=True), jnp.max(s_near, axis=1, keepdims=True)
        )
        e_far = jnp.exp(s_far - row_max)
        e_near = jnp.exp(s_near - row_max)
        top[at, :] = row_max
        denom[at, :] = jnp.sum(e_far, axis=1, keepdims=True) + jnp.sum(e_near, axis=1, keepdims=True)
        out = jnp.dot(e_far.astype(bf16), prefix[1, pl.ds(0, 1024), :], preferred_element_type=f32)
        total[at, :] = out + jnp.dot(e_near.astype(bf16), qkv[2, near, :], preferred_element_type=f32)

    for k in (2, 3):
        dealt(k)
        more = pl.ds(k * 512, 512)

        @pl.loop(0, 4)
        def _(i):
            at = pl.ds(pl.multiple_of(i * 256, 256), 256)
            scores = lax.dot_general(
                qkv[0, at, :], prefix[0, more, :], contract, preferred_element_type=f32
            ) * factor
            row_max = jnp.maximum(top[at, :], jnp.max(scores, axis=1, keepdims=True))
            keep = jnp.exp(top[at, :] - row_max)
            expos = jnp.exp(scores - row_max)
            row_sum = denom[at, :] * keep + jnp.sum(expos, axis=1, keepdims=True)
            out = total[at, :] * keep + jnp.dot(
                expos.astype(bf16), prefix[1, more, :], preferred_element_type=f32
            )
            if k == 2:
                top[at, :] = row_max
                denom[at, :] = row_sum
                total[at, :] = out
            else:
                heads_ref[at, :] = (out / row_sum)[:, :HD].astype(bf16)

    mail.drain()


def front(slots, choices, lengths, tokens, gain_in, adapt_down, up_t, w_t, cache):
    rows, width = tokens.shape
    tok_grp = rows * 32
    bf16 = jnp.bfloat16
    smem = pl.BlockSpec(memory_space=pltpu.SMEM)
    vmem = pl.BlockSpec(memory_space=pltpu.VMEM)
    anywhere = pl.BlockSpec(memory_space=pl.ANY)
    roles = GATHER_ROLES + 4 * CHUNKS + 31 * CHUNKS

    def halves(count):
        return [pltpu.VMEM((count, STEP, 2, width), bf16)] * CHUNKS

    return pl.pallas_call(
        front_kernel,
        out_shape=jax.ShapeDtypeStruct((tok_grp, HD), bf16),
        in_specs=[smem, smem, smem, vmem, vmem, anywhere, vmem, anywhere, anywhere],
        out_specs=vmem,
        scratch_shapes=[
            pltpu.VMEM(w_t.shape, bf16), pltpu.VMEM(adapt_down.shape, bf16),
            pltpu.VMEM((tok_grp, width + 128), bf16),
            pltpu.SemaphoreType.DMA((2 + 2 * CHUNKS,)), pltpu.SemaphoreType.DMA((roles,)),
            pltpu.SemaphoreType.DMA((roles,)),
            pltpu.VMEM((2, 2048, 256), bf16), pltpu.VMEM((3, tok_grp, 256), bf16),
            pltpu.VMEM((tok_grp, 1), jnp.float32), pltpu.VMEM((tok_grp, 1), jnp.float32),
            pltpu.VMEM((tok_grp, 256), jnp.float32),
            *halves(4), *halves(2), *halves(2),
            *([pltpu.VMEM((32, 2, 2 * STEP, 256), bf16)] * CHUNKS),
        ],
        compiler_params=pltpu.CompilerParams(
            collective_id=1, has_side_effects=True, vmem_limit_bytes=66000000
        ),
        name="front",
    )(slots, choices, lengths, tokens, gain_in, adapt_down, up_t, w_t, cache)


def settle_kernel(attn_ref, block_ref, attn_out, block_out):
    attn_out[...] = attn_ref[...]
    block_out[...] = block_ref[...]


def settle(attn, block):
    vmem = pl.BlockSpec(memory_space=pltpu.VMEM)
    return pl.pallas_call(
        settle_kernel,
        out_shape=(jax.ShapeDtypeStruct(attn.shape, attn.dtype), jax.ShapeDtypeStruct(block.shape, block.dtype)),
        in_specs=[vmem, vmem],
        out_specs=(vmem, vmem),
        name="settle",
    )(attn, block)


def per_device(
    tokens,
    gain_in,
    w_qkv,
    adapt_down,
    adapt_up,
    w_out,
    gain_ff,
    w_gate_up,
    w_down,
    prefix_cache,
    prefix_owner,
    group_prefix,
    lengths,
):
    w_t = jnp.transpose(w_qkv, (1, 2, 0)).reshape(3 * w_qkv.shape[2], w_qkv.shape[0])
    w_gu = jnp.transpose(w_gate_up, (1, 2, 0)).reshape(2 * w_gate_up.shape[2], w_gate_up.shape[0])
    heads_out = front(
        prefix_owner, group_prefix, lengths, tokens, gain_in, adapt_down, adapt_up.T, w_t, prefix_cache[0]
    )
    return settle(*tail(heads_out, w_out, gain_ff, w_gu, w_down))


def solution(mesh):
    placed = (
        P(("req", "hid"), None),
        P(),
        P(None, None, "hid"),
        P(),
        P(None, "hid"),
        P("hid", None),
        P(),
        P(None, None, "hid"),
        P("hid", None),
        P("req", "hid", None, None),
        P(),
        P(),
        P("req", None),
    )
    return jax.shard_map(
        per_device,
        mesh=mesh,
        in_specs=placed,
        out_specs=(P(("req", "hid"), None), P(("req", "hid"), None)),
        check_vma=False,
    )
```

```python
import jax
import jax.numpy as jnp
from jax import lax
from jax.experimental import pallas as pl
from jax.experimental.pallas import tpu as pltpu
from jax.sharding import PartitionSpec as P

HD = 224


EPS = 1e-05


def rms_scale(matrix, gain_vec):
    return matrix * lax.rsqrt(jnp.mean(matrix * matrix, axis=-1, keepdims=True) + EPS) * gain_vec


MESH = pl.DeviceIdType.MESH
NX, NZ = 4, 4


def place():
    hid = lax.axis_index("hid")
    return hid // 8, (hid // 2) % 4, hid % 2


def moved(da, db, core_flip=0):
    x, z, c = place()
    xn = (x + 4 + (1 - c) * db + c * da) % 4
    zn = (z + 4 + (1 - c) * da + c * db) % 4
    cn = c + core_flip * (1 - 2 * c)
    return xn * 8 + zn * 2 + cn


def remote(src, dst, send, recv, hid):
    return pltpu.make_async_remote_copy(
        src_ref=src, dst_ref=dst, send_sem=send, recv_sem=recv,
        device_id={"hid": hid}, device_id_type=MESH,
    )


class Mail:
    def __init__(self, send_sems, recv_sems):
        self.send_sems, self.recv_sems, self.sent = send_sems, recv_sems, {}

    def send(self, role, src, dst, hid):
        copy = remote(src, dst, self.send_sems.at[role], self.recv_sems.at[role], hid)
        copy.start()
        self.sent[role] = copy

    def await_recv(self, role, dst, hid):
        remote(dst, dst, self.send_sems.at[role], self.recv_sems.at[role], hid).wait_recv()

    def drain(self):
        for copy in self.sent.values():
            copy.wait_send()


GATHER_ROLES = 36
OFFS = (0, -1, 1, 2)


class Gather:
    def __init__(self, mail, base, buf, rows, first_row=0, split_columns=False):
        self.mail, self.base, self.buf, self.rows = mail, base, buf, rows
        self.first_row, self.split_columns = first_row, split_columns
        self.a_plus, self.a_minus = moved(1, 0), moved(-1, 0)
        self.b_plus, self.b_minus = moved(0, 1), moved(0, -1)
        self.partner = moved(0, 0, 1)
        self.seen = set()

    def row_slice(self, hid):
        return pl.ds(pl.multiple_of(self.first_row + hid * self.rows, self.rows), self.rows)

    def blk(self, hid, part=None):
        start = pl.multiple_of(self.first_row + hid * self.rows, self.rows)
        if part is None:
            return self.buf.at[self.row_slice(hid)]
        if self.split_columns:
            half = self.buf.shape[1] // 2
            return self.buf.at[self.row_slice(hid), pl.ds(part * half, half)]
        half = self.rows // 2
        return self.buf.at[pl.ds(start + part * half, half)]

    def owner(self, ia, ib, from_partner=False):
        if from_partner:
            return moved(OFFS[ib], OFFS[ia], 1)
        return moved(OFFS[ia], OFFS[ib])

    def forward(self, role, block, to):
        self.mail.send(self.base + role, block, block, to)

    def to_partner(self, ia, ib):
        self.forward(20 + ia * 4 + ib, self.blk(self.owner(ia, ib)), self.partner)

    def from_partner(self, *places):
        for ia, ib in places:
            if (ia, ib) not in self.seen:
                self.seen.add((ia, ib))
                self.mail.await_recv(
                    self.base + 20 + ia * 4 + ib, self.blk(self.owner(ia, ib, True)), self.partner
                )

    def line_out(self, i):
        block = self.blk(self.owner(0, i))
        self.forward(4 + 4 * i, block, self.a_plus)
        self.forward(5 + 4 * i, block, self.a_minus)

    def line_relay(self, i):
        low, high = self.owner(1, i), self.owner(2, i)
        self.mail.await_recv(self.base + 4 + 4 * i, self.blk(low), self.a_minus)
        self.forward(6 + 4 * i, self.blk(low, 0), self.a_plus)
        self.mail.await_recv(self.base + 5 + 4 * i, self.blk(high), self.a_plus)
        self.forward(7 + 4 * i, self.blk(high, 1), self.a_minus)
        self.to_partner(1, i)
        self.to_partner(2, i)

    def line_far(self, i):
        far = self.owner(3, i)
        self.mail.await_recv(self.base + 6 + 4 * i, self.blk(far, 0), self.a_minus)
        self.mail.await_recv(self.base + 7 + 4 * i, self.blk(far, 1), self.a_plus)
        self.to_partner(3, i)

    def stages(self):
        mail, base, blk = self.mail, self.base, self.blk
        own, low, high, far = (self.owner(0, i) for i in range(4))
        self.forward(0, blk(own), self.b_plus)
        self.forward(1, blk(own), self.b_minus)
        self.line_out(0)
        self.to_partner(0, 0)
        yield "start"
        mail.await_recv(base + 0, blk(low), self.b_minus)
        self.forward(2, blk(low, 0), self.b_plus)
        self.line_out(1)
        self.to_partner(0, 1)
        mail.await_recv(base + 1, blk(high), self.b_plus)
        self.forward(3, blk(high, 1), self.b_minus)
        self.line_out(2)
        self.to_partner(0, 2)
        self.line_relay(0)
        yield "relay0"
        mail.await_recv(base + 2, blk(far, 0), self.b_minus)
        mail.await_recv(base + 3, blk(far, 1), self.b_plus)
        self.line_out(3)
        self.to_partner(0, 3)
        self.line_relay(1)
        yield "relay1"
        self.line_relay(2)
        yield "relay2"
        self.line_far(0)
        yield "far0"
        self.line_relay(3)
        yield "relay3"
        self.line_far(1)
        yield "far1"
        self.line_far(2)
        yield "far2"
        self.line_far(3)
        yield "far3"

    def finish(self):
        self.from_partner(*[(ia, ib) for ia in range(4) for ib in range(4)])


PIECES = 2
PART = 16
PIECE_ROLES = 14


class Scatter:
    def __init__(self, mail, base, product, xs, xr, sums, acc, near, mid, last, swap_out, swap_in):
        self.mail, self.base, self.product = mail, base, product
        self.xs, self.xr, self.sums, self.acc = xs, xr, sums, acc
        self.near, self.mid, self.last = near, mid, last
        self.swap_out, self.swap_in = swap_out, swap_in
        self.made = set()
        x, z, c = place()
        self.c = c
        self.a = (1 - c) * z + c * x
        self.b = (1 - c) * x + c * z
        self.partner = moved(0, 0, 1)
        self.a_plus, self.a_minus = moved(1, 0), moved(-1, 0)
        self.b_plus, self.b_minus, self.b_far = moved(0, 1), moved(0, -1), moved(0, 2)
        self.lo, self.hi = pl.ds(0, 4 * PART), pl.ds(4 * PART, 4 * PART)

    def role(self, p, n):
        return self.base + PIECE_ROLES * p + n

    def set_chips(self, k, cc):
        return [(1 - cc) * (j * 4 + k) + cc * (k * 4 + j) for j in range(4)]

    def partner_product(self, p, idx):
        c, step = self.c, (2, 1, 3, 0)[idx]
        if (p, idx) not in self.made:
            self.made.add((p, idx))
            chips = self.set_chips((self.b + step) % 4, 1 - c)
            self.product(chips, 1 - c, p, self.xs.at[p, idx], None)

    def partner_part(self, p, idx):
        self.partner_product(p, idx)
        self.mail.send(self.role(p, idx), self.xs.at[p, idx], self.xr.at[p, idx], self.partner)

    def own_part(self, p, idx, out):
        c, step = self.c, (2, 1, 3, 0)[idx]
        self.mail.await_recv(self.role(p, idx), self.xr.at[p, idx], self.partner)
        self.product(self.set_chips((self.a + step) % 4, c), c, p, out, self.xr.at[p, idx])

    def far_sets(self, p):
        sums, near = self.sums, self.near
        self.partner_part(p, 0)
        self.partner_part(p, 1)
        self.own_part(p, 0, sums.at[p, 0])
        self.mail.send(self.role(p, 4), sums.at[p, 0, self.lo], near.at[p, self.lo], self.a_plus)
        self.mail.send(self.role(p, 5), sums.at[p, 0, self.hi], near.at[p, self.hi], self.a_minus)

    def next_sets(self, p):
        sums, mid = self.sums, self.mid
        self.partner_part(p, 2)
        self.own_part(p, 1, sums.at[p, 1])
        self.mail.send(self.role(p, 6), sums.at[p, 1, self.hi], mid.at[p, 0, self.hi], self.a_plus)
        self.partner_part(p, 3)
        self.own_part(p, 2, sums.at[p, 2])
        self.mail.send(self.role(p, 7), sums.at[p, 2, self.lo], mid.at[p, 1, self.lo], self.a_minus)

    def pass_on(self, p):
        f32, bf16 = jnp.float32, jnp.bfloat16
        sums, near, mid, lo, hi = self.sums, self.near, self.mid, self.lo, self.hi
        self.mail.await_recv(self.role(p, 4), near.at[p, lo], self.a_minus)
        sums[p, 1, lo] = (sums[p, 1, lo].astype(f32) + near[p, lo].astype(f32)).astype(bf16)
        self.mail.send(self.role(p, 8), sums.at[p, 1, lo], mid.at[p, 0, lo], self.a_plus)
        self.mail.await_recv(self.role(p, 5), near.at[p, hi], self.a_plus)
        sums[p, 2, hi] = (sums[p, 2, hi].astype(f32) + near[p, hi].astype(f32)).astype(bf16)
        self.mail.send(self.role(p, 9), sums.at[p, 2, hi], mid.at[p, 1, hi], self.a_minus)

    def own_set(self, p):
        self.own_part(p, 3, self.acc.at[p])

    def chunk(self, j):
        return pl.ds(pl.multiple_of(j * 2 * PART, 2 * PART), 2 * PART)

    def chunk_sum(self, p, j):
        at = self.chunk(j)
        value = self.acc[p, at] + self.mid[p, 0, at].astype(jnp.float32)
        return value + self.mid[p, 1, at].astype(jnp.float32)

    def second(self, p):
        mid, q = self.mid, self.sums
        self.mail.await_recv(self.role(p, 6), mid.at[p, 0, self.hi], self.a_minus)
        self.mail.await_recv(self.role(p, 7), mid.at[p, 1, self.lo], self.a_plus)
        self.mail.await_recv(self.role(p, 8), mid.at[p, 0, self.lo], self.a_minus)
        self.mail.await_recv(self.role(p, 9), mid.at[p, 1, self.hi], self.a_plus)
        for n, (step, to) in enumerate(((2, self.b_far), (1, self.b_plus), (3, self.b_minus))):
            j = (self.b + step) % 4
            q[p, 3, self.chunk(j)] = self.chunk_sum(p, j).astype(jnp.bfloat16)
            self.mail.send(self.role(p, 10 + n), q.at[p, 3, self.chunk(j)], self.last.at[p, n], to)

    def settle(self, p):
        value = self.chunk_sum(p, self.b)
        for n, source in ((1, self.b_minus), (2, self.b_plus), (0, self.b_far)):
            self.mail.await_recv(self.role(p, 10 + n), self.last.at[p, n], source)
        for n in range(3):
            value = value + self.last[p, n].astype(jnp.float32)
        is_first = self.c == 0
        self.swap_out[p] = jnp.where(is_first, value[PART:], value[:PART])
        self.mail.send(self.role(p, 13), self.swap_out.at[p], self.swap_in.at[p], self.partner)
        return jnp.where(is_first, value[:PART], value[PART:])

    def other(self, p):
        self.mail.await_recv(self.role(p, 13), self.swap_in.at[p], self.partner)
        return self.swap_in[p]


TAIL_ROLES = PIECE_ROLES * PIECES * 2 + GATHER_ROLES * PIECES


def tail_kernel(
    heads_ref, w_out_hbm, gain_ref, w_gu_hbm, w_down_hbm, attn_ref, block_ref,
    w_out, w_gu, w_down, load_sems, send_sems, recv_sems, *scratch,
):
    *scatter_refs, ff_buf, hidden = scratch
    x, z, c = place()
    loads = [
        pltpu.make_async_copy(w_out_hbm, w_out, load_sems.at[0]),
        pltpu.make_async_copy(w_gu_hbm, w_gu, load_sems.at[1]),
        pltpu.make_async_copy(w_down_hbm, w_down, load_sems.at[2]),
    ]
    peers = [
        {"hid": moved(1, 0)}, {"hid": moved(-1, 0)}, {"hid": moved(0, 1)},
        {"hid": moved(0, -1)}, {"hid": moved(0, 2)}, {"hid": moved(0, 0, 1)},
    ]
    barrier = pltpu.get_barrier_semaphore()
    for peer in peers:
        pl.semaphore_signal(barrier, inc=1, device_id=peer, device_id_type=MESH)
    for load in loads:
        load.start()
    mail = Mail(send_sems, recv_sems)
    width = w_out.shape[1] // 2
    units = w_down.shape[0]
    count = heads_ref.shape[0] // PIECES

    def product_of(lhs_rows, weight):
        def product(chips, half, p, out, other):
            rows = jnp.concatenate([r for chip in chips for r in lhs_rows(p, chip)], axis=0)
            cols = pl.ds(pl.multiple_of(half * width, 128), width)
            value = jnp.dot(rows, weight[:, cols], preferred_element_type=jnp.float32)
            if other is not None:
                value = value + other[...].astype(jnp.float32)
            out[...] = value.astype(out.dtype)
        return product

    def heads_rows(p, chip):
        return [
            heads_ref[pl.ds(pl.multiple_of(chip * 64 + core * 32 + p * PART, PART), PART), :]
            for core in range(2)
        ]

    def hidden_rows(p, chip):
        return [hidden[pl.ds(pl.multiple_of(p * count + chip * 2 * PART, 2 * PART), 2 * PART), :]]

    outer = Scatter(mail, 0, product_of(heads_rows, w_out), *scatter_refs[:9])
    gathers = [
        Gather(
            mail, PIECE_ROLES * PIECES + GATHER_ROLES * p, ff_buf, PART,
            first_row=p * count, split_columns=True,
        )
        for p in range(PIECES)
    ]
    inner = Scatter(
        mail, PIECE_ROLES * PIECES + GATHER_ROLES * PIECES, product_of(hidden_rows, w_down), *scatter_refs[9:]
    )
    mine_at = pl.ds(pl.multiple_of(c * width, 128), width)
    other_at = pl.ds(pl.multiple_of((1 - c) * width, 128), width)
    gain_mine = gain_ref[mine_at].reshape(1, width)
    gain_other = gain_ref[other_at].reshape(1, width)

    def normalise(p, mine):
        other = outer.other(p)
        rows = pl.ds(p * PART, PART)
        attn_ref[rows, mine_at] = mine.astype(jnp.bfloat16)
        attn_ref[rows, other_at] = other.astype(jnp.bfloat16)
        total = jnp.sum(mine * mine, axis=1, keepdims=True) + jnp.sum(other * other, axis=1, keepdims=True)
        scale = lax.rsqrt(total / (2 * width) + EPS)
        own_rows = gathers[p].row_slice(moved(0, 0))
        ff_buf[own_rows, mine_at] = (mine * scale * gain_mine).astype(jnp.bfloat16)
        ff_buf[own_rows, other_at] = (other * scale * gain_other).astype(jnp.bfloat16)

    def feed(p, part):
        contract = (((1,), (1,)), ((), ()))
        at = pl.ds(p * count + part * (count // 2), count // 2)
        rows = ff_buf[at, :]
        gate = lax.dot_general(rows, w_gu[pl.ds(0, units), :], contract, preferred_element_type=jnp.float32)
        up = lax.dot_general(rows, w_gu[pl.ds(units, units), :], contract, preferred_element_type=jnp.float32)
        hidden[at, :] = (jax.nn.silu(gate) * up).astype(jnp.bfloat16)

    loads[0].wait()
    outer.partner_product(0, 0)
    outer.partner_product(0, 1)
    pl.semaphore_wait(barrier, len(peers))
    outer.far_sets(0)
    outer.next_sets(0)
    outer.pass_on(0)
    outer.far_sets(1)
    outer.next_sets(1)
    outer.own_set(0)
    outer.second(0)
    outer.pass_on(1)
    outer.own_set(1)
    stages = [gather.stages() for gather in gathers]
    normalise(0, outer.settle(0))
    next(stages[0])
    outer.second(1)
    assert next(stages[0]) == "relay0"
    normalise(1, outer.settle(1))
    next(stages[1])
    assert next(stages[0]) == "relay1"
    assert next(stages[1]) == "relay0"
    assert next(stages[0]) == "relay2"
    assert next(stages[1]) == "relay1"
    next(stages[0])
    assert next(stages[0]) == "relay3"
    assert next(stages[1]) == "relay2"
    next(stages[1])
    for name in ("far1", "far2", "far3"):
        assert next(stages[0]) == name
    assert next(stages[1]) == "relay3"
    loads[1].wait()
    gathers[0].finish()
    feed(0, 0)
    for name in ("far1", "far2", "far3"):
        assert next(stages[1]) == name
    feed(0, 1)
    loads[2].wait()
    inner.far_sets(0)
    inner.next_sets(0)
    gathers[1].finish()
    feed(1, 0)
    inner.pass_on(0)
    feed(1, 1)
    inner.far_sets(1)
    inner.next_sets(1)
    inner.own_set(0)
    inner.second(0)
    inner.pass_on(1)
    inner.own_set(1)
    first = inner.settle(0)
    inner.second(1)
    for p, mine in enumerate((first, None)):
        if mine is None:
            mine = inner.settle(p)
        rows = pl.ds(p * PART, PART)
        block_ref[rows, mine_at] = mine.astype(jnp.bfloat16)
        block_ref[rows, other_at] = inner.other(p).astype(jnp.bfloat16)
    mail.drain()


def tail(heads_out, w_out, gain_ff, w_gu, w_down):
    tok_grp = heads_out.shape[0]
    width = w_out.shape[1]
    half = width // 2
    units = w_down.shape[0]
    bf16, f32 = jnp.bfloat16, jnp.float32
    vmem = pl.BlockSpec(memory_space=pltpu.VMEM)
    anywhere = pl.BlockSpec(memory_space=pl.ANY)

    set_rows = 8 * PART

    def scatter_scratch():
        return [
            pltpu.VMEM((PIECES, 4, set_rows, half), bf16), pltpu.VMEM((PIECES, 4, set_rows, half), bf16),
            pltpu.VMEM((PIECES, 4, set_rows, half), bf16), pltpu.VMEM((PIECES, set_rows, half), f32),
            pltpu.VMEM((PIECES, set_rows, half), bf16), pltpu.VMEM((PIECES, 2, set_rows, half), bf16),
            pltpu.VMEM((PIECES, 3, 2 * PART, half), bf16), pltpu.VMEM((PIECES, PART, half), f32),
            pltpu.VMEM((PIECES, PART, half), f32),
        ]

    return pl.pallas_call(
        tail_kernel,
        out_shape=(jax.ShapeDtypeStruct((32, width), bf16), jax.ShapeDtypeStruct((32, width), bf16)),
        in_specs=[vmem, anywhere, vmem, anywhere, anywhere],
        out_specs=(vmem, vmem),
        scratch_shapes=[
            pltpu.VMEM(w_out.shape, bf16), pltpu.VMEM(w_gu.shape, bf16), pltpu.VMEM(w_down.shape, bf16),
            pltpu.SemaphoreType.DMA((3,)), pltpu.SemaphoreType.DMA((TAIL_ROLES,)),
            pltpu.SemaphoreType.DMA((TAIL_ROLES,)),
            *scatter_scratch(), *scatter_scratch(),
            pltpu.VMEM((tok_grp, width), bf16), pltpu.VMEM((tok_grp, units), bf16),
        ],
        compiler_params=pltpu.CompilerParams(
            collective_id=0, has_side_effects=True, vmem_limit_bytes=66000000
        ),
        name="tail",
    )(heads_out, w_out, gain_ff, w_gu, w_down)


CHUNKS = 4
STEP = 8


def deal_order():
    near = [(0, dz, dc) for dc in range(2) for dz in (1, 3, 2)] + [(0, 0, 1)]
    order = []
    for n in range(8):
        order += [(dx, n % 4, n // 4) for dx in (1, 3, 2)] + near[n:n + 1]
    return order


def at_offset(dx, dz, dc, sign=1):
    x, z, c = place()
    return ((x + 4 + sign * dx) % 4) * 8 + ((z + 4 + sign * dz) % 4) * 2 + (c + dc) % 2
WINDOW = 768


def front_kernel(
    slot_ref, choice_ref, lengths_ref, tokens_ref, gain_ref, down_hbm, up_ref, w_hbm, cache_hbm, heads_ref,
    w_qkv, w_latent, rows_buf, latents_buf, load_sems, send_sems, recv_sems,
    prefix, qkv, top, denom, total, *chunked,
):
    x, z, c = place()
    hid = lax.axis_index("hid")
    req = lax.axis_index("req")
    lower, upper = (req + 3) % 4, (req + 1) % 4
    width = tokens_ref.shape[1]
    bf16, f32 = jnp.bfloat16, jnp.float32
    first, second, passed, split = (chunked[n * CHUNKS:(n + 1) * CHUNKS] for n in range(4))

    def owner(group):
        return slot_ref[choice_ref[group]]

    peers = [{"hid": (hid + d) % 32} for d in range(1, 32)] + [{"req": lower}, {"req": upper}]
    barrier = pltpu.get_barrier_semaphore()
    for peer in peers:
        pl.semaphore_signal(barrier, inc=1, device_id=peer, device_id_type=MESH)
    latent_load = pltpu.make_async_copy(down_hbm, w_latent, load_sems.at[1])
    latent_load.start()
    def part_of(half, k):
        return cache_hbm.at[pl.ds(half * STEP * CHUNKS + k * STEP, STEP)]

    loads = []
    for k in range(CHUNKS):
        for half in range(2):
            copy = pltpu.make_async_copy(part_of(half, k), first[k].at[half], load_sems.at[2 + 2 * k + half])
            copy.start()
            loads.append(copy)
    w_load = pltpu.make_async_copy(w_hbm, w_qkv, load_sems.at[0])
    w_load.start()

    matrix = tokens_ref[...].astype(f32)
    normed = rms_scale(matrix, gain_ref[...].reshape(1, width)).astype(bf16)
    own_rows = pl.ds(pl.multiple_of(hid * 32, 32), 32)
    rows_buf[own_rows, :] = normed
    pl.semaphore_wait(barrier, len(peers))

    mail = Mail(send_sems, recv_sems)
    y_base = GATHER_ROLES
    deal_base = y_base + 4 * CHUNKS
    deal_rows = 2 * STEP

    def y_copy(role, src, dst, to):
        return pltpu.make_async_remote_copy(
            src_ref=src, dst_ref=dst, send_sem=send_sems.at[role], recv_sem=recv_sems.at[role],
            device_id={"req": to}, device_id_type=MESH,
        )

    def y_send(role, src, dst, to):
        copy = y_copy(role, src, dst, to)
        copy.start()
        mail.sent[role] = copy

    def y_start():
        for k in range(CHUNKS):
            y_send(y_base + k, part_of(0, k), first[k].at[2], lower)
            y_send(y_base + CHUNKS + k, part_of(1, k), first[k].at[3], upper)

    def y_pass(k):
        loads[2 * k].wait()
        loads[2 * k + 1].wait()
        y_copy(y_base + k, first[k].at[2], first[k].at[2], upper).wait_recv()
        y_copy(y_base + CHUNKS + k, first[k].at[3], first[k].at[3], lower).wait_recv()
        passed[k][0] = first[k][jnp.where(owner(lower) == req, 1, 2)]
        y_send(y_base + 2 * CHUNKS + k, passed[k].at[0], second[k].at[0], lower)
        passed[k][1] = first[k][jnp.where(owner(upper) == req, 0, 3)]
        y_send(y_base + 3 * CHUNKS + k, passed[k].at[1], second[k].at[1], upper)

    def deal(k):
        y_copy(y_base + 2 * CHUNKS + k, second[k].at[0], second[k].at[0], upper).wait_recv()
        y_copy(y_base + 3 * CHUNKS + k, second[k].at[1], second[k].at[1], lower).wait_recv()
        away = (owner(req) - req + 4) % 4
        late_a = jnp.full((1, 1, 1), (away >= 2).astype(jnp.int32)) > 0
        late_b = jnp.full((1, 1, 1), jnp.logical_or(away == 1, away == 2).astype(jnp.int32)) > 0
        half_a = jnp.where(late_a, second[k][jnp.where(away == 2, 0, 1)], first[k][jnp.where(away == 0, 0, 2)])
        half_b = jnp.where(late_b, second[k][jnp.where(away == 1, 0, 1)], first[k][jnp.where(away == 0, 1, 3)])
        r = lax.broadcasted_iota(jnp.int32, (32, 32), 0)
        s = lax.broadcasted_iota(jnp.int32, (32, 32), 1)
        sort = (s == jnp.where(r < 16, 2 * r, 2 * r - 31)).astype(bf16)
        zeros = jnp.zeros((deal_rows, 256 - HD), bf16)
        value = jnp.concatenate([half_a.reshape(2 * STEP, width), half_b.reshape(2 * STEP, width)], axis=0)
        planes = jnp.dot(sort, value, preferred_element_type=f32).astype(bf16)
        for kv in range(2):
            for h in range(32):
                piece = planes[kv * deal_rows:(kv + 1) * deal_rows, h * HD:(h + 1) * HD]
                split[k][h, kv] = jnp.concatenate([piece, zeros], axis=1)

        for n, offset in enumerate(deal_order()):
            to = at_offset(*offset)
            mail.send(deal_base + k * 31 + n, split[k].at[to], landing(k, hid), to)
        prefix[:, pl.ds(pl.multiple_of(k * 512 + hid * deal_rows, deal_rows), deal_rows)] = split[k][hid]

    def landing(k, source):
        start = pl.multiple_of(k * 512 + source * deal_rows, deal_rows)
        return prefix.at[:, pl.ds(start, deal_rows)]

    def dealt(k):
        for n, offset in enumerate(deal_order()):
            source = at_offset(*offset, sign=-1)
            mail.await_recv(deal_base + k * 31 + n, landing(k, source), source)

    y_start()
    gather = Gather(mail, 0, rows_buf, 32)
    latent_base = deal_base + 31 * CHUNKS

    def latent_rows(device):
        return latents_buf.at[pl.ds(pl.multiple_of(device * 32, 32), 32)]

    def send_latents():
        latent_load.wait()
        latent = jnp.dot(normed, w_latent[...], preferred_element_type=f32)
        latents_buf[own_rows, :] = latent.astype(bf16)
        for n, offset in enumerate(deal_order()):
            mail.send(latent_base + n, latent_rows(hid), latent_rows(hid), at_offset(*offset))

    def await_latents():
        for n, offset in enumerate(deal_order()):
            source = at_offset(*offset, sign=-1)
            mail.await_recv(latent_base + n, latent_rows(source), source)

    contract = (((1,), (1,)), ((), ()))

    def project(own, partners):
        gather.from_partner(*partners)
        places = [gather.owner(*at) for at in own] + [gather.owner(*at, True) for at in partners]
        slices = [pl.ds(pl.multiple_of(place * 32, 32), 32) for place in places]
        rows = jnp.concatenate([rows_buf[at, :] for at in slices], axis=0)
        latents = jnp.concatenate([latents_buf[at, :] for at in slices], axis=0)
        pad = jnp.zeros((rows.shape[0], 256 - HD), bf16)

        def keep(part, value):
            value = jnp.concatenate([value.astype(bf16), pad], axis=1)
            for n, at in enumerate(slices):
                qkv[part, at, :] = value[n * 32:(n + 1) * 32]

        value = lax.dot_general(rows, w_qkv[pl.ds(0, HD), :], contract, preferred_element_type=f32)
        keep(0, value + lax.dot_general(latents, up_ref[...], contract, preferred_element_type=f32))

        @pl.loop(1, 3)
        def _(part):
            weight = w_qkv[pl.ds(pl.multiple_of(part * HD, 32), HD), :]
            keep(part, lax.dot_general(rows, weight, contract, preferred_element_type=f32))

    for stage in gather.stages():
        if stage == "start":
            send_latents()
        if stage == "relay0":
            y_pass(0)
            y_pass(1)
        if stage == "relay2":
            w_load.wait()
            await_latents()
            project([(0, 0), (0, 1), (0, 2), (1, 0), (2, 0)], [(0, 0), (0, 1), (0, 2)])
            y_pass(2)
            y_pass(3)
        if stage == "relay3":
            project([(1, 1), (2, 1), (1, 2), (2, 2), (0, 3), (3, 0)], [(1, 0), (2, 0)])
            deal(0)
        if stage == "far1":
            deal(1)
        if stage == "far3":
            deal(2)
            deal(3)
            project([(1, 3), (2, 3)], [(0, 3), (1, 1), (2, 1), (1, 2), (2, 2), (3, 0)])
    project([(3, 1), (3, 2), (3, 3)], [(1, 3), (2, 3), (3, 1), (3, 2), (3, 3)])

    dealt(0)
    dealt(1)

    ends = [lengths_ref[0, 0]]
    for n in range(1, lengths_ref.shape[1]):
        ends.append(ends[-1] + lengths_ref[0, n])
    factor = HD ** (-0.5)

    @pl.loop(0, 8)
    def _(i):
        at = pl.ds(pl.multiple_of(i * 128, 128), 128)
        begin = jnp.minimum(jnp.maximum(i * 128 - 512, 0), 1024 - WINDOW)
        near = pl.ds(pl.multiple_of(begin, 128), WINDOW)
        q = qkv[0, at, :]
        s_far = lax.dot_general(q, prefix[0, pl.ds(0, 1024), :], contract, preferred_element_type=f32) * factor
        s_near = lax.dot_general(q, qkv[1, near, :], contract, preferred_element_type=f32) * factor
        row = lax.broadcasted_iota(jnp.int32, (128, 1), 0) + i * 128
        since = jnp.zeros((128, 1), jnp.int32)
        for end in ends:
            since = jnp.where(row >= end, jnp.maximum(since, end), since)
        col = lax.broadcasted_iota(jnp.int32, (128, WINDOW), 1) + begin
        s_near = jnp.where(jnp.logical_and(col >= since, col <= row), s_near, -jnp.inf)
        row_max = jnp.maximum(
            jnp.max(s_far, axis=1, keepdims=True), jnp.max(s_near, axis=1, keepdims=True)
        )
        e_far = jnp.exp(s_far - row_max)
        e_near = jnp.exp(s_near - row_max)
        top[at, :] = row_max
        denom[at, :] = jnp.sum(e_far, axis=1, keepdims=True) + jnp.sum(e_near, axis=1, keepdims=True)
        out = jnp.dot(e_far.astype(bf16), prefix[1, pl.ds(0, 1024), :], preferred_element_type=f32)
        total[at, :] = out + jnp.dot(e_near.astype(bf16), qkv[2, near, :], preferred_element_type=f32)

    for k in (2, 3):
        dealt(k)
        more = pl.ds(k * 512, 512)

        @pl.loop(0, 4)
        def _(i):
            at = pl.ds(pl.multiple_of(i * 256, 256), 256)
            scores = lax.dot_general(
                qkv[0, at, :], prefix[0, more, :], contract, preferred_element_type=f32
            ) * factor
            row_max = jnp.maximum(top[at, :], jnp.max(scores, axis=1, keepdims=True))
            keep = jnp.exp(top[at, :] - row_max)
            expos = jnp.exp(scores - row_max)
            row_sum = denom[at, :] * keep + jnp.sum(expos, axis=1, keepdims=True)
            out = total[at, :] * keep + jnp.dot(
                expos.astype(bf16), prefix[1, more, :], preferred_element_type=f32
            )
            if k == 2:
                top[at, :] = row_max
                denom[at, :] = row_sum
                total[at, :] = out
            else:
                heads_ref[at, :] = (out / row_sum)[:, :HD].astype(bf16)

    mail.drain()


def front(slots, choices, lengths, tokens, gain_in, adapt_down, up_t, w_t, cache):
    rows, width = tokens.shape
    tok_grp = rows * 32
    bf16 = jnp.bfloat16
    smem = pl.BlockSpec(memory_space=pltpu.SMEM)
    vmem = pl.BlockSpec(memory_space=pltpu.VMEM)
    anywhere = pl.BlockSpec(memory_space=pl.ANY)
    roles = GATHER_ROLES + 4 * CHUNKS + 31 * (CHUNKS + 1)

    def halves(count):
        return [pltpu.VMEM((count, STEP, 2, width), bf16)] * CHUNKS

    return pl.pallas_call(
        front_kernel,
        out_shape=jax.ShapeDtypeStruct((tok_grp, HD), bf16),
        in_specs=[smem, smem, smem, vmem, vmem, anywhere, vmem, anywhere, anywhere],
        out_specs=vmem,
        scratch_shapes=[
            pltpu.VMEM(w_t.shape, bf16), pltpu.VMEM(adapt_down.shape, bf16),
            pltpu.VMEM((tok_grp, width), bf16), pltpu.VMEM((tok_grp, 128), bf16),
            pltpu.SemaphoreType.DMA((2 + 2 * CHUNKS,)), pltpu.SemaphoreType.DMA((roles,)),
            pltpu.SemaphoreType.DMA((roles,)),
            pltpu.VMEM((2, 2048, 256), bf16), pltpu.VMEM((3, tok_grp, 256), bf16),
            pltpu.VMEM((tok_grp, 1), jnp.float32), pltpu.VMEM((tok_grp, 1), jnp.float32),
            pltpu.VMEM((tok_grp, 256), jnp.float32),
            *halves(4), *halves(2), *halves(2),
            *([pltpu.VMEM((32, 2, 2 * STEP, 256), bf16)] * CHUNKS),
        ],
        compiler_params=pltpu.CompilerParams(
            collective_id=1, has_side_effects=True, vmem_limit_bytes=66000000
        ),
        name="front",
    )(slots, choices, lengths, tokens, gain_in, adapt_down, up_t, w_t, cache)


def settle_kernel(attn_ref, block_ref, attn_out, block_out):
    attn_out[...] = attn_ref[...]
    block_out[...] = block_ref[...]


def settle(attn, block):
    vmem = pl.BlockSpec(memory_space=pltpu.VMEM)
    return pl.pallas_call(
        settle_kernel,
        out_shape=(jax.ShapeDtypeStruct(attn.shape, attn.dtype), jax.ShapeDtypeStruct(block.shape, block.dtype)),
        in_specs=[vmem, vmem],
        out_specs=(vmem, vmem),
        name="settle",
    )(attn, block)


def per_device(
    tokens,
    gain_in,
    w_qkv,
    adapt_down,
    adapt_up,
    w_out,
    gain_ff,
    w_gate_up,
    w_down,
    prefix_cache,
    prefix_owner,
    group_prefix,
    lengths,
):
    w_t = jnp.transpose(w_qkv, (1, 2, 0)).reshape(3 * w_qkv.shape[2], w_qkv.shape[0])
    w_gu = jnp.transpose(w_gate_up, (1, 2, 0)).reshape(2 * w_gate_up.shape[2], w_gate_up.shape[0])
    heads_out = front(
        prefix_owner, group_prefix, lengths, tokens, gain_in, adapt_down, adapt_up.T, w_t, prefix_cache[0]
    )
    return settle(*tail(heads_out, w_out, gain_ff, w_gu, w_down))


def solution(mesh):
    placed = (
        P(("req", "hid"), None),
        P(),
        P(None, None, "hid"),
        P(),
        P(None, "hid"),
        P("hid", None),
        P(),
        P(None, None, "hid"),
        P("hid", None),
        P("req", "hid", None, None),
        P(),
        P(),
        P("req", None),
    )
    return jax.shard_map(
        per_device,
        mesh=mesh,
        in_specs=placed,
        out_specs=(P(("req", "hid"), None), P(("req", "hid"), None)),
        check_vma=False,
    )
```

```python
import jax
import jax.numpy as jnp
from jax import lax
from jax.experimental import pallas as pl
from jax.experimental.pallas import tpu as pltpu
from jax.sharding import PartitionSpec as P

HD = 224


EPS = 1e-05


def rms_scale(matrix, gain_vec):
    return matrix * lax.rsqrt(jnp.mean(matrix * matrix, axis=-1, keepdims=True) + EPS) * gain_vec


MESH = pl.DeviceIdType.MESH
NX, NZ = 4, 4


def place():
    hid = lax.axis_index("hid")
    return hid // 8, (hid // 2) % 4, hid % 2


def moved(da, db, core_flip=0):
    x, z, c = place()
    xn = (x + 4 + (1 - c) * db + c * da) % 4
    zn = (z + 4 + (1 - c) * da + c * db) % 4
    cn = c + core_flip * (1 - 2 * c)
    return xn * 8 + zn * 2 + cn


def remote(src, dst, send, recv, hid):
    return pltpu.make_async_remote_copy(
        src_ref=src, dst_ref=dst, send_sem=send, recv_sem=recv,
        device_id={"hid": hid}, device_id_type=MESH,
    )


class Mail:
    def __init__(self, send_sems, recv_sems):
        self.send_sems, self.recv_sems, self.sent = send_sems, recv_sems, {}

    def send(self, role, src, dst, hid):
        copy = remote(src, dst, self.send_sems.at[role], self.recv_sems.at[role], hid)
        copy.start()
        self.sent[role] = copy

    def await_recv(self, role, dst, hid):
        remote(dst, dst, self.send_sems.at[role], self.recv_sems.at[role], hid).wait_recv()

    def drain(self):
        for copy in self.sent.values():
            copy.wait_send()


GATHER_ROLES = 36
OFFS = (0, -1, 1, 2)


class Gather:
    def __init__(self, mail, base, buf, rows, first_row=0, split_columns=False):
        self.mail, self.base, self.buf, self.rows = mail, base, buf, rows
        self.first_row, self.split_columns = first_row, split_columns
        self.a_plus, self.a_minus = moved(1, 0), moved(-1, 0)
        self.b_plus, self.b_minus = moved(0, 1), moved(0, -1)
        self.partner = moved(0, 0, 1)
        self.seen = set()

    def row_slice(self, hid):
        return pl.ds(pl.multiple_of(self.first_row + hid * self.rows, self.rows), self.rows)

    def blk(self, hid, part=None):
        start = pl.multiple_of(self.first_row + hid * self.rows, self.rows)
        if part is None:
            return self.buf.at[self.row_slice(hid)]
        if self.split_columns:
            half = self.buf.shape[1] // 2
            return self.buf.at[self.row_slice(hid), pl.ds(part * half, half)]
        half = self.rows // 2
        return self.buf.at[pl.ds(start + part * half, half)]

    def owner(self, ia, ib, from_partner=False):
        if from_partner:
            return moved(OFFS[ib], OFFS[ia], 1)
        return moved(OFFS[ia], OFFS[ib])

    def forward(self, role, block, to):
        self.mail.send(self.base + role, block, block, to)

    def to_partner(self, ia, ib):
        self.forward(20 + ia * 4 + ib, self.blk(self.owner(ia, ib)), self.partner)

    def from_partner(self, *places):
        for ia, ib in places:
            if (ia, ib) not in self.seen:
                self.seen.add((ia, ib))
                self.mail.await_recv(
                    self.base + 20 + ia * 4 + ib, self.blk(self.owner(ia, ib, True)), self.partner
                )

    def line_out(self, i):
        block = self.blk(self.owner(0, i))
        self.forward(4 + 4 * i, block, self.a_plus)
        self.forward(5 + 4 * i, block, self.a_minus)

    def line_relay(self, i):
        low, high = self.owner(1, i), self.owner(2, i)
        self.mail.await_recv(self.base + 4 + 4 * i, self.blk(low), self.a_minus)
        self.forward(6 + 4 * i, self.blk(low, 0), self.a_plus)
        self.mail.await_recv(self.base + 5 + 4 * i, self.blk(high), self.a_plus)
        self.forward(7 + 4 * i, self.blk(high, 1), self.a_minus)
        self.to_partner(1, i)
        self.to_partner(2, i)

    def line_far(self, i):
        far = self.owner(3, i)
        self.mail.await_recv(self.base + 6 + 4 * i, self.blk(far, 0), self.a_minus)
        self.mail.await_recv(self.base + 7 + 4 * i, self.blk(far, 1), self.a_plus)
        self.to_partner(3, i)

    def stages(self):
        mail, base, blk = self.mail, self.base, self.blk
        own, low, high, far = (self.owner(0, i) for i in range(4))
        self.forward(0, blk(own), self.b_plus)
        self.forward(1, blk(own), self.b_minus)
        self.line_out(0)
        self.to_partner(0, 0)
        yield "start"
        mail.await_recv(base + 0, blk(low), self.b_minus)
        self.forward(2, blk(low, 0), self.b_plus)
        self.line_out(1)
        self.to_partner(0, 1)
        mail.await_recv(base + 1, blk(high), self.b_plus)
        self.forward(3, blk(high, 1), self.b_minus)
        self.line_out(2)
        self.to_partner(0, 2)
        self.line_relay(0)
        yield "relay0"
        mail.await_recv(base + 2, blk(far, 0), self.b_minus)
        mail.await_recv(base + 3, blk(far, 1), self.b_plus)
        self.line_out(3)
        self.to_partner(0, 3)
        self.line_relay(1)
        yield "relay1"
        self.line_relay(2)
        yield "relay2"
        self.line_far(0)
        yield "far0"
        self.line_relay(3)
        yield "relay3"
        self.line_far(1)
        yield "far1"
        self.line_far(2)
        yield "far2"
        self.line_far(3)
        yield "far3"

    def finish(self):
        self.from_partner(*[(ia, ib) for ia in range(4) for ib in range(4)])


PIECES = 2
PART = 16
PIECE_ROLES = 14


class Scatter:
    def __init__(self, mail, base, product, xs, xr, sums, acc, near, mid, last, swap_out, swap_in):
        self.mail, self.base, self.product = mail, base, product
        self.xs, self.xr, self.sums, self.acc = xs, xr, sums, acc
        self.near, self.mid, self.last = near, mid, last
        self.swap_out, self.swap_in = swap_out, swap_in
        self.made = set()
        x, z, c = place()
        self.c = c
        self.a = (1 - c) * z + c * x
        self.b = (1 - c) * x + c * z
        self.partner = moved(0, 0, 1)
        self.a_plus, self.a_minus = moved(1, 0), moved(-1, 0)
        self.b_plus, self.b_minus, self.b_far = moved(0, 1), moved(0, -1), moved(0, 2)
        self.lo, self.hi = pl.ds(0, 4 * PART), pl.ds(4 * PART, 4 * PART)

    def role(self, p, n):
        return self.base + PIECE_ROLES * p + n

    def set_chips(self, k, cc):
        return [(1 - cc) * (j * 4 + k) + cc * (k * 4 + j) for j in range(4)]

    def partner_product(self, p, idx):
        c, step = self.c, (2, 1, 3, 0)[idx]
        if (p, idx) not in self.made:
            self.made.add((p, idx))
            chips = self.set_chips((self.b + step) % 4, 1 - c)
            self.product(chips, 1 - c, p, self.xs.at[p, idx], None)

    def partner_part(self, p, idx):
        self.partner_product(p, idx)
        self.mail.send(self.role(p, idx), self.xs.at[p, idx], self.xr.at[p, idx], self.partner)

    def own_part(self, p, idx, out):
        c, step = self.c, (2, 1, 3, 0)[idx]
        self.mail.await_recv(self.role(p, idx), self.xr.at[p, idx], self.partner)
        self.product(self.set_chips((self.a + step) % 4, c), c, p, out, self.xr.at[p, idx])

    def far_sets(self, p):
        sums, near = self.sums, self.near
        self.partner_part(p, 0)
        self.partner_part(p, 1)
        self.own_part(p, 0, sums.at[p, 0])
        self.mail.send(self.role(p, 4), sums.at[p, 0, self.lo], near.at[p, self.lo], self.a_plus)
        self.mail.send(self.role(p, 5), sums.at[p, 0, self.hi], near.at[p, self.hi], self.a_minus)

    def next_sets(self, p):
        sums, mid = self.sums, self.mid
        self.partner_part(p, 2)
        self.own_part(p, 1, sums.at[p, 1])
        self.mail.send(self.role(p, 6), sums.at[p, 1, self.hi], mid.at[p, 0, self.hi], self.a_plus)
        self.partner_part(p, 3)
        self.own_part(p, 2, sums.at[p, 2])
        self.mail.send(self.role(p, 7), sums.at[p, 2, self.lo], mid.at[p, 1, self.lo], self.a_minus)

    def pass_on(self, p):
        f32, bf16 = jnp.float32, jnp.bfloat16
        sums, near, mid, lo, hi = self.sums, self.near, self.mid, self.lo, self.hi
        self.mail.await_recv(self.role(p, 4), near.at[p, lo], self.a_minus)
        sums[p, 1, lo] = (sums[p, 1, lo].astype(f32) + near[p, lo].astype(f32)).astype(bf16)
        self.mail.send(self.role(p, 8), sums.at[p, 1, lo], mid.at[p, 0, lo], self.a_plus)
        self.mail.await_recv(self.role(p, 5), near.at[p, hi], self.a_plus)
        sums[p, 2, hi] = (sums[p, 2, hi].astype(f32) + near[p, hi].astype(f32)).astype(bf16)
        self.mail.send(self.role(p, 9), sums.at[p, 2, hi], mid.at[p, 1, hi], self.a_minus)

    def own_set(self, p):
        self.own_part(p, 3, self.acc.at[p])

    def chunk(self, j):
        return pl.ds(pl.multiple_of(j * 2 * PART, 2 * PART), 2 * PART)

    def chunk_sum(self, p, j):
        at = self.chunk(j)
        value = self.acc[p, at] + self.mid[p, 0, at].astype(jnp.float32)
        return value + self.mid[p, 1, at].astype(jnp.float32)

    def second(self, p):
        mid, q = self.mid, self.sums
        self.mail.await_recv(self.role(p, 6), mid.at[p, 0, self.hi], self.a_minus)
        self.mail.await_recv(self.role(p, 7), mid.at[p, 1, self.lo], self.a_plus)
        self.mail.await_recv(self.role(p, 8), mid.at[p, 0, self.lo], self.a_minus)
        self.mail.await_recv(self.role(p, 9), mid.at[p, 1, self.hi], self.a_plus)
        for n, (step, to) in enumerate(((2, self.b_far), (1, self.b_plus), (3, self.b_minus))):
            j = (self.b + step) % 4
            q[p, 3, self.chunk(j)] = self.chunk_sum(p, j).astype(jnp.bfloat16)
            self.mail.send(self.role(p, 10 + n), q.at[p, 3, self.chunk(j)], self.last.at[p, n], to)

    def settle(self, p):
        value = self.chunk_sum(p, self.b)
        for n, source in ((1, self.b_minus), (2, self.b_plus), (0, self.b_far)):
            self.mail.await_recv(self.role(p, 10 + n), self.last.at[p, n], source)
        for n in range(3):
            value = value + self.last[p, n].astype(jnp.float32)
        is_first = self.c == 0
        self.swap_out[p] = jnp.where(is_first, value[PART:], value[:PART])
        self.mail.send(self.role(p, 13), self.swap_out.at[p], self.swap_in.at[p], self.partner)
        return jnp.where(is_first, value[:PART], value[PART:])

    def other(self, p):
        self.mail.await_recv(self.role(p, 13), self.swap_in.at[p], self.partner)
        return self.swap_in[p]


TAIL_ROLES = PIECE_ROLES * PIECES * 2 + GATHER_ROLES * PIECES


def tail_kernel(
    heads_ref, w_out_hbm, gain_ref, w_gu_hbm, w_down_hbm, attn_ref, block_ref,
    w_out, w_gu, w_down, load_sems, send_sems, recv_sems, *scratch,
):
    *scatter_refs, ff_buf, hidden = scratch
    x, z, c = place()
    loads = [
        pltpu.make_async_copy(w_out_hbm, w_out, load_sems.at[0]),
        pltpu.make_async_copy(w_gu_hbm, w_gu, load_sems.at[1]),
        pltpu.make_async_copy(w_down_hbm, w_down, load_sems.at[2]),
    ]
    peers = [
        {"hid": moved(1, 0)}, {"hid": moved(-1, 0)}, {"hid": moved(0, 1)},
        {"hid": moved(0, -1)}, {"hid": moved(0, 2)}, {"hid": moved(0, 0, 1)},
    ]
    barrier = pltpu.get_barrier_semaphore()
    for peer in peers:
        pl.semaphore_signal(barrier, inc=1, device_id=peer, device_id_type=MESH)
    for load in loads:
        load.start()
    mail = Mail(send_sems, recv_sems)
    width = w_out.shape[1] // 2
    units = w_down.shape[0]
    count = heads_ref.shape[0] // PIECES

    def product_of(lhs_rows, weight):
        def product(chips, half, p, out, other):
            rows = jnp.concatenate([r for chip in chips for r in lhs_rows(p, chip)], axis=0)
            cols = pl.ds(pl.multiple_of(half * width, 128), width)
            value = jnp.dot(rows, weight[:, cols], preferred_element_type=jnp.float32)
            if other is not None:
                value = value + other[...].astype(jnp.float32)
            out[...] = value.astype(out.dtype)
        return product

    def heads_rows(p, chip):
        return [
            heads_ref[pl.ds(pl.multiple_of(chip * 64 + core * 32 + p * PART, PART), PART), :]
            for core in range(2)
        ]

    def hidden_rows(p, chip):
        return [hidden[pl.ds(pl.multiple_of(p * count + chip * 2 * PART, 2 * PART), 2 * PART), :]]

    outer = Scatter(mail, 0, product_of(heads_rows, w_out), *scatter_refs[:9])
    gathers = [
        Gather(
            mail, PIECE_ROLES * PIECES + GATHER_ROLES * p, ff_buf, PART,
            first_row=p * count, split_columns=True,
        )
        for p in range(PIECES)
    ]
    inner = Scatter(
        mail, PIECE_ROLES * PIECES + GATHER_ROLES * PIECES, product_of(hidden_rows, w_down), *scatter_refs[9:]
    )
    mine_at = pl.ds(pl.multiple_of(c * width, 128), width)
    other_at = pl.ds(pl.multiple_of((1 - c) * width, 128), width)
    gain_mine = gain_ref[mine_at].reshape(1, width)
    gain_other = gain_ref[other_at].reshape(1, width)

    def normalise(p, mine):
        other = outer.other(p)
        rows = pl.ds(p * PART, PART)
        attn_ref[rows, mine_at] = mine.astype(jnp.bfloat16)
        attn_ref[rows, other_at] = other.astype(jnp.bfloat16)
        total = jnp.sum(mine * mine, axis=1, keepdims=True) + jnp.sum(other * other, axis=1, keepdims=True)
        scale = lax.rsqrt(total / (2 * width) + EPS)
        own_rows = gathers[p].row_slice(moved(0, 0))
        ff_buf[own_rows, mine_at] = (mine * scale * gain_mine).astype(jnp.bfloat16)
        ff_buf[own_rows, other_at] = (other * scale * gain_other).astype(jnp.bfloat16)

    def feed(p, part):
        contract = (((1,), (1,)), ((), ()))
        at = pl.ds(p * count + part * (count // 2), count // 2)
        rows = ff_buf[at, :]
        gate = lax.dot_general(rows, w_gu[pl.ds(0, units), :], contract, preferred_element_type=jnp.float32)
        up = lax.dot_general(rows, w_gu[pl.ds(units, units), :], contract, preferred_element_type=jnp.float32)
        hidden[at, :] = (jax.nn.silu(gate) * up).astype(jnp.bfloat16)

    loads[0].wait()
    outer.partner_product(0, 0)
    outer.partner_product(0, 1)
    pl.semaphore_wait(barrier, len(peers))
    outer.far_sets(0)
    outer.next_sets(0)
    outer.pass_on(0)
    outer.far_sets(1)
    outer.next_sets(1)
    outer.own_set(0)
    outer.second(0)
    outer.pass_on(1)
    outer.own_set(1)
    stages = [gather.stages() for gather in gathers]
    normalise(0, outer.settle(0))
    next(stages[0])
    outer.second(1)
    assert next(stages[0]) == "relay0"
    normalise(1, outer.settle(1))
    next(stages[1])
    assert next(stages[0]) == "relay1"
    assert next(stages[1]) == "relay0"
    assert next(stages[0]) == "relay2"
    assert next(stages[1]) == "relay1"
    next(stages[0])
    assert next(stages[0]) == "relay3"
    assert next(stages[1]) == "relay2"
    next(stages[1])
    for name in ("far1", "far2", "far3"):
        assert next(stages[0]) == name
    assert next(stages[1]) == "relay3"
    loads[1].wait()
    gathers[0].finish()
    feed(0, 0)
    for name in ("far1", "far2", "far3"):
        assert next(stages[1]) == name
    feed(0, 1)
    loads[2].wait()
    inner.far_sets(0)
    inner.next_sets(0)
    gathers[1].finish()
    feed(1, 0)
    inner.pass_on(0)
    feed(1, 1)
    inner.far_sets(1)
    inner.next_sets(1)
    inner.own_set(0)
    inner.second(0)
    inner.pass_on(1)
    inner.own_set(1)
    first = inner.settle(0)
    inner.second(1)
    for p, mine in enumerate((first, None)):
        if mine is None:
            mine = inner.settle(p)
        rows = pl.ds(p * PART, PART)
        block_ref[rows, mine_at] = mine.astype(jnp.bfloat16)
        block_ref[rows, other_at] = inner.other(p).astype(jnp.bfloat16)
    mail.drain()


def tail(heads_out, w_out, gain_ff, w_gu, w_down):
    tok_grp = heads_out.shape[0]
    width = w_out.shape[1]
    half = width // 2
    units = w_down.shape[0]
    bf16, f32 = jnp.bfloat16, jnp.float32
    vmem = pl.BlockSpec(memory_space=pltpu.VMEM)
    anywhere = pl.BlockSpec(memory_space=pl.ANY)

    set_rows = 8 * PART

    def scatter_scratch():
        return [
            pltpu.VMEM((PIECES, 4, set_rows, half), bf16), pltpu.VMEM((PIECES, 4, set_rows, half), bf16),
            pltpu.VMEM((PIECES, 4, set_rows, half), bf16), pltpu.VMEM((PIECES, set_rows, half), f32),
            pltpu.VMEM((PIECES, set_rows, half), bf16), pltpu.VMEM((PIECES, 2, set_rows, half), bf16),
            pltpu.VMEM((PIECES, 3, 2 * PART, half), bf16), pltpu.VMEM((PIECES, PART, half), f32),
            pltpu.VMEM((PIECES, PART, half), f32),
        ]

    return pl.pallas_call(
        tail_kernel,
        out_shape=(jax.ShapeDtypeStruct((32, width), bf16), jax.ShapeDtypeStruct((32, width), bf16)),
        in_specs=[vmem, anywhere, vmem, anywhere, anywhere],
        out_specs=(vmem, vmem),
        scratch_shapes=[
            pltpu.VMEM(w_out.shape, bf16), pltpu.VMEM(w_gu.shape, bf16), pltpu.VMEM(w_down.shape, bf16),
            pltpu.SemaphoreType.DMA((3,)), pltpu.SemaphoreType.DMA((TAIL_ROLES,)),
            pltpu.SemaphoreType.DMA((TAIL_ROLES,)),
            *scatter_scratch(), *scatter_scratch(),
            pltpu.VMEM((tok_grp, width), bf16), pltpu.VMEM((tok_grp, units), bf16),
        ],
        compiler_params=pltpu.CompilerParams(
            collective_id=0, has_side_effects=True, vmem_limit_bytes=66000000
        ),
        name="tail",
    )(heads_out, w_out, gain_ff, w_gu, w_down)


CHUNKS = 4
STEP = 8


def deal_order():
    near = [(0, dz, dc) for dc in range(2) for dz in (1, 3, 2)] + [(0, 0, 1)]
    order = []
    for n in range(8):
        order += [(dx, n % 4, n // 4) for dx in (1, 3, 2)] + near[n:n + 1]
    return order


def at_offset(dx, dz, dc, sign=1):
    x, z, c = place()
    return ((x + 4 + sign * dx) % 4) * 8 + ((z + 4 + sign * dz) % 4) * 2 + (c + dc) % 2
WINDOW = 768


def front_kernel(
    slot_ref, choice_ref, lengths_ref, tokens_ref, gain_ref, down_hbm, up_ref, w_hbm, cache_hbm, heads_ref,
    w_qkv, w_latent, rows_buf, latents_buf, load_sems, send_sems, recv_sems,
    prefix, qkv, top, denom, total, *chunked,
):
    x, z, c = place()
    hid = lax.axis_index("hid")
    req = lax.axis_index("req")
    lower, upper = (req + 3) % 4, (req + 1) % 4
    width = tokens_ref.shape[1]
    bf16, f32 = jnp.bfloat16, jnp.float32
    first, second, passed, split = (chunked[n * CHUNKS:(n + 1) * CHUNKS] for n in range(4))

    def owner(group):
        return slot_ref[choice_ref[group]]

    peers = [{"hid": (hid + d) % 32} for d in range(1, 32)] + [{"req": lower}, {"req": upper}]
    barrier = pltpu.get_barrier_semaphore()
    for peer in peers:
        pl.semaphore_signal(barrier, inc=1, device_id=peer, device_id_type=MESH)
    latent_load = pltpu.make_async_copy(down_hbm, w_latent, load_sems.at[1])
    latent_load.start()
    def part_of(half, k):
        return cache_hbm.at[pl.ds(half * STEP * CHUNKS + k * STEP, STEP)]

    loads = []
    for k in range(CHUNKS):
        for half in range(2):
            copy = pltpu.make_async_copy(part_of(half, k), first[k].at[half], load_sems.at[2 + 2 * k + half])
            copy.start()
            loads.append(copy)
    w_load = pltpu.make_async_copy(w_hbm, w_qkv, load_sems.at[0])
    w_load.start()

    matrix = tokens_ref[...].astype(f32)
    normed = rms_scale(matrix, gain_ref[...].reshape(1, width)).astype(bf16)
    own_rows = pl.ds(pl.multiple_of(hid * 32, 32), 32)
    rows_buf[own_rows, :] = normed
    pl.semaphore_wait(barrier, len(peers))

    mail = Mail(send_sems, recv_sems)
    y_base = GATHER_ROLES
    deal_base = y_base + 4 * CHUNKS
    deal_rows = 2 * STEP

    def y_copy(role, src, dst, to):
        return pltpu.make_async_remote_copy(
            src_ref=src, dst_ref=dst, send_sem=send_sems.at[role], recv_sem=recv_sems.at[role],
            device_id={"req": to}, device_id_type=MESH,
        )

    def y_send(role, src, dst, to):
        copy = y_copy(role, src, dst, to)
        copy.start()
        mail.sent[role] = copy

    def y_start(*chunks):
        for k in chunks:
            y_send(y_base + k, part_of(0, k), first[k].at[2], lower)
            y_send(y_base + CHUNKS + k, part_of(1, k), first[k].at[3], upper)

    def y_pass(k):
        loads[2 * k].wait()
        loads[2 * k + 1].wait()
        y_copy(y_base + k, first[k].at[2], first[k].at[2], upper).wait_recv()
        y_copy(y_base + CHUNKS + k, first[k].at[3], first[k].at[3], lower).wait_recv()
        passed[k][0] = first[k][jnp.where(owner(lower) == req, 1, 2)]
        y_send(y_base + 2 * CHUNKS + k, passed[k].at[0], second[k].at[0], lower)
        passed[k][1] = first[k][jnp.where(owner(upper) == req, 0, 3)]
        y_send(y_base + 3 * CHUNKS + k, passed[k].at[1], second[k].at[1], upper)

    def deal(k):
        y_copy(y_base + 2 * CHUNKS + k, second[k].at[0], second[k].at[0], upper).wait_recv()
        y_copy(y_base + 3 * CHUNKS + k, second[k].at[1], second[k].at[1], lower).wait_recv()
        away = (owner(req) - req + 4) % 4
        late_a = jnp.full((1, 1, 1), (away >= 2).astype(jnp.int32)) > 0
        late_b = jnp.full((1, 1, 1), jnp.logical_or(away == 1, away == 2).astype(jnp.int32)) > 0
        half_a = jnp.where(late_a, second[k][jnp.where(away == 2, 0, 1)], first[k][jnp.where(away == 0, 0, 2)])
        half_b = jnp.where(late_b, second[k][jnp.where(away == 1, 0, 1)], first[k][jnp.where(away == 0, 1, 3)])
        r = lax.broadcasted_iota(jnp.int32, (32, 32), 0)
        s = lax.broadcasted_iota(jnp.int32, (32, 32), 1)
        sort = (s == jnp.where(r < 16, 2 * r, 2 * r - 31)).astype(bf16)
        zeros = jnp.zeros((deal_rows, 256 - HD), bf16)
        value = jnp.concatenate([half_a.reshape(2 * STEP, width), half_b.reshape(2 * STEP, width)], axis=0)
        planes = jnp.dot(sort, value, preferred_element_type=f32).astype(bf16)
        for kv in range(2):
            for h in range(32):
                piece = planes[kv * deal_rows:(kv + 1) * deal_rows, h * HD:(h + 1) * HD]
                split[k][h, kv] = jnp.concatenate([piece, zeros], axis=1)

        for n, offset in enumerate(deal_order()):
            to = at_offset(*offset)
            mail.send(deal_base + k * 31 + n, split[k].at[to], landing(k, hid), to)
        prefix[:, pl.ds(pl.multiple_of(k * 512 + hid * deal_rows, deal_rows), deal_rows)] = split[k][hid]

    def landing(k, source):
        start = pl.multiple_of(k * 512 + source * deal_rows, deal_rows)
        return prefix.at[:, pl.ds(start, deal_rows)]

    def dealt(k):
        for n, offset in enumerate(deal_order()):
            source = at_offset(*offset, sign=-1)
            mail.await_recv(deal_base + k * 31 + n, landing(k, source), source)

    y_start(0, 1)
    gather = Gather(mail, 0, rows_buf, 32)
    latent_base = deal_base + 31 * CHUNKS

    def latent_rows(device):
        return latents_buf.at[pl.ds(pl.multiple_of(device * 32, 32), 32)]

    def send_latents():
        latent_load.wait()
        latent = jnp.dot(normed, w_latent[...], preferred_element_type=f32)
        latents_buf[own_rows, :] = latent.astype(bf16)
        for n, offset in enumerate(deal_order()):
            mail.send(latent_base + n, latent_rows(hid), latent_rows(hid), at_offset(*offset))

    def await_latents():
        for n, offset in enumerate(deal_order()):
            source = at_offset(*offset, sign=-1)
            mail.await_recv(latent_base + n, latent_rows(source), source)

    contract = (((1,), (1,)), ((), ()))

    def project(own, partners):
        gather.from_partner(*partners)
        places = [gather.owner(*at) for at in own] + [gather.owner(*at, True) for at in partners]
        slices = [pl.ds(pl.multiple_of(place * 32, 32), 32) for place in places]
        rows = jnp.concatenate([rows_buf[at, :] for at in slices], axis=0)
        latents = jnp.concatenate([latents_buf[at, :] for at in slices], axis=0)
        pad = jnp.zeros((rows.shape[0], 256 - HD), bf16)

        def keep(part, value):
            value = jnp.concatenate([value.astype(bf16), pad], axis=1)
            for n, at in enumerate(slices):
                qkv[part, at, :] = value[n * 32:(n + 1) * 32]

        value = lax.dot_general(rows, w_qkv[pl.ds(0, HD), :], contract, preferred_element_type=f32)
        keep(0, value + lax.dot_general(latents, up_ref[...], contract, preferred_element_type=f32))

        @pl.loop(1, 3)
        def _(part):
            weight = w_qkv[pl.ds(pl.multiple_of(part * HD, 32), HD), :]
            keep(part, lax.dot_general(rows, weight, contract, preferred_element_type=f32))

    for stage in gather.stages():
        if stage == "start":
            send_latents()
            y_pass(0)
            y_start(2)
        if stage == "relay0":
            y_pass(1)
            y_start(3)
        if stage == "relay2":
            deal(0)
            w_load.wait()
            await_latents()
            project([(0, 0), (0, 1), (0, 2), (1, 0), (2, 0)], [(0, 0), (0, 1), (0, 2)])
            y_pass(2)
        if stage == "relay3":
            deal(1)
            y_pass(3)
            project([(1, 1), (2, 1), (1, 2), (2, 2), (0, 3), (3, 0)], [(1, 0), (2, 0)])
        if stage == "far1":
            project([(1, 3), (2, 3)], [(0, 3), (1, 1), (2, 1), (1, 2), (2, 2), (3, 0)])
        if stage == "far2":
            deal(2)
        if stage == "far3":
            deal(3)
    project([(3, 1), (3, 2), (3, 3)], [(1, 3), (2, 3), (3, 1), (3, 2), (3, 3)])

    dealt(0)
    dealt(1)

    ends = [lengths_ref[0, 0]]
    for n in range(1, lengths_ref.shape[1]):
        ends.append(ends[-1] + lengths_ref[0, n])
    factor = HD ** (-0.5)

    @pl.loop(0, 8)
    def _(i):
        at = pl.ds(pl.multiple_of(i * 128, 128), 128)
        begin = jnp.minimum(jnp.maximum(i * 128 - 512, 0), 1024 - WINDOW)
        near = pl.ds(pl.multiple_of(begin, 128), WINDOW)
        q = qkv[0, at, :]
        s_far = lax.dot_general(q, prefix[0, pl.ds(0, 1024), :], contract, preferred_element_type=f32) * factor
        s_near = lax.dot_general(q, qkv[1, near, :], contract, preferred_element_type=f32) * factor
        row = lax.broadcasted_iota(jnp.int32, (128, 1), 0) + i * 128
        since = jnp.zeros((128, 1), jnp.int32)
        for end in ends:
            since = jnp.where(row >= end, jnp.maximum(since, end), since)
        col = lax.broadcasted_iota(jnp.int32, (128, WINDOW), 1) + begin
        s_near = jnp.where(jnp.logical_and(col >= since, col <= row), s_near, -jnp.inf)
        row_max = jnp.maximum(
            jnp.max(s_far, axis=1, keepdims=True), jnp.max(s_near, axis=1, keepdims=True)
        )
        e_far = jnp.exp(s_far - row_max)
        e_near = jnp.exp(s_near - row_max)
        top[at, :] = row_max
        denom[at, :] = jnp.sum(e_far, axis=1, keepdims=True) + jnp.sum(e_near, axis=1, keepdims=True)
        out = jnp.dot(e_far.astype(bf16), prefix[1, pl.ds(0, 1024), :], preferred_element_type=f32)
        total[at, :] = out + jnp.dot(e_near.astype(bf16), qkv[2, near, :], preferred_element_type=f32)

    for k in (2, 3):
        dealt(k)
        more = pl.ds(k * 512, 512)

        @pl.loop(0, 4)
        def _(i):
            at = pl.ds(pl.multiple_of(i * 256, 256), 256)
            scores = lax.dot_general(
                qkv[0, at, :], prefix[0, more, :], contract, preferred_element_type=f32
            ) * factor
            row_max = jnp.maximum(top[at, :], jnp.max(scores, axis=1, keepdims=True))
            keep = jnp.exp(top[at, :] - row_max)
            expos = jnp.exp(scores - row_max)
            row_sum = denom[at, :] * keep + jnp.sum(expos, axis=1, keepdims=True)
            out = total[at, :] * keep + jnp.dot(
                expos.astype(bf16), prefix[1, more, :], preferred_element_type=f32
            )
            if k == 2:
                top[at, :] = row_max
                denom[at, :] = row_sum
                total[at, :] = out
            else:
                heads_ref[at, :] = (out / row_sum)[:, :HD].astype(bf16)

    mail.drain()


def front(slots, choices, lengths, tokens, gain_in, adapt_down, up_t, w_t, cache):
    rows, width = tokens.shape
    tok_grp = rows * 32
    bf16 = jnp.bfloat16
    smem = pl.BlockSpec(memory_space=pltpu.SMEM)
    vmem = pl.BlockSpec(memory_space=pltpu.VMEM)
    anywhere = pl.BlockSpec(memory_space=pl.ANY)
    roles = GATHER_ROLES + 4 * CHUNKS + 31 * (CHUNKS + 1)

    def halves(count):
        return [pltpu.VMEM((count, STEP, 2, width), bf16)] * CHUNKS

    return pl.pallas_call(
        front_kernel,
        out_shape=jax.ShapeDtypeStruct((tok_grp, HD), bf16),
        in_specs=[smem, smem, smem, vmem, vmem, anywhere, vmem, anywhere, anywhere],
        out_specs=vmem,
        scratch_shapes=[
            pltpu.VMEM(w_t.shape, bf16), pltpu.VMEM(adapt_down.shape, bf16),
            pltpu.VMEM((tok_grp, width), bf16), pltpu.VMEM((tok_grp, 128), bf16),
            pltpu.SemaphoreType.DMA((2 + 2 * CHUNKS,)), pltpu.SemaphoreType.DMA((roles,)),
            pltpu.SemaphoreType.DMA((roles,)),
            pltpu.VMEM((2, 2048, 256), bf16), pltpu.VMEM((3, tok_grp, 256), bf16),
            pltpu.VMEM((tok_grp, 1), jnp.float32), pltpu.VMEM((tok_grp, 1), jnp.float32),
            pltpu.VMEM((tok_grp, 256), jnp.float32),
            *halves(4), *halves(2), *halves(2),
            *([pltpu.VMEM((32, 2, 2 * STEP, 256), bf16)] * CHUNKS),
        ],
        compiler_params=pltpu.CompilerParams(
            collective_id=1, has_side_effects=True, vmem_limit_bytes=66000000
        ),
        name="front",
    )(slots, choices, lengths, tokens, gain_in, adapt_down, up_t, w_t, cache)


def settle_kernel(attn_ref, block_ref, attn_out, block_out):
    attn_out[...] = attn_ref[...]
    block_out[...] = block_ref[...]


def settle(attn, block):
    vmem = pl.BlockSpec(memory_space=pltpu.VMEM)
    return pl.pallas_call(
        settle_kernel,
        out_shape=(jax.ShapeDtypeStruct(attn.shape, attn.dtype), jax.ShapeDtypeStruct(block.shape, block.dtype)),
        in_specs=[vmem, vmem],
        out_specs=(vmem, vmem),
        name="settle",
    )(attn, block)


def per_device(
    tokens,
    gain_in,
    w_qkv,
    adapt_down,
    adapt_up,
    w_out,
    gain_ff,
    w_gate_up,
    w_down,
    prefix_cache,
    prefix_owner,
    group_prefix,
    lengths,
):
    w_t = jnp.transpose(w_qkv, (1, 2, 0)).reshape(3 * w_qkv.shape[2], w_qkv.shape[0])
    w_gu = jnp.transpose(w_gate_up, (1, 2, 0)).reshape(2 * w_gate_up.shape[2], w_gate_up.shape[0])
    heads_out = front(
        prefix_owner, group_prefix, lengths, tokens, gain_in, adapt_down, adapt_up.T, w_t, prefix_cache[0]
    )
    return settle(*tail(heads_out, w_out, gain_ff, w_gu, w_down))


def solution(mesh):
    placed = (
        P(("req", "hid"), None),
        P(),
        P(None, None, "hid"),
        P(),
        P(None, "hid"),
        P("hid", None),
        P(),
        P(None, None, "hid"),
        P("hid", None),
        P("req", "hid", None, None),
        P(),
        P(),
        P("req", None),
    )
    return jax.shard_map(
        per_device,
        mesh=mesh,
        in_specs=placed,
        out_specs=(P(("req", "hid"), None), P(("req", "hid"), None)),
        check_vma=False,
    )
```
